128 devices in a mesh: dp: 8 (over y, x_lo), seq: 16 (over z, x_hi, core).
Axes of the slice: x: 4 (x_hi: 2, x_lo: 2; x = x_hi * 2 + x_lo), y: 4, z: 4, core: 2. Of those that a mesh axis runs over, the one named last changes fastest.
Arguments:
- hidden_in: bfloat16 [2, 8, 2048, 1024], P(None, 'dp', 'seq'), may hold values from -6 to 6
- seg_ids: int32 [2, 8, 2048], P(None, 'dp', 'seq'), may hold values from 0 to 11, never falling along the last dimension, each value on 1 to 1024 neighbouring positions
- decay_rates: float32 [8], replicated, may hold values from 0.00012207031 to 0.033
- grad_out: bfloat16 [2, 8, 2048, 1024], P(None, 'dp', 'seq'), may hold values from -6 to 6
- w_query: bfloat16 [1048576], P(('dp', 'seq')), may hold values from -0.1875 to 0.1875
- w_key: bfloat16 [1048576], P(('dp', 'seq')), may hold values from -0.1875 to 0.1875
- w_value: bfloat16 [1048576], P(('dp', 'seq')), may hold values from -0.1875 to 0.1875
- w_gate: bfloat16 [1048576], P(('dp', 'seq')), may hold values from -0.1875 to 0.1875
- w_output: bfloat16 [1048576], P(('dp', 'seq')), may hold values from -0.1875 to 0.1875
- w_left: bfloat16 [2883584], P(('dp', 'seq')), may hold values from -0.1875 to 0.1875
- w_right: bfloat16 [2883584], P(('dp', 'seq')), may hold values from -0.1875 to 0.1875
- w_down: bfloat16 [2883584], P(('dp', 'seq')), may hold values from -0.109375 to 0.109375
Outputs:
- activations: bfloat16 [2, 8, 2048, 1024], P(None, 'dp', 'seq')
- input_grad: float32 [2, 8, 2048, 1024], P(None, 'dp', 'seq')
- grad_query: float32 [1048576], P(('dp', 'seq'))
- grad_key: float32 [1048576], P(('dp', 'seq'))
- grad_value: float32 [1048576], P(('dp', 'seq'))
- grad_gate: float32 [1048576], P(('dp', 'seq'))
- grad_output: float32 [1048576], P(('dp', 'seq'))
- grad_left: float32 [2883584], P(('dp', 'seq'))
- grad_right: float32 [2883584], P(('dp', 'seq'))
- grad_down: float32 [2883584], P(('dp', 'seq'))
The draws below stay inside these ranges and needn't reach their ends.
Inputs may be any that keep to these rules, and one draw needn't show every extreme that they name: `seg_ids`: along each sequence the document ids never fall; a document has 1 to 1024 tokens, and one of each sequence has exactly that many.
All inputs are finite; a program needn't handle non-finite values.
Results may differ from the reference program's by a relative error of at most 0.017.
Values may be sent and summed in bfloat16 or wider, within the bound.
A program may use at most 320 MiB of HBM per device.

```python
import math
from functools import partial
import jax
import jax.numpy as jnp
import numpy as np
from jax import lax

D = 1024
H = 8
HD = 128
FF = 2816
SEQ_DEV = 128
MB = 2
SEQLEN = 2048
SEQS = 8
N_SEQ = 16


def block_scale(rng, shape, shards, low, largest):
    level = 1.0
    for axis_at, parts in shards:
        draws = jax.random.uniform(jax.random.fold_in(jax.random.fold_in(rng, 6), axis_at), (parts,), jnp.float32, low / len(shards), largest / len(shards))
        level = level * jnp.repeat(jnp.exp(draws), shape[axis_at] // parts).reshape((-1,) + (1,) * (len(shape) - 1 - axis_at))
    return level


def length_profile(count, total, bound, skew):
    loads = [(1 << 20) // math.isqrt(rank ** skew) + 1 for rank in range(2, count + 1)]
    spare, holding = total - bound - (count - 1), [1] * (count - 1)
    while spare > 0:
        candidates = [i for i in range(count - 1) if holding[i] < bound]
        pool, remaining = sum([loads[i] for i in candidates]), spare
        for i in candidates:
            extra = min(bound - holding[i], max(1, remaining * loads[i] // pool), spare)
            holding[i] = holding[i] + extra
            spare = spare - extra
    return np.array([bound] + holding)


def ragged_sizes(own_key, amount, total, limit, lean):
    if amount == 2:
        one = jax.random.randint(own_key, (), max(1, total - limit), min(limit, total - 1) + 1)
        return jnp.stack([one, total - one])
    tallies = jnp.asarray(length_profile(amount, total, limit, lean), jnp.int32)
    twos = (amount - 1) // 2
    giver, taker = tallies[1:1 + 2 * twos:2], tallies[2:2 + 2 * twos:2]
    room = jnp.minimum(giver - 1, limit - taker)
    moved = jax.random.randint(jax.random.fold_in(own_key, 1), (twos,), 0, 1 << 20) % (room + 1)
    tallies = tallies.at[1:1 + 2 * twos:2].set(giver - moved).at[2:2 + 2 * twos:2].set(taker + moved)
    return tallies[jax.random.permutation(jax.random.fold_in(own_key, 2), amount)]


def normal_values(rng, extent, scale, reach, split=(), kind=jnp.bfloat16):
    factor_of = block_scale(rng, extent, split, -0.22, 0.18) if split else 1.0
    values = jax.random.normal(rng, extent, jnp.float32) * scale * factor_of
    return jnp.minimum(jnp.maximum(values, -reach), reach).astype(kind)


def setup_inputs(seed: int = 0) -> dict:
    keys = jax.random.split(jax.random.key(seed), 13)
    return {
        "hidden_in": normal_values(keys[0], (MB, SEQS, SEQLEN, D), 1.0, 6.0, ((1, 8), (2, 16))),
        "seg_ids": jax.vmap(lambda own: jnp.searchsorted(jnp.cumsum(ragged_sizes(own, SEQLEN // 256 + 4, SEQLEN, SEQLEN // 2, 2)), jnp.arange(SEQLEN), side="right"))(jax.random.split(keys[1], MB * SEQS)).reshape((MB, SEQS, SEQLEN)).astype(jnp.int32),
        "decay_rates": jnp.clip(jnp.exp(jax.random.uniform(keys[2], (H,), jnp.float32, math.log(0.00012207031), math.log(0.033))), 0.00012207031, 0.033),
        "grad_out": normal_values(keys[3], (MB, SEQS, SEQLEN, D), 1.0, 6.0, ((1, 8), (2, 16))),
        "w_query": normal_values(keys[4], (D * D,), D ** -0.5, 0.1875, ((0, 128),)),
        "w_key": normal_values(keys[5], (D * D,), D ** -0.5, 0.1875, ((0, 128),)),
        "w_value": normal_values(keys[6], (D * D,), D ** -0.5, 0.1875, ((0, 128),)),
        "w_gate": normal_values(keys[7], (D * D,), D ** -0.5, 0.1875, ((0, 128),)),
        "w_output": normal_values(keys[8], (D * D,), D ** -0.5, 0.1875, ((0, 128),)),
        "w_left": normal_values(keys[9], (D * FF,), D ** -0.5, 0.1875, ((0, 128),)),
        "w_right": normal_values(keys[10], (D * FF,), D ** -0.5, 0.1875, ((0, 128),)),
        "w_down": normal_values(keys[11], (FF * D,), FF ** -0.5, 0.109375, ((0, 128),)),
    }


@jax.custom_vjp
def low(v):
    return lax.optimization_barrier(v.astype(jnp.bfloat16)).astype(jnp.float32)

@jax.custom_vjp
def low_back(v):
    return v

def low_keep(v):
    return (low(v), None)

def low_pass(kept, grad):
    return (grad,)

def back_keep(v):
    return (v, None)

def back_low(kept, grad):
    return (low(grad),)
low.defvjp(low_keep, low_pass)
low_back.defvjp(back_keep, back_low)
EPSILON = 1e-06

def exact(form, left_op, right_op):
    return jnp.einsum(form, left_op, right_op, precision=lax.Precision.HIGHEST, preferred_element_type=jnp.float32)

def normalize(values):
    return values * lax.rsqrt(lax.optimization_barrier(jnp.mean(values * values, axis=-1, keepdims=True)) + EPSILON)

def swish(values):
    return values * jax.nn.sigmoid(values)

def mixer_block(decays, carry, block):
    carried, boundary = carry
    queries, key_rows, value_rows, segments = block
    length = queries.shape[0]
    places = jnp.arange(length, dtype=jnp.float32)
    distance = places[:, None] - places[None, :]
    allowed = (distance >= 0.0) & (segments[:, None] == segments[None, :])
    decay_mask = jnp.where(allowed[None], jnp.exp(-decays[:, None, None] * jnp.maximum(distance, 0.0)[None]), 0.0)
    scores = low_back(exact('ihd,jhd->hij', queries, key_rows))
    weighted = low(scores * decay_mask)
    within = exact('hij,jhe->ihe', weighted, value_rows)
    reaching = jnp.exp(-(places[:, None] + 1.0) * decays[None, :]) * jnp.where(segments == boundary, 1.0, 0.0)[:, None]
    crossed = exact('ihd,hde->ihe', queries, low(carried)) * reaching[:, :, None]
    keeping = jnp.exp(-(length - 1.0 - places)[:, None] * decays[None, :]) * jnp.where(segments == segments[-1], 1.0, 0.0)[:, None]
    local_state = low_back(exact('jhd,jhe->hde', key_rows * keeping[:, :, None], value_rows))
    passing = jnp.where((segments[0] == boundary) & (segments[0] == segments[-1]), 1.0, 0.0)
    carried = local_state + passing * jnp.exp(-length * decays)[:, None, None] * carried
    return ((carried, segments[-1]), within + crossed)

def block_forward(decays, segments, inputs, weights):
    w_query, w_key, w_value, w_gate, w_output, w_left, w_right, w_down = weights
    total = inputs.shape[0]
    normed_in = low(normalize(inputs))
    q_pre = low_back(exact('rd,de->re', normed_in, w_query))
    k_pre = low_back(exact('rd,de->re', normed_in, w_key))
    v_pre = low_back(exact('rd,de->re', normed_in, w_value))
    gate = low_back(exact('rd,de->re', normed_in, w_gate))
    queries = low(swish(q_pre)).reshape(N_SEQ, SEQ_DEV, H, HD)
    key_rows = low(swish(k_pre)).reshape(N_SEQ, SEQ_DEV, H, HD)
    value_rows = low(v_pre).reshape(N_SEQ, SEQ_DEV, H, HD)
    start = (jnp.zeros((H, HD, HD), jnp.float32), jnp.array(-1, jnp.int32))
    stepper = jax.checkpoint(partial(mixer_block, decays))
    ending, mixed = lax.scan(stepper, start, (queries, key_rows, value_rows, segments.reshape(N_SEQ, SEQ_DEV).astype(jnp.int32)))
    mixed = low_back(mixed.reshape(total, D))
    gated = low(normalize(mixed) * gate)
    resid = inputs + low_back(exact('rd,de->re', gated, w_output))
    second = low(normalize(resid))
    left_proj = low_back(exact('rd,df->rf', second, w_left))
    right_proj = low_back(exact('rd,df->rf', second, w_right))
    product = low(left_proj * right_proj)
    return resid + low_back(exact('rf,fd->rd', product, w_down))

def reference(hidden_in, seg_ids, decay_rates, grad_out, w_query, w_key, w_value, w_gate, w_output, w_left, w_right, w_down):
    flats = (w_query, w_key, w_value, w_gate, w_output, w_left, w_right, w_down)
    shapes = ((D, D), (D, D), (D, D), (D, D), (D, D), (D, FF), (D, FF), (FF, D))
    weights = tuple((piece.astype(jnp.float32).reshape(target) for piece, target in zip(flats, shapes)))
    count_seq = MB * SEQS
    inputs = hidden_in.astype(jnp.float32).reshape(count_seq, SEQLEN, D)
    segments = seg_ids.reshape(count_seq, SEQLEN).astype(jnp.int32)
    cotangent = grad_out.astype(jnp.float32).reshape(count_seq, SEQLEN, D)

    def per_sequence(totals, sequence):
        rows_here, segs_here, cot_here = sequence

        def forward(tokens, params):
            return block_forward(decay_rates, segs_here, tokens, params)
        result, pullback = jax.vjp(forward, rows_here, weights)
        d_rows, d_params = pullback(cot_here)
        return (tuple((total + grad for total, grad in zip(totals, d_params))), (result, d_rows))
    zeros = tuple((jnp.zeros(target, jnp.float32) for target in shapes))
    totals, outputs = lax.scan(per_sequence, zeros, (inputs, segments, cotangent))
    results, d_inputs = outputs
    return (results.reshape(MB, SEQS, SEQLEN, D).astype(jnp.bfloat16), d_inputs.reshape(MB, SEQS, SEQLEN, D), totals[0].reshape(-1), totals[1].reshape(-1), totals[2].reshape(-1), totals[3].reshape(-1), totals[4].reshape(-1), totals[5].reshape(-1), totals[6].reshape(-1), totals[7].reshape(-1))
```

```python
import functools
import jax, jax.numpy as jnp
from jax import lax
from jax.experimental import pallas as pl
from jax.experimental.pallas import tpu as pltpu
from jax.sharding import PartitionSpec as P

MESH = pl.DeviceIdType.MESH
RING = 4

UNITS = (
    (0, 0, 0, 13 * 128), (0, 1, 13 * 128, 26 * 128), (0, 2, 26 * 128, 32 * 128),
    (1, 2, 0, 8 * 128),
    (2, 0, 0, 22 * 128), (2, 1, 22 * 128, 44 * 128),
    (3, 2, 0, 176),
)
ORDERS = (("x", "y", "z"), ("y", "z", "x"), ("z", "x", "y"))
SPLIT_ROWS = (False, False, False, True)


def where_am_i():
    dp = lax.axis_index("dp")
    seq = lax.axis_index("seq")
    return {"x": (seq // 2 % 2) * 2 + dp % 2, "y": dp // 2, "z": seq // 4, "c": seq % 2}


def device(at):
    return (at["y"] * 2 + at["x"] % 2, at["z"] * 4 + (at["x"] // 2) * 2 + at["c"])


def moved(at, axis, by):
    out = dict(at)
    out[axis] = (at[axis] + by) % RING if axis != "c" else 1 - at[axis]
    return out


def block(ref, at, whole, lo, hi, rows):
    every = slice(None)
    pick = lambda axis, value: every if axis in whole else value
    span = pl.ds(lo, hi - lo)
    return ref.at[
        pick("y", at["y"]), pick("x", at["x"] % 2), pick("z", at["z"]), pick("x", at["x"] // 2), at["c"],
        span if rows else every, every if rows else span,
    ]


def middle(lo, hi, rows):
    grain = 8 if rows else 128
    return lo + ((hi - lo) // grain // 2) * grain


def ag_kernel(*refs):
    n_arr = 4
    ins, outs = refs[:n_arr], refs[n_arr:2 * n_arr]
    local_sem, send_sem, recv_sem, csend_sem, crecv_sem = refs[2 * n_arr:]
    me = where_am_i()
    barrier = pltpu.get_barrier_semaphore()
    partners = [moved(me, a, d) for a in "xyz" for d in (1, -1)] + [moved(me, "c", 1)]
    for other in partners:
        pl.semaphore_signal(barrier, inc=1, device_id=device(other), device_id_type=MESH)

    copies = []
    for i in range(n_arr):
        cp = pltpu.make_async_copy(
            ins[i], outs[i].at[me["y"], me["x"] % 2, me["z"], me["x"] // 2, me["c"]], local_sem.at[i])
        cp.start()
        copies.append(cp)
    pl.semaphore_wait(barrier, len(partners))
    for cp in copies:
        cp.wait()

    sends = []
    def send(src, u, slot, to):
        cp = pltpu.make_async_remote_copy(src_ref=src, dst_ref=src, send_sem=send_sem.at[u, slot],
            recv_sem=recv_sem.at[u, slot], device_id=device(to), device_id_type=MESH)
        cp.start()
        sends.append(cp)

    def got(ref, u, slot):
        pltpu.make_async_remote_copy(src_ref=ref, dst_ref=ref, send_sem=send_sem.at[u, slot],
            recv_sem=recv_sem.at[u, slot], device_id=device(me), device_id_type=MESH).wait_recv()

    def csend(src, u, slot):
        cp = pltpu.make_async_remote_copy(src_ref=src, dst_ref=src, send_sem=csend_sem.at[u, slot],
            recv_sem=crecv_sem.at[u, slot], device_id=device(moved(me, "c", 1)), device_id_type=MESH)
        cp.start()
        sends.append(cp)

    ctail = []
    for stage in range(3):
        for u, (i, s, lo, hi) in enumerate(UNITS):
            axis, whole = ORDERS[s][stage], ORDERS[s][:stage]
            mine = block(outs[i], me, whole, lo, hi, SPLIT_ROWS[i])
            send(mine, u, 4 * stage + 0, moved(me, axis, 1))
            send(mine, u, 4 * stage + 1, moved(me, axis, -1))
            if stage == 2:
                csend(mine, u, 0)
        for u, (i, s, lo, hi) in enumerate(UNITS):
            axis, whole = ORDERS[s][stage], ORDERS[s][:stage]
            rows = SPLIT_ROWS[i]
            mid = middle(lo, hi, rows)
            below, above = moved(me, axis, -1), moved(me, axis, 1)
            got(block(outs[i], below, whole, lo, hi, rows), u, 4 * stage + 0)
            send(block(outs[i], below, whole, lo, mid, rows), u, 4 * stage + 2, above)
            got(block(outs[i], above, whole, lo, hi, rows), u, 4 * stage + 1)
            send(block(outs[i], above, whole, mid, hi, rows), u, 4 * stage + 3, below)
            if stage == 2:
                csend(block(outs[i], below, whole, lo, hi, rows), u, 1)
                csend(block(outs[i], above, whole, lo, hi, rows), u, 2)
        for u, (i, s, lo, hi) in enumerate(UNITS):
            axis, whole = ORDERS[s][stage], ORDERS[s][:stage]
            rows = SPLIT_ROWS[i]
            mid = middle(lo, hi, rows)
            far = moved(me, axis, 2)
            got(block(outs[i], far, whole, lo, mid, rows), u, 4 * stage + 2)
            got(block(outs[i], far, whole, mid, hi, rows), u, 4 * stage + 3)
            if stage == 2:
                csend(block(outs[i], far, whole, lo, hi, rows), u, 3)
    sib = moved(me, "c", 1)
    for u, (i, s, lo, hi) in enumerate(UNITS):
        axis, whole = ORDERS[s][2], ORDERS[s][:2]
        for k, by in enumerate((0, -1, 1, 2)):
            ref = block(outs[i], moved(sib, axis, by), whole, lo, hi, SPLIT_ROWS[i])
            pltpu.make_async_remote_copy(src_ref=ref, dst_ref=ref, send_sem=csend_sem.at[u, k],
                recv_sem=crecv_sem.at[u, k], device_id=device(sib), device_id_type=MESH).wait_recv()
    for cp in sends:
        cp.wait_send()


def gather_all(pieces):
    outs = [jax.ShapeDtypeStruct((4, 2, 4, 2, 2) + p.shape, p.dtype) for p in pieces]
    n = len(UNITS)
    return pl.pallas_call(
        ag_kernel, out_shape=outs,
        in_specs=[pl.BlockSpec(memory_space=pl.ANY)] * len(pieces),
        out_specs=[pl.BlockSpec(memory_space=pl.ANY)] * len(pieces),
        scratch_shapes=[pltpu.SemaphoreType.DMA((4,)), pltpu.SemaphoreType.DMA((n, 12)), pltpu.SemaphoreType.DMA((n, 12)),
            pltpu.SemaphoreType.DMA((n, 4)), pltpu.SemaphoreType.DMA((n, 4))],
        compiler_params=pltpu.CompilerParams(collective_id=0, has_side_effects=True),
        name="gather_weights",
    )(*pieces)


RS_ORDERS = tuple(o[::-1] for o in ORDERS)
SIZES = {"y": (4,), "x": (2, 2), "z": (4,)}
DIMS = (("y", 4), ("x", 2), ("z", 4), ("x", 2))


def live_dims(fixed):
    return tuple(n for a, n in DIMS if a not in fixed)


def part(ref, at, fixed, gone, lo, hi, rows, lead=()):
    every = slice(None)
    idx = []
    for k, (a, n) in enumerate(DIMS):
        if a in gone:
            continue
        if a in fixed:
            idx.append((at["x"] % 2 if k == 1 else at["x"] // 2) if a == "x" else at[a])
        else:
            idx.append(every)
    span = pl.ds(lo, hi - lo)
    return ref.at[(*lead, *idx, span if rows else every, every if rows else span)]


def accumulate(dst, srcs, dims, out=None):
    n = 1
    for d in dims:
        n *= d
    def one(k, _):
        idx = []
        rest = k
        for d in dims[::-1]:
            idx.append(rest % d)
            rest = rest // d
        idx = tuple(idx[::-1])
        total = dst[idx].astype(jnp.float32) if dims else dst[...].astype(jnp.float32)
        for s in srcs:
            total = total + (s[idx] if dims else s[...]).astype(jnp.float32)
        target = dst if out is None else out
        if dims:
            target[idx] = total.astype(target.dtype)
        else:
            target[...] = total.astype(target.dtype)
        return 0
    if n == 1:
        one(0, 0)
    else:
        lax.fori_loop(0, n, one, 0)


def rs_kernel(*refs):
    n_arr, n = 4, len(UNITS)
    ins, outs = refs[:n_arr], refs[n_arr:2 * n_arr]
    refs = refs[2 * n_arr:]
    held, other = refs[:n], refs[n:2 * n]
    slots = [refs[2 * n + k * n: 3 * n + k * n] for k in range(3)]
    load_sem, csend_sem, crecv_sem, send_sem, recv_sem = refs[5 * n:]
    me = where_am_i()
    sib = moved(me, "c", 1)
    barrier = pltpu.get_barrier_semaphore()
    partners = [moved(me, a, d) for a in "xyz" for d in (1, -1)] + [sib]
    for one in partners:
        pl.semaphore_signal(barrier, inc=1, device_id=device(one), device_id_type=MESH)
    loads = []
    def half_of(i, c, lo, hi, rows):
        every, span = slice(None), pl.ds(lo, hi - lo)
        return ins[i].at[:, :, :, :, c, span if rows else every, every if rows else span]
    for u, (i, s, lo, hi) in enumerate(UNITS):
        cp = pltpu.make_async_copy(half_of(i, me["c"], lo, hi, SPLIT_ROWS[i]), held[u], load_sem.at[u])
        cp.start()
        loads.append(cp)
    pl.semaphore_wait(barrier, len(partners))
    sends = []
    for u, (i, s, lo, hi) in enumerate(UNITS):
        cp = pltpu.make_async_remote_copy(src_ref=half_of(i, sib["c"], lo, hi, SPLIT_ROWS[i]), dst_ref=other[u],
            send_sem=csend_sem.at[u], recv_sem=crecv_sem.at[u], device_id=device(sib), device_id_type=MESH)
        cp.start()
        sends.append(cp)

    def send(src, dst, u, stage, slot, to):
        cp = pltpu.make_async_remote_copy(src_ref=src, dst_ref=dst, send_sem=send_sem.at[u, stage, slot],
            recv_sem=recv_sem.at[u, stage, slot], device_id=device(to), device_id_type=MESH)
        cp.start()
        sends.append(cp)

    def got(ref, u, stage, slot):
        pltpu.make_async_remote_copy(src_ref=ref, dst_ref=ref, send_sem=send_sem.at[u, stage, slot],
            recv_sem=recv_sem.at[u, stage, slot], device_id=device(sib), device_id_type=MESH).wait_recv()

    def spans(u):
        i, s, lo, hi = UNITS[u]
        width = hi - lo
        return s, SPLIT_ROWS[i], width, middle(0, width, SPLIT_ROWS[i])

    def send_far(u, stage):
        s, rows, width, mid = spans(u)
        order = RS_ORDERS[s]
        axis, gone, fixed = order[stage], order[:stage], order[:stage + 1]
        far = moved(me, axis, 2)
        send(part(held[u], far, fixed, (), 0, mid, rows), part(slots[stage][u], me, (), fixed, 0, mid, rows, (0,)), u, stage, 0, moved(me, axis, 1))
        send(part(held[u], far, fixed, (), mid, width, rows), part(slots[stage][u], me, (), fixed, mid, width, rows, (0,)), u, stage, 1, moved(me, axis, -1))

    for u in range(n):
        loads[u].wait()
        pltpu.make_async_remote_copy(src_ref=other[u], dst_ref=other[u], send_sem=csend_sem.at[u], recv_sem=crecv_sem.at[u],
            device_id=device(sib), device_id_type=MESH).wait_recv()
        accumulate(held[u], [other[u]], live_dims(()))
        send_far(u, 0)
    for stage in range(3):
        for u in range(n):
            s, rows, width, mid = spans(u)
            order = RS_ORDERS[s]
            axis, fixed = order[stage], order[:stage + 1]
            above, below = moved(me, axis, 1), moved(me, axis, -1)
            dims = live_dims(fixed)
            for k, (to, lo, hi) in enumerate(((above, 0, mid), (below, mid, width))):
                came = part(slots[stage][u], me, (), fixed, lo, hi, rows, (0,))
                got(came, u, stage, k)
                accumulate(part(held[u], to, fixed, (), lo, hi, rows), [came], dims)
                send(part(held[u], to, fixed, (), 0, width, rows), part(slots[stage][u], me, (), fixed, 0, width, rows, (1 + k,)), u, stage, 2 + k, to)
        for u in range(n):
            i, _, lo, hi = UNITS[u]
            s, rows, width, mid = spans(u)
            order = RS_ORDERS[s]
            fixed = order[:stage + 1]
            came = []
            for k in range(2):
                ref = part(slots[stage][u], me, (), fixed, 0, width, rows, (1 + k,))
                got(ref, u, stage, 2 + k)
                came.append(ref)
            mine = part(held[u], me, fixed, (), 0, width, rows)
            if stage == 2:
                span = pl.ds(lo, hi - lo)
                accumulate(mine, came, (), outs[i].at[(span, slice(None)) if rows else (slice(None), span)])
            else:
                accumulate(mine, came, live_dims(fixed))
                send_far(u, stage + 1)
    for cp in sends:
        cp.wait_send()


def scatter_all(grads):
    outs = [jax.ShapeDtypeStruct(g.shape[5:], jnp.float32) for g in grads]
    n = len(UNITS)
    held, slots = [], [[], [], []]
    for i, s, lo, hi in UNITS:
        tail = (hi - lo, 128) if SPLIT_ROWS[i] else (8, hi - lo)
        held.append(pltpu.VMEM(live_dims(()) + tail, jnp.bfloat16))
        for k in range(3):
            slots[k].append(pltpu.VMEM((3,) + live_dims(RS_ORDERS[s][:k + 1]) + tail, jnp.bfloat16))
    return pl.pallas_call(
        rs_kernel, out_shape=outs,
        in_specs=[pl.BlockSpec(memory_space=pl.ANY)] * len(grads),
        out_specs=[pl.BlockSpec(memory_space=pltpu.VMEM)] * len(grads),
        scratch_shapes=held + held + slots[0] + slots[1] + slots[2] + [
            pltpu.SemaphoreType.DMA((n,)), pltpu.SemaphoreType.DMA((n,)), pltpu.SemaphoreType.DMA((n,)),
            pltpu.SemaphoreType.DMA((n, 3, 4)), pltpu.SemaphoreType.DMA((n, 3, 4))],
        compiler_params=pltpu.CompilerParams(collective_id=1, has_side_effects=True, vmem_limit_bytes=60 << 20),
        name="scatter_grads",
    )(*grads)


def scan_kernel(backward, *refs):
    local, tags, fade, carried = refs[0], refs[1], refs[2], refs[3]
    tags_all = refs[4]
    came, going, tag_send, tag_recv, send1, recv1, send2, recv2 = refs[5:]
    me = lax.axis_index("seq")
    dp = lax.axis_index("dp")
    n = 16
    barrier = pltpu.get_barrier_semaphore()
    def greet(k, _):
        pl.semaphore_signal(barrier, inc=1, device_id=(dp, (me + k) % n), device_id_type=MESH)
        return 0
    lax.fori_loop(1, n, greet, 0)
    tags_all[me] = tags[...]
    came[me] = local[me]
    pl.semaphore_wait(barrier, n - 1)

    def tag_copy(to):
        return pltpu.make_async_remote_copy(src_ref=tags, dst_ref=tags_all.at[me], send_sem=tag_send.at[to],
            recv_sem=tag_recv.at[me], device_id=(dp, to), device_id_type=MESH)
    def state_copy(to):
        return pltpu.make_async_remote_copy(src_ref=local.at[to], dst_ref=came.at[me], send_sem=send1.at[to],
            recv_sem=recv1.at[me], device_id=(dp, to), device_id_type=MESH)
    def back_copy(to):
        return pltpu.make_async_remote_copy(src_ref=going.at[to], dst_ref=carried.at[me], send_sem=send2.at[to],
            recv_sem=recv2.at[me], device_id=(dp, to), device_id_type=MESH)
    def arrival(ref, ssem, rsem, frm):
        return pltpu.make_async_remote_copy(src_ref=ref.at[frm], dst_ref=ref.at[frm], send_sem=ssem.at[frm],
            recv_sem=rsem.at[frm], device_id=(dp, (me + 1) % n), device_id_type=MESH)

    def start1(k, _):
        to = (me + k) % n
        tag_copy(to).start()
        state_copy(to).start()
        return 0
    lax.fori_loop(1, n, start1, 0)
    def wait1(k, _):
        frm = (me + k) % n
        arrival(tags_all, tag_send, tag_recv, frm).wait_recv()
        arrival(came, send1, recv1, frm).wait_recv()
        return 0
    lax.fori_loop(1, n, wait1, 0)

    micro, head = me // 8, me % 8
    lam = fade[pl.ds(head, 1), :]
    def first(b):
        return tags_all[b, pl.ds(2 * micro, 1), :]
    def last(b):
        return tags_all[b, pl.ds(2 * micro + 1, 1), :]
    acc = jnp.zeros((128, 128), jnp.float32)
    order = range(n - 1, -1, -1) if backward else range(n)
    previous = None
    for b in order:
        going[b] = acc.astype(jnp.bfloat16)
        whole = first(b) == last(b)
        if previous is None:
            acc = came[b].astype(jnp.float32)
        else:
            near = (last(b) == first(previous)) if backward else (first(b) == last(previous))
            acc = came[b].astype(jnp.float32) + jnp.where(whole & near, lam, 0.0) * acc
        previous = b
    carried[me] = going[me]
    def start2(k, _):
        back_copy((me + k) % n).start()
        return 0
    lax.fori_loop(1, n, start2, 0)
    def wait2(k, _):
        frm = (me + k) % n
        arrival(carried, send2, recv2, frm).wait_recv()
        return 0
    lax.fori_loop(1, n, wait2, 0)
    def drain(k, _):
        to = (me + k) % n
        tag_copy(to).wait_send()
        state_copy(to).wait_send()
        back_copy(to).wait_send()
        return 0
    lax.fori_loop(1, n, drain, 0)


def scan_states(local, tags, fade, backward):
    D = pltpu.SemaphoreType.DMA
    v = pl.BlockSpec(memory_space=pltpu.VMEM)
    return pl.pallas_call(
        functools.partial(scan_kernel, backward),
        out_shape=[jax.ShapeDtypeStruct((16, 128, 128), jnp.bfloat16), jax.ShapeDtypeStruct((16, 8, 128), jnp.float32)],
        in_specs=[v] * 3, out_specs=[v] * 2,
        scratch_shapes=[pltpu.VMEM((16, 128, 128), jnp.bfloat16), pltpu.VMEM((16, 128, 128), jnp.bfloat16)] + [D((16,))] * 6,
        compiler_params=pltpu.CompilerParams(collective_id=3 if backward else 2, has_side_effects=True),
        name="scan_back" if backward else "scan_ahead",
    )(local, tags, fade)


D = 1024
H = 8
HD = 128
FF = 2816
EPSILON = 1e-06


def swish(values):
    return values * jax.nn.sigmoid(values)


def swish_slope(values):
    sigma = jax.nn.sigmoid(values)
    return sigma * (1.0 + values * (1.0 - sigma))


def rms_factor(values):
    return lax.rsqrt(jnp.mean(values * values, axis=-1, keepdims=True) + EPSILON)


def norm_back(upstream, normed, factor):
    return factor * (upstream - normed * jnp.mean(upstream * normed, axis=-1, keepdims=True))


def matmul(form, left_op, right_op):
    return jnp.einsum(form, left_op, right_op, preferred_element_type=jnp.float32)


def on_device(hidden_in, seg_ids, decay_rates, grad_out, w_query, w_key, w_value, w_gate, w_output, w_left, w_right, w_down):
    micros, length = hidden_in.shape[0], hidden_in.shape[2]
    rows = micros * length
    low = jnp.bfloat16
    pieces = [
        jnp.concatenate([w.reshape(8, D) for w in (w_query, w_key, w_value, w_gate)], axis=1),
        w_output.reshape(8, D),
        jnp.concatenate([w.reshape(8, FF) for w in (w_left, w_right)], axis=1),
        w_down.reshape(176, 128),
    ]
    m_in, m_output, m_up, m_down = gather_all(pieces)
    m_in = m_in.reshape(D, 4 * D)
    m_output = m_output.reshape(D, D)
    m_up = m_up.reshape(D, 2 * FF)
    m_down = m_down.reshape(FF, D)

    segments = seg_ids.reshape(micros, length)
    tags = jnp.stack([segments[0, 0], segments[0, -1], segments[1, 0], segments[1, -1]]).astype(jnp.float32)
    tags = jnp.concatenate([tags, jnp.zeros((4,), jnp.float32)])[:, None] * jnp.ones((8, 128), jnp.float32)
    fade = jnp.exp(-length * decay_rates)[:, None] * jnp.ones((8, 128), jnp.float32)
    places = jnp.arange(length, dtype=jnp.float32)
    distance = places[:, None] - places[None, :]
    allowed = (distance >= 0.0)[None] & (segments[:, :, None] == segments[:, None, :])
    decay_mask = jnp.where(
        allowed[:, None], jnp.exp(-decay_rates[None, :, None, None] * jnp.maximum(distance, 0.0)[None, None]), 0.0)
    rising = jnp.exp(-(places + 1.0)[None, :, None] * decay_rates)
    falling = jnp.exp(-(length - 1.0 - places)[None, :, None] * decay_rates)

    inputs = hidden_in.reshape(rows, D).astype(jnp.float32)
    factor_in = rms_factor(inputs)
    normed_in = inputs * factor_in
    first_in = normed_in.astype(low)
    pre = matmul("rd,de->re", first_in, m_in)
    q_pre, k_pre, v_pre, gate = (pre[:, k * D:(k + 1) * D] for k in range(4))
    heads = (micros, length, H, HD)
    queries = swish(q_pre).astype(low).reshape(heads)
    key_rows = swish(k_pre).astype(low).reshape(heads)
    value_rows = v_pre.astype(low).reshape(heads)
    keeping = falling * (segments == segments[:, -1:]).astype(jnp.float32)[:, :, None]
    kept = (key_rows.astype(jnp.float32) * keeping[..., None]).astype(low)
    local = matmul("sjhd,sjhe->shde", kept, value_rows).astype(low).reshape(micros * H, HD, HD)
    carried, tags_all = scan_states(local, tags, fade, False)
    carried = carried.reshape(micros, H, HD, HD)
    me = lax.axis_index("seq")
    ends = tags_all[:, :4, 0]
    before = jnp.where(me > 0, ends[jnp.maximum(me - 1, 0)], -1.0)
    after = jnp.where(me < 15, ends[jnp.minimum(me + 1, 15)], -1.0)
    boundary = before[1::2]
    reverse_tag = after[0::2]
    tokens = segments.astype(jnp.float32)
    scores = matmul("sihd,sjhd->shij", queries, key_rows)
    weighted = (scores * decay_mask).astype(low)
    within = matmul("shij,sjhe->sihe", weighted, value_rows)
    reaching = rising * (tokens == boundary[:, None]).astype(jnp.float32)[:, :, None]
    crossed = matmul("sihd,shde->sihe", queries, carried) * reaching[..., None]
    mixed = (within + crossed).reshape(rows, D)
    factor_mix = rms_factor(mixed)
    normed_mix = mixed * factor_mix
    gated = (normed_mix * gate).astype(low)
    resid = inputs + matmul("rd,de->re", gated, m_output)
    factor_res = rms_factor(resid)
    normed_res = resid * factor_res
    second = normed_res.astype(low)
    up = matmul("rd,df->rf", second, m_up)
    left_proj, right_proj = up[:, :FF], up[:, FF:]
    product = (left_proj * right_proj).astype(low)
    result = (resid + matmul("rf,fd->rd", product, m_down)).astype(low)

    d_branch = grad_out.reshape(rows, D)
    cotangent = d_branch.astype(jnp.float32)
    g_down = matmul("rf,rd->fd", product, d_branch).astype(low)
    d_prod = matmul("rd,fd->rf", d_branch, m_down)
    d_up = jnp.concatenate([(d_prod * right_proj).astype(low), (d_prod * left_proj).astype(low)], axis=1)
    g_up = matmul("rd,rf->df", second, d_up).astype(low)
    d_second = matmul("rf,df->rd", d_up, m_up)
    d_resid = cotangent + norm_back(d_second, normed_res, factor_res)
    d_attn = d_resid.astype(low)
    g_output = matmul("rd,re->de", gated, d_attn).astype(low)
    d_gated = matmul("re,de->rd", d_attn, m_output)
    d_gate = (d_gated * normed_mix).astype(low)
    d_mixed = norm_back(d_gated * gate, normed_mix, factor_mix).astype(low).reshape(heads)
    d_weighted = matmul("sihe,sjhe->shij", d_mixed, value_rows)
    d_scores = (d_weighted * decay_mask).astype(low)
    opening = rising * (segments == segments[:, :1]).astype(jnp.float32)[:, :, None]
    opened = (queries.astype(jnp.float32) * opening[..., None]).astype(low)
    back_local = matmul("sihd,sihe->shde", opened, d_mixed).astype(low).reshape(micros * H, HD, HD)
    reverse, _ = scan_states(back_local, tags, fade, True)
    reverse = reverse.reshape(micros, H, HD, HD)
    d_query = matmul("shij,sjhd->sihd", d_scores, key_rows)
    d_query = d_query + matmul("sihe,shde->sihd", d_mixed, carried) * reaching[..., None]
    d_key = matmul("shij,sihd->sjhd", d_scores, queries)
    d_value = matmul("shij,sihe->sjhe", weighted, d_mixed)
    closing = falling * (tokens == reverse_tag[:, None]).astype(jnp.float32)[:, :, None]
    d_key = d_key + matmul("sjhe,shde->sjhd", value_rows, reverse) * closing[..., None]
    d_value = d_value + matmul("sjhd,shde->sjhe", key_rows, reverse) * closing[..., None]
    d_pre = jnp.concatenate([
        (d_query.reshape(rows, D) * swish_slope(q_pre)).astype(low),
        (d_key.reshape(rows, D) * swish_slope(k_pre)).astype(low),
        d_value.reshape(rows, D).astype(low),
        d_gate,
    ], axis=1)
    g_in = matmul("rd,re->de", first_in, d_pre).astype(low)
    d_first = matmul("re,de->rd", d_pre, m_in)
    d_inputs = d_resid + norm_back(d_first, normed_in, factor_in)

    owners = (4, 2, 4, 2, 2)
    s_in, s_output, s_up, s_down = scatter_all([
        g_in.reshape(owners + (8, 4 * D)), g_output.reshape(owners + (8, D)),
        g_up.reshape(owners + (8, 2 * FF)), g_down.reshape(owners + (176, 128))])
    shape = hidden_in.shape
    return (
        result.reshape(shape), d_inputs.reshape(shape),
        *(s_in[:, k * D:(k + 1) * D].reshape(-1) for k in range(4)),
        s_output.reshape(-1), s_up[:, :FF].reshape(-1), s_up[:, FF:].reshape(-1), s_down.reshape(-1),
    )


def solution(mesh):
    tokens = P(None, "dp", "seq", None)
    flat = P(("dp", "seq"))
    return jax.shard_map(
        on_device, mesh=mesh,
        in_specs=(tokens, P(None, "dp", "seq"), P(), tokens) + (flat,) * 8,
        out_specs=(tokens, tokens) + (flat,) * 8,
        check_vma=False,
    )
```

```python
import functools
import jax, jax.numpy as jnp
from jax import lax
from jax.experimental import pallas as pl
from jax.experimental.pallas import tpu as pltpu
from jax.sharding import PartitionSpec as P

MESH = pl.DeviceIdType.MESH
RING = 4
D = 1024
H = 8
HD = 128
FF = 2816
ROWS = 256
N_SEQ = 16
EPSILON = 1e-06
LOW = jnp.bfloat16
F32 = jnp.float32
OWNERS = (4, 2, 4, 2, 2)
DMA = pltpu.SemaphoreType.DMA
ORDERS = (("x", "y", "z"), ("y", "z", "x"), ("z", "x", "y"))
SPLIT_ROWS = (False, False, False, True)


def tiles(array, bounds, grain=128):
    return [(array, s, lo * grain, hi * grain) for s, (lo, hi) in enumerate(zip(bounds[:-1], bounds[1:]))]


CHUNKS = (
    tuple(tiles(0, (0, 11, 22, 32)) + tiles(1, (0, 2, 5, 8))),
    tuple(tiles(2, (0, 15, 30, 44))),
    tuple(tiles(3, (0, 7, 14, 22), 8)),
)
UNITS = CHUNKS[0] + CHUNKS[1] + CHUNKS[2]
C1, C2, C3 = (tuple(UNITS.index(u) for u in chunk) for chunk in CHUNKS)


def where_am_i():
    dp = lax.axis_index("dp")
    seq = lax.axis_index("seq")
    return {"x": (seq // 2 % 2) * 2 + dp % 2, "y": dp // 2, "z": seq // 4, "c": seq % 2}


def device(at):
    return (at["y"] * 2 + at["x"] % 2, at["z"] * 4 + (at["x"] // 2) * 2 + at["c"])


def moved(at, axis, by):
    out = dict(at)
    out[axis] = (at[axis] + by) % RING if axis != "c" else 1 - at[axis]
    return out


def block(ref, at, whole, lo, hi, rows):
    every = slice(None)
    pick = lambda axis, value: every if axis in whole else value
    span = pl.ds(lo, hi - lo)
    return ref.at[
        pick("y", at["y"]), pick("x", at["x"] % 2), pick("z", at["z"]), pick("x", at["x"] // 2), at["c"],
        span if rows else every, every if rows else span,
    ]


def middle(lo, hi, rows):
    grain = 8 if rows else 128
    return lo + ((hi - lo) // grain // 2) * grain


def neighbours(me):
    return [moved(me, a, d) for a in "xyz" for d in (1, -1)] + [moved(me, "c", 1)]


def dot(a, b, dims=((1,), (0,))):
    return lax.dot_general(a, b, (dims, ((), ())), preferred_element_type=F32)


def by_rows(count, size, body):
    def one(k, _):
        body(pl.ds(pl.multiple_of(k * size, size), size))
        return 0
    lax.fori_loop(0, count // size, one, 0)


def columns_of(k, size):
    return pl.ds(pl.multiple_of(k * size, size), size)


def sigmoid(u):
    return 1.0 / (1.0 + jnp.exp(-u))


def rms_factor(v):
    return lax.rsqrt(jnp.mean(v * v, axis=-1, keepdims=True) + EPSILON)


class Gather:
    def __init__(self, arrays, me, send_sem, recv_sem, csend_sem, crecv_sem):
        self.arrays, self.me = arrays, me
        self.send_sem, self.recv_sem, self.csend_sem, self.crecv_sem = send_sem, recv_sem, csend_sem, crecv_sem
        self.sends = []

    def copy(self, ref, u, slot, to):
        return pltpu.make_async_remote_copy(src_ref=ref, dst_ref=ref, send_sem=self.send_sem.at[u, slot],
            recv_sem=self.recv_sem.at[u, slot], device_id=device(to), device_id_type=MESH)

    def ccopy(self, ref, u, slot):
        return pltpu.make_async_remote_copy(src_ref=ref, dst_ref=ref, send_sem=self.csend_sem.at[u, slot],
            recv_sem=self.crecv_sem.at[u, slot], device_id=device(moved(self.me, "c", 1)), device_id_type=MESH)

    def go(self, cp):
        cp.start()
        self.sends.append(cp)

    def part(self, u, at, stage, half=None):
        i, s, lo, hi = UNITS[u]
        rows = SPLIT_ROWS[i]
        mid = middle(lo, hi, rows)
        lo, hi = (lo, hi) if half is None else ((lo, mid), (mid, hi))[half]
        return block(self.arrays[i], at, ORDERS[s][:stage], lo, hi, rows)

    def axis(self, u, stage):
        return ORDERS[UNITS[u][1]][stage]

    def begin(self, units, stage):
        for u in units:
            a = self.axis(u, stage)
            mine = self.part(u, self.me, stage)
            self.go(self.copy(mine, u, 4 * stage, moved(self.me, a, 1)))
            self.go(self.copy(mine, u, 4 * stage + 1, moved(self.me, a, -1)))
            if stage == 2:
                self.go(self.ccopy(mine, u, 0))

    def relay(self, units, stage):
        for u in units:
            a = self.axis(u, stage)
            above, below = moved(self.me, a, 1), moved(self.me, a, -1)
            self.copy(self.part(u, below, stage), u, 4 * stage, below).wait_recv()
            self.go(self.copy(self.part(u, below, stage, 0), u, 4 * stage + 2, above))
            self.copy(self.part(u, above, stage), u, 4 * stage + 1, above).wait_recv()
            self.go(self.copy(self.part(u, above, stage, 1), u, 4 * stage + 3, below))
            if stage == 2:
                self.go(self.ccopy(self.part(u, below, stage), u, 1))
                self.go(self.ccopy(self.part(u, above, stage), u, 2))

    def finish(self, units, stage):
        for u in units:
            a = self.axis(u, stage)
            far = moved(self.me, a, 2)
            for half in range(2):
                self.copy(self.part(u, far, stage, half), u, 4 * stage + 2 + half, moved(self.me, a, 1)).wait_recv()
            if stage == 2:
                self.go(self.ccopy(self.part(u, far, stage), u, 3))

    def arrive(self, units):
        sib = moved(self.me, "c", 1)
        for u in units:
            for k, by in enumerate((0, -1, 1, 2)):
                self.ccopy(self.part(u, moved(sib, self.axis(u, 2), by), 2), u, k).wait_recv()

    def drain(self):
        for cp in self.sends:
            cp.wait_send()


class Scan:
    def __init__(self, local, came, going, carried, sems):
        self.me, self.dp = lax.axis_index("seq"), lax.axis_index("dp")
        self.local, self.came, self.going, self.carried = local, came, going, carried
        self.send1, self.recv1, self.send2, self.recv2 = sems

    def to(self, k):
        return (self.me + k) % N_SEQ

    def out(self, to):
        return pltpu.make_async_remote_copy(src_ref=self.local.at[to], dst_ref=self.came.at[self.me], send_sem=self.send1.at[to],
            recv_sem=self.recv1.at[self.me], device_id=(self.dp, to), device_id_type=MESH)

    def back(self, to):
        return pltpu.make_async_remote_copy(src_ref=self.going.at[to], dst_ref=self.carried.at[self.me], send_sem=self.send2.at[to],
            recv_sem=self.recv2.at[self.me], device_id=(self.dp, to), device_id_type=MESH)

    def arrival(self, ref, ssem, rsem, frm):
        return pltpu.make_async_remote_copy(src_ref=ref.at[frm], dst_ref=ref.at[frm], send_sem=ssem.at[frm],
            recv_sem=rsem.at[frm], device_id=(self.dp, self.to(1)), device_id_type=MESH)

    def each(self, body):
        def one(k, _):
            body(self.to(k))
            return 0
        lax.fori_loop(1, N_SEQ, one, 0)

    def start(self):
        self.each(lambda to: self.out(to).start())
        self.came[self.me] = self.local[self.me]

    def join(self, tags_all, decays, backward):
        self.each(lambda frm: self.arrival(self.came, self.send1, self.recv1, frm).wait_recv())
        micro, head = self.me // H, self.me % H
        fade = jnp.exp(-float(HD) * jnp.full((1, HD), decays[head], F32))
        first = lambda b: tags_all[b, pl.ds(2 * micro, 1), :]
        last = lambda b: tags_all[b, pl.ds(2 * micro + 1, 1), :]
        acc = jnp.zeros((HD, HD), F32)
        previous = None
        for b in (range(N_SEQ - 1, -1, -1) if backward else range(N_SEQ)):
            self.going[b] = acc.astype(LOW)
            if previous is None:
                acc = self.came[b].astype(F32)
            else:
                near = (last(b) == first(previous)) if backward else (first(b) == last(previous))
                acc = self.came[b].astype(F32) + jnp.where((first(b) == last(b)) & near, fade, 0.0) * acc
            previous = b
        self.carried[self.me] = self.going[self.me]
        self.each(lambda to: self.back(to).start())

    def finish(self):
        self.each(lambda frm: self.arrival(self.carried, self.send2, self.recv2, frm).wait_recv())

    def drain(self):
        def one(to):
            self.out(to).wait_send()
            self.back(to).wait_send()
        self.each(one)


def spread(row):
    across = jnp.broadcast_to(row, (HD, HD))
    return across.T, across


def row_index():
    return lax.broadcasted_iota(jnp.int32, (HD, HD), 0).astype(F32)


def column_index():
    return lax.broadcasted_iota(jnp.int32, (HD, HD), 1).astype(F32)


def pair_at(p):
    micro, head = p // H, p % H
    return micro, head, pl.ds(pl.multiple_of(micro * HD, HD), HD), pl.ds(pl.multiple_of(head * HD, HD), HD)


def forward_kernel(*refs):
    (x, ids, decays), small = refs[:3], refs[3:11]
    (act, pre, mixed, resid, up, carried, tags_all, out_in, out_output, out_up, out_down) = refs[11:22]
    (w_in, w_output, w_up, w_flat, w_down, first_in, qs, ks, vs, gated, second, product, local, came, going,
     spare, tag, allowed, kept_mask, ids_down,
     send_sem, recv_sem, csend_sem, crecv_sem, tag_send, tag_recv, s1, r1, s2, r2, out_sem) = refs[22:]
    me = where_am_i()
    seq, dp = lax.axis_index("seq"), lax.axis_index("dp")
    to = lambda k: (seq + k) % N_SEQ
    barrier = pltpu.get_barrier_semaphore()
    close = neighbours(me)
    for other in close:
        pl.semaphore_signal(barrier, inc=1, device_id=device(other), device_id_type=MESH)

    def greet(k, _):
        pl.semaphore_signal(barrier, inc=1, device_id=(dp, to(k)), device_id_type=MESH)
        return 0
    lax.fori_loop(1, N_SEQ, greet, 0)

    here = (me["y"], me["x"] % 2, me["z"], me["x"] // 2, me["c"])
    def place(src, target, base, width):
        n = width // 128
        spare[pl.ds(0, 8 * n), :] = src[...].astype(F32)
        for c in range(n):
            target[(*here, slice(None), pl.ds(base + c * 128, 128))] = spare[pl.ds(c, 8, stride=n), :].astype(LOW)
    for k in range(4):
        place(small[k], w_in, k * D, D)
    place(small[4], w_output, 0, D)
    place(small[5], w_up, 0, FF)
    place(small[6], w_up, FF, FF)
    w_flat[here] = small[7][...]
    for m in range(2):
        down, across = spread(ids[m:m + 1, :])
        ids_down[m] = down
        allowed[m] = jnp.where((down == across) & (row_index() >= column_index()), 1.0, 0.0)
        kept_mask[m] = jnp.where(down == jnp.broadcast_to(ids[m:m + 1, HD - 1:HD], (HD, HD)), 1.0, 0.0)
    tag[...] = jnp.zeros((8, HD), F32)
    for m in range(2):
        tag[2 * m:2 * m + 1, :] = jnp.broadcast_to(ids[m:m + 1, 0:1], (1, HD))
        tag[2 * m + 1:2 * m + 2, :] = jnp.broadcast_to(ids[m:m + 1, HD - 1:HD], (1, HD))
    tags_all[seq] = tag[...]
    pl.semaphore_wait(barrier, len(close) + N_SEQ - 1)

    g = Gather((w_in, w_output, w_up, w_flat), me, send_sem, recv_sem, csend_sem, crecv_sem)
    scan = Scan(local, came, going, carried, (s1, r1, s2, r2))
    g.begin(C1, 0)
    g.begin(C2, 0)
    g.begin(C3, 0)

    def tag_copy(other):
        return pltpu.make_async_remote_copy(src_ref=tag, dst_ref=tags_all.at[seq], send_sem=tag_send.at[other],
            recv_sem=tag_recv.at[seq], device_id=(dp, other), device_id_type=MESH)
    scan.each(lambda other: tag_copy(other).start())

    def norm_in(rows):
        v = x[rows, :].astype(F32)
        first_in[rows, :] = (v * rms_factor(v)).astype(LOW)
    by_rows(ROWS, 32, norm_in)

    g.relay(C1, 0)
    g.relay(C2, 0)
    g.relay(C3, 0)
    g.finish(C1, 0)
    g.begin(C1, 1)
    g.finish(C2, 0)
    g.begin(C2, 1)
    g.finish(C3, 0)
    g.begin(C3, 1)
    g.relay(C1, 1)
    g.relay(C2, 1)
    g.relay(C3, 1)
    g.finish(C1, 1)
    g.begin(C1, 2)
    g.finish(C2, 1)
    g.finish(C3, 1)
    g.relay(C1, 2)
    g.begin(C2, 2)
    g.finish(C1, 2)
    g.arrive(C1)
    keep = [pltpu.make_async_copy(w_in, out_in, out_sem.at[0]), pltpu.make_async_copy(w_output, out_output, out_sem.at[1])]
    for cp in keep:
        cp.start()

    m_in = w_in.reshape(D, 4 * D)
    def project(k, _):
        cols = columns_of(k, 512)
        pre[:, cols] = dot(first_in[...], m_in[:, cols])
        return 0
    lax.fori_loop(0, 8, project, 0)
    g.relay(C2, 2)
    g.begin(C3, 2)

    def rows_of_heads(rows):
        q = pre[rows, 0:D]
        qs[rows, :] = (q * sigmoid(q)).astype(LOW)
        k = pre[rows, D:2 * D]
        ks[rows, :] = (k * sigmoid(k)).astype(LOW)
        vs[rows, :] = pre[rows, 2 * D:3 * D].astype(LOW)
    by_rows(ROWS, 16, rows_of_heads)

    def states(p, _):
        micro, head, rows, cols = pair_at(p)
        keeping = jnp.exp((row_index() - (HD - 1.0)) * decays[head]) * kept_mask[micro]
        kept = (ks[rows, cols].astype(F32) * keeping).astype(LOW)
        local[p] = dot(kept, vs[rows, cols], ((0,), (0,))).astype(LOW)
        return 0
    lax.fori_loop(0, 2 * H, states, 0)
    scan.start()
    g.finish(C2, 2)

    def within(p, _):
        micro, head, rows, cols = pair_at(p)
        mask = allowed[micro] * jnp.exp(jnp.minimum(column_index() - row_index(), 0.0) * decays[head])
        weighted = (dot(qs[rows, cols], ks[rows, cols], ((1,), (1,))) * mask).astype(LOW)
        mixed[rows, cols] = dot(weighted, vs[rows, cols])
        return 0
    lax.fori_loop(0, 2 * H, within, 0)
    scan.each(lambda frm: pltpu.make_async_remote_copy(src_ref=tag, dst_ref=tags_all.at[frm], send_sem=tag_send.at[frm],
        recv_sem=tag_recv.at[frm], device_id=(dp, to(1)), device_id_type=MESH).wait_recv())
    scan.join(tags_all, decays, False)
    g.relay(C3, 2)
    scan.finish()

    def crossing(p, _):
        micro, head, rows, cols = pair_at(p)
        boundary = jnp.where(seq > 0, tags_all[jnp.maximum(seq - 1, 0), pl.ds(2 * micro + 1, 1), :], -1.0)
        reaching = jnp.where(ids_down[micro] == boundary, jnp.exp(-(row_index() + 1.0) * decays[head]), 0.0)
        mixed[rows, cols] += dot(qs[rows, cols], carried[p]) * reaching
        return 0
    lax.fori_loop(0, 2 * H, crossing, 0)

    def gate_rows(rows):
        v = mixed[rows, :]
        gated[rows, :] = (v * rms_factor(v) * pre[rows, 3 * D:4 * D]).astype(LOW)
    by_rows(ROWS, 16, gate_rows)
    m_output = w_output.reshape(D, D)
    def output(k, _):
        cols = columns_of(k, 512)
        resid[:, cols] = x[:, cols].astype(F32) + dot(gated[...], m_output[:, cols])
        return 0
    lax.fori_loop(0, 2, output, 0)
    def norm_second(rows):
        v = resid[rows, :]
        second[rows, :] = (v * rms_factor(v)).astype(LOW)
    by_rows(ROWS, 32, norm_second)
    g.finish(C3, 2)
    g.arrive(C2)
    keep.append(pltpu.make_async_copy(w_up, out_up, out_sem.at[2]))
    keep[-1].start()
    m_up = w_up.reshape(D, 2 * FF)
    def widen(k, _):
        cols = columns_of(k, 512)
        up[:, cols] = dot(second[...], m_up[:, cols])
        return 0
    lax.fori_loop(0, 11, widen, 0)
    def multiply(rows):
        product[rows, :] = (up[rows, 0:FF] * up[rows, FF:2 * FF]).astype(LOW)
    by_rows(ROWS, 16, multiply)
    g.arrive(C3)
    flat = w_flat.reshape(128 * 176, 128)
    def arrange(k, _):
        spare[...] = flat[pl.ds(pl.multiple_of(k * 1408, 1408), 1408), :].astype(F32)
        for c in range(8):
            w_down[pl.ds(pl.multiple_of(k * 176, 176), 176), c * 128:(c + 1) * 128] = spare[pl.ds(c, 176, stride=8), :].astype(LOW)
        return 0
    lax.fori_loop(0, 16, arrange, 0)
    keep.append(pltpu.make_async_copy(w_down, out_down, out_sem.at[3]))
    keep[-1].start()
    def last(k, _):
        cols = columns_of(k, 512)
        act[:, cols] = (resid[:, cols] + dot(product[...], w_down[:, cols])).astype(LOW)
        return 0
    lax.fori_loop(0, 2, last, 0)
    for cp in keep:
        cp.wait()
    scan.each(lambda other: tag_copy(other).wait_send())
    scan.drain()
    g.drain()


def forward(x, ids, decays, pieces):
    v = pl.BlockSpec(memory_space=pltpu.VMEM)
    anywhere = pl.BlockSpec(memory_space=pl.ANY)
    sds = jax.ShapeDtypeStruct
    n = len(UNITS)
    outs = [sds((ROWS, D), LOW), sds((ROWS, 4 * D), F32), sds((ROWS, D), F32), sds((ROWS, D), F32), sds((ROWS, 2 * FF), F32),
        sds((N_SEQ, HD, HD), LOW), sds((N_SEQ, 8, HD), F32),
        sds(OWNERS + (8, 4 * D), LOW), sds(OWNERS + (8, D), LOW), sds(OWNERS + (8, 2 * FF), LOW), sds((FF, D), LOW)]
    vm = pltpu.VMEM
    scratch = [vm(OWNERS + (8, 4 * D), LOW), vm(OWNERS + (8, D), LOW), vm(OWNERS + (8, 2 * FF), LOW), vm(OWNERS + (176, 128), LOW),
        vm((FF, D), LOW)] + [vm((ROWS, D), LOW)] * 6 + [vm((ROWS, FF), LOW)] + [vm((N_SEQ, HD, HD), LOW)] * 3 + [
        vm((1408, 128), F32), vm((8, HD), F32)] + [vm((2, HD, HD), F32)] * 3 + [
        DMA((n, 12)), DMA((n, 12)), DMA((n, 4)), DMA((n, 4))] + [DMA((N_SEQ,))] * 6 + [DMA((4,))]
    return pl.pallas_call(
        forward_kernel, out_shape=outs,
        in_specs=[v, v, pl.BlockSpec(memory_space=pltpu.SMEM)] + [v] * 8,
        out_specs=[v] * 7 + [anywhere] * 4,
        scratch_shapes=scratch,
        compiler_params=pltpu.CompilerParams(collective_id=0, has_side_effects=True, vmem_limit_bytes=60 << 20),
        name="gather_and_forward",
    )(x, ids, decays, *pieces)

RS_UNITS = (
    (0, 0, 0, 13 * 128), (0, 1, 13 * 128, 26 * 128), (0, 2, 26 * 128, 32 * 128),
    (1, 2, 0, 8 * 128),
    (2, 0, 0, 22 * 128), (2, 1, 22 * 128, 44 * 128),
    (3, 2, 0, 176),
)


RS_ORDERS = tuple(o[::-1] for o in ORDERS)
SIZES = {"y": (4,), "x": (2, 2), "z": (4,)}
DIMS = (("y", 4), ("x", 2), ("z", 4), ("x", 2))


def live_dims(fixed):
    return tuple(n for a, n in DIMS if a not in fixed)


def part(ref, at, fixed, gone, lo, hi, rows, lead=()):
    every = slice(None)
    idx = []
    for k, (a, n) in enumerate(DIMS):
        if a in gone:
            continue
        if a in fixed:
            idx.append((at["x"] % 2 if k == 1 else at["x"] // 2) if a == "x" else at[a])
        else:
            idx.append(every)
    span = pl.ds(lo, hi - lo)
    return ref.at[(*lead, *idx, span if rows else every, every if rows else span)]


def accumulate(dst, srcs, dims, out=None):
    n = 1
    for d in dims:
        n *= d
    def one(k, _):
        idx = []
        rest = k
        for d in dims[::-1]:
            idx.append(rest % d)
            rest = rest // d
        idx = tuple(idx[::-1])
        total = dst[idx].astype(jnp.float32) if dims else dst[...].astype(jnp.float32)
        for s in srcs:
            total = total + (s[idx] if dims else s[...]).astype(jnp.float32)
        target = dst if out is None else out
        if dims:
            target[idx] = total.astype(target.dtype)
        else:
            target[...] = total.astype(target.dtype)
        return 0
    if n == 1:
        one(0, 0)
    else:
        lax.fori_loop(0, n, one, 0)


def rs_kernel(*refs):
    n_arr, n = 4, len(RS_UNITS)
    ins, outs = refs[:n_arr], refs[n_arr:2 * n_arr]
    refs = refs[2 * n_arr:]
    held, other = refs[:n], refs[n:2 * n]
    slots = [refs[2 * n + k * n: 3 * n + k * n] for k in range(3)]
    load_sem, csend_sem, crecv_sem, send_sem, recv_sem = refs[5 * n:]
    me = where_am_i()
    sib = moved(me, "c", 1)
    barrier = pltpu.get_barrier_semaphore()
    partners = [moved(me, a, d) for a in "xyz" for d in (1, -1)] + [sib]
    for one in partners:
        pl.semaphore_signal(barrier, inc=1, device_id=device(one), device_id_type=MESH)
    loads = []
    def half_of(i, c, lo, hi, rows):
        every, span = slice(None), pl.ds(lo, hi - lo)
        return ins[i].at[:, :, :, :, c, span if rows else every, every if rows else span]
    for u, (i, s, lo, hi) in enumerate(RS_UNITS):
        cp = pltpu.make_async_copy(half_of(i, me["c"], lo, hi, SPLIT_ROWS[i]), held[u], load_sem.at[u])
        cp.start()
        loads.append(cp)
    pl.semaphore_wait(barrier, len(partners))
    sends = []
    for u, (i, s, lo, hi) in enumerate(RS_UNITS):
        cp = pltpu.make_async_remote_copy(src_ref=half_of(i, sib["c"], lo, hi, SPLIT_ROWS[i]), dst_ref=other[u],
            send_sem=csend_sem.at[u], recv_sem=crecv_sem.at[u], device_id=device(sib), device_id_type=MESH)
        cp.start()
        sends.append(cp)

    def send(src, dst, u, stage, slot, to):
        cp = pltpu.make_async_remote_copy(src_ref=src, dst_ref=dst, send_sem=send_sem.at[u, stage, slot],
            recv_sem=recv_sem.at[u, stage, slot], device_id=device(to), device_id_type=MESH)
        cp.start()
        sends.append(cp)

    def got(ref, u, stage, slot):
        pltpu.make_async_remote_copy(src_ref=ref, dst_ref=ref, send_sem=send_sem.at[u, stage, slot],
            recv_sem=recv_sem.at[u, stage, slot], device_id=device(sib), device_id_type=MESH).wait_recv()

    def spans(u):
        i, s, lo, hi = RS_UNITS[u]
        width = hi - lo
        return s, SPLIT_ROWS[i], width, middle(0, width, SPLIT_ROWS[i])

    def send_far(u, stage):
        s, rows, width, mid = spans(u)
        order = RS_ORDERS[s]
        axis, gone, fixed = order[stage], order[:stage], order[:stage + 1]
        far = moved(me, axis, 2)
        send(part(held[u], far, fixed, (), 0, mid, rows), part(slots[stage][u], me, (), fixed, 0, mid, rows, (0,)), u, stage, 0, moved(me, axis, 1))
        send(part(held[u], far, fixed, (), mid, width, rows), part(slots[stage][u], me, (), fixed, mid, width, rows, (0,)), u, stage, 1, moved(me, axis, -1))

    for u in range(n):
        loads[u].wait()
        pltpu.make_async_remote_copy(src_ref=other[u], dst_ref=other[u], send_sem=csend_sem.at[u], recv_sem=crecv_sem.at[u],
            device_id=device(sib), device_id_type=MESH).wait_recv()
        accumulate(held[u], [other[u]], live_dims(()))
        send_far(u, 0)
    for stage in range(3):
        for u in range(n):
            s, rows, width, mid = spans(u)
            order = RS_ORDERS[s]
            axis, fixed = order[stage], order[:stage + 1]
            above, below = moved(me, axis, 1), moved(me, axis, -1)
            dims = live_dims(fixed)
            for k, (to, lo, hi) in enumerate(((above, 0, mid), (below, mid, width))):
                came = part(slots[stage][u], me, (), fixed, lo, hi, rows, (0,))
                got(came, u, stage, k)
                accumulate(part(held[u], to, fixed, (), lo, hi, rows), [came], dims)
                send(part(held[u], to, fixed, (), 0, width, rows), part(slots[stage][u], me, (), fixed, 0, width, rows, (1 + k,)), u, stage, 2 + k, to)
        for u in range(n):
            i, _, lo, hi = RS_UNITS[u]
            s, rows, width, mid = spans(u)
            order = RS_ORDERS[s]
            fixed = order[:stage + 1]
            came = []
            for k in range(2):
                ref = part(slots[stage][u], me, (), fixed, 0, width, rows, (1 + k,))
                got(ref, u, stage, 2 + k)
                came.append(ref)
            mine = part(held[u], me, fixed, (), 0, width, rows)
            if stage == 2:
                span = pl.ds(lo, hi - lo)
                accumulate(mine, came, (), outs[i].at[(span, slice(None)) if rows else (slice(None), span)])
            else:
                accumulate(mine, came, live_dims(fixed))
                send_far(u, stage + 1)
    for cp in sends:
        cp.wait_send()


def scatter_all(grads):
    outs = [jax.ShapeDtypeStruct(g.shape[5:], jnp.float32) for g in grads]
    n = len(RS_UNITS)
    held, slots = [], [[], [], []]
    for i, s, lo, hi in RS_UNITS:
        tail = (hi - lo, 128) if SPLIT_ROWS[i] else (8, hi - lo)
        held.append(pltpu.VMEM(live_dims(()) + tail, jnp.bfloat16))
        for k in range(3):
            slots[k].append(pltpu.VMEM((3,) + live_dims(RS_ORDERS[s][:k + 1]) + tail, jnp.bfloat16))
    return pl.pallas_call(
        rs_kernel, out_shape=outs,
        in_specs=[pl.BlockSpec(memory_space=pl.ANY)] * len(grads),
        out_specs=[pl.BlockSpec(memory_space=pltpu.VMEM)] * len(grads),
        scratch_shapes=held + held + slots[0] + slots[1] + slots[2] + [
            pltpu.SemaphoreType.DMA((n,)), pltpu.SemaphoreType.DMA((n,)), pltpu.SemaphoreType.DMA((n,)),
            pltpu.SemaphoreType.DMA((n, 3, 4)), pltpu.SemaphoreType.DMA((n, 3, 4))],
        compiler_params=pltpu.CompilerParams(collective_id=1, has_side_effects=True, vmem_limit_bytes=60 << 20),
        name="scatter_grads",
    )(*grads)


def scan_kernel(backward, *refs):
    local, tags, fade, carried = refs[0], refs[1], refs[2], refs[3]
    tags_all = refs[4]
    came, going, tag_send, tag_recv, send1, recv1, send2, recv2 = refs[5:]
    me = lax.axis_index("seq")
    dp = lax.axis_index("dp")
    n = 16
    barrier = pltpu.get_barrier_semaphore()
    def greet(k, _):
        pl.semaphore_signal(barrier, inc=1, device_id=(dp, (me + k) % n), device_id_type=MESH)
        return 0
    lax.fori_loop(1, n, greet, 0)
    tags_all[me] = tags[...]
    came[me] = local[me]
    pl.semaphore_wait(barrier, n - 1)

    def tag_copy(to):
        return pltpu.make_async_remote_copy(src_ref=tags, dst_ref=tags_all.at[me], send_sem=tag_send.at[to],
            recv_sem=tag_recv.at[me], device_id=(dp, to), device_id_type=MESH)
    def state_copy(to):
        return pltpu.make_async_remote_copy(src_ref=local.at[to], dst_ref=came.at[me], send_sem=send1.at[to],
            recv_sem=recv1.at[me], device_id=(dp, to), device_id_type=MESH)
    def back_copy(to):
        return pltpu.make_async_remote_copy(src_ref=going.at[to], dst_ref=carried.at[me], send_sem=send2.at[to],
            recv_sem=recv2.at[me], device_id=(dp, to), device_id_type=MESH)
    def arrival(ref, ssem, rsem, frm):
        return pltpu.make_async_remote_copy(src_ref=ref.at[frm], dst_ref=ref.at[frm], send_sem=ssem.at[frm],
            recv_sem=rsem.at[frm], device_id=(dp, (me + 1) % n), device_id_type=MESH)

    def start1(k, _):
        to = (me + k) % n
        tag_copy(to).start()
        state_copy(to).start()
        return 0
    lax.fori_loop(1, n, start1, 0)
    def wait1(k, _):
        frm = (me + k) % n
        arrival(tags_all, tag_send, tag_recv, frm).wait_recv()
        arrival(came, send1, recv1, frm).wait_recv()
        return 0
    lax.fori_loop(1, n, wait1, 0)

    micro, head = me // 8, me % 8
    lam = fade[pl.ds(head, 1), :]
    def first(b):
        return tags_all[b, pl.ds(2 * micro, 1), :]
    def last(b):
        return tags_all[b, pl.ds(2 * micro + 1, 1), :]
    acc = jnp.zeros((128, 128), jnp.float32)
    order = range(n - 1, -1, -1) if backward else range(n)
    previous = None
    for b in order:
        going[b] = acc.astype(jnp.bfloat16)
        whole = first(b) == last(b)
        if previous is None:
            acc = came[b].astype(jnp.float32)
        else:
            near = (last(b) == first(previous)) if backward else (first(b) == last(previous))
            acc = came[b].astype(jnp.float32) + jnp.where(whole & near, lam, 0.0) * acc
        previous = b
    carried[me] = going[me]
    def start2(k, _):
        back_copy((me + k) % n).start()
        return 0
    lax.fori_loop(1, n, start2, 0)
    def wait2(k, _):
        frm = (me + k) % n
        arrival(carried, send2, recv2, frm).wait_recv()
        return 0
    lax.fori_loop(1, n, wait2, 0)
    def drain(k, _):
        to = (me + k) % n
        tag_copy(to).wait_send()
        state_copy(to).wait_send()
        back_copy(to).wait_send()
        return 0
    lax.fori_loop(1, n, drain, 0)


def scan_states(local, tags, fade, backward):
    D = pltpu.SemaphoreType.DMA
    v = pl.BlockSpec(memory_space=pltpu.VMEM)
    return pl.pallas_call(
        functools.partial(scan_kernel, backward),
        out_shape=[jax.ShapeDtypeStruct((16, 128, 128), jnp.bfloat16), jax.ShapeDtypeStruct((16, 8, 128), jnp.float32)],
        in_specs=[v] * 3, out_specs=[v] * 2,
        scratch_shapes=[pltpu.VMEM((16, 128, 128), jnp.bfloat16), pltpu.VMEM((16, 128, 128), jnp.bfloat16)] + [D((16,))] * 6,
        compiler_params=pltpu.CompilerParams(collective_id=3 if backward else 2, has_side_effects=True),
        name="scan_back" if backward else "scan_ahead",
    )(local, tags, fade)


def swish_slope(values):
    sigma = jax.nn.sigmoid(values)
    return sigma * (1.0 + values * (1.0 - sigma))


def norm_back(upstream, normed, factor):
    return factor * (upstream - normed * jnp.mean(upstream * normed, axis=-1, keepdims=True))


def matmul(form, left_op, right_op):
    return jnp.einsum(form, left_op, right_op, preferred_element_type=jnp.float32)


def on_device(hidden_in, seg_ids, decay_rates, grad_out, *weights):
    micros, length = hidden_in.shape[0], hidden_in.shape[2]
    rows = micros * length
    low = jnp.bfloat16
    segments = seg_ids.reshape(micros, length)
    tokens = segments.astype(jnp.float32)
    (act, pre, mixed, resid, up, carried, tags_all, m_in, m_output, m_up, m_down) = forward(
        hidden_in.reshape(rows, D), tokens, decay_rates, [w.reshape(-1, 128) for w in weights])
    m_in, m_output, m_up = m_in.reshape(D, 4 * D), m_output.reshape(D, D), m_up.reshape(D, 2 * FF)

    places = jnp.arange(length, dtype=jnp.float32)
    distance = places[:, None] - places[None, :]
    allowed = (distance >= 0.0)[None] & (segments[:, :, None] == segments[:, None, :])
    decay_mask = jnp.where(
        allowed[:, None], jnp.exp(-decay_rates[None, :, None, None] * jnp.maximum(distance, 0.0)[None, None]), 0.0)
    rising = jnp.exp(-(places + 1.0)[None, :, None] * decay_rates)
    falling = jnp.exp(-(length - 1.0 - places)[None, :, None] * decay_rates)
    fade = jnp.exp(-length * decay_rates)[:, None] * jnp.ones((8, 128), jnp.float32)
    inputs = hidden_in.reshape(rows, D).astype(jnp.float32)
    factor_in = rms_factor(inputs)
    normed_in = inputs * factor_in
    first_in = normed_in.astype(low)
    q_pre, k_pre, v_pre, gate = (pre[:, k * D:(k + 1) * D] for k in range(4))
    heads = (micros, length, H, HD)
    queries = (q_pre * jax.nn.sigmoid(q_pre)).astype(low).reshape(heads)
    key_rows = (k_pre * jax.nn.sigmoid(k_pre)).astype(low).reshape(heads)
    value_rows = v_pre.astype(low).reshape(heads)
    carried = carried.reshape(micros, H, HD, HD)
    me = lax.axis_index("seq")
    ends = tags_all[:, :4, 0]
    before = jnp.where(me > 0, ends[jnp.maximum(me - 1, 0)], -1.0)
    after = jnp.where(me < 15, ends[jnp.minimum(me + 1, 15)], -1.0)
    boundary = before[1::2]
    reverse_tag = after[0::2]
    scores = matmul("sihd,sjhd->shij", queries, key_rows)
    weighted = (scores * decay_mask).astype(low)
    reaching = rising * (tokens == boundary[:, None]).astype(jnp.float32)[:, :, None]
    factor_mix = rms_factor(mixed)
    normed_mix = mixed * factor_mix
    gated = (normed_mix * gate).astype(low)
    factor_res = rms_factor(resid)
    normed_res = resid * factor_res
    second = normed_res.astype(low)
    left_proj, right_proj = up[:, :FF], up[:, FF:]
    product = (left_proj * right_proj).astype(low)

    d_branch = grad_out.reshape(rows, D)
    cotangent = d_branch.astype(jnp.float32)
    g_down = matmul("rf,rd->fd", product, d_branch).astype(low)
    d_prod = matmul("rd,fd->rf", d_branch, m_down)
    d_up = jnp.concatenate([(d_prod * right_proj).astype(low), (d_prod * left_proj).astype(low)], axis=1)
    g_up = matmul("rd,rf->df", second, d_up).astype(low)
    d_second = matmul("rf,df->rd", d_up, m_up)
    d_resid = cotangent + norm_back(d_second, normed_res, factor_res)
    d_attn = d_resid.astype(low)
    g_output = matmul("rd,re->de", gated, d_attn).astype(low)
    d_gated = matmul("re,de->rd", d_attn, m_output)
    d_gate = (d_gated * normed_mix).astype(low)
    d_mixed = norm_back(d_gated * gate, normed_mix, factor_mix).astype(low).reshape(heads)
    d_weighted = matmul("sihe,sjhe->shij", d_mixed, value_rows)
    d_scores = (d_weighted * decay_mask).astype(low)
    opening = rising * (segments == segments[:, :1]).astype(jnp.float32)[:, :, None]
    opened = (queries.astype(jnp.float32) * opening[..., None]).astype(low)
    back_local = matmul("sihd,sihe->shde", opened, d_mixed).astype(low).reshape(micros * H, HD, HD)
    tags = jnp.stack([segments[0, 0], segments[0, -1], segments[1, 0], segments[1, -1]]).astype(jnp.float32)
    tags = jnp.concatenate([tags, jnp.zeros((4,), jnp.float32)])[:, None] * jnp.ones((8, 128), jnp.float32)
    reverse, _ = scan_states(back_local, tags, fade, True)
    reverse = reverse.reshape(micros, H, HD, HD)
    d_query = matmul("shij,sjhd->sihd", d_scores, key_rows)
    d_query = d_query + matmul("sihe,shde->sihd", d_mixed, carried) * reaching[..., None]
    d_key = matmul("shij,sihd->sjhd", d_scores, queries)
    d_value = matmul("shij,sihe->sjhe", weighted, d_mixed)
    closing = falling * (tokens == reverse_tag[:, None]).astype(jnp.float32)[:, :, None]
    d_key = d_key + matmul("sjhe,shde->sjhd", value_rows, reverse) * closing[..., None]
    d_value = d_value + matmul("sjhd,shde->sjhe", key_rows, reverse) * closing[..., None]
    d_pre = jnp.concatenate([
        (d_query.reshape(rows, D) * swish_slope(q_pre)).astype(low),
        (d_key.reshape(rows, D) * swish_slope(k_pre)).astype(low),
        d_value.reshape(rows, D).astype(low),
        d_gate,
    ], axis=1)
    g_in = matmul("rd,re->de", first_in, d_pre).astype(low)
    d_first = matmul("re,de->rd", d_pre, m_in)
    d_inputs = d_resid + norm_back(d_first, normed_in, factor_in)

    s_in, s_output, s_up, s_down = scatter_all([
        g_in.reshape(OWNERS + (8, 4 * D)), g_output.reshape(OWNERS + (8, D)),
        g_up.reshape(OWNERS + (8, 2 * FF)), g_down.reshape(OWNERS + (176, 128))])
    shape = hidden_in.shape
    return (
        act.reshape(shape), d_inputs.reshape(shape),
        *(s_in[:, k * D:(k + 1) * D].reshape(-1) for k in range(4)),
        s_output.reshape(-1), s_up[:, :FF].reshape(-1), s_up[:, FF:].reshape(-1), s_down.reshape(-1),
    )


def solution(mesh):
    tokens = P(None, "dp", "seq", None)
    flat = P(("dp", "seq"))
    return jax.shard_map(
        on_device, mesh=mesh,
        in_specs=(tokens, P(None, "dp", "seq"), P(), tokens) + (flat,) * 8,
        out_specs=(tokens, tokens) + (flat,) * 8,
        check_vma=False,
    )
```

```python
import functools
import jax, jax.numpy as jnp
from jax import lax
from jax.experimental import pallas as pl
from jax.experimental.pallas import tpu as pltpu
from jax.sharding import PartitionSpec as P

MESH = pl.DeviceIdType.MESH
RING = 4
D = 1024
H = 8
HD = 128
FF = 2816
ROWS = 256
N_SEQ = 16
EPSILON = 1e-06
LOW = jnp.bfloat16
F32 = jnp.float32
OWNERS = (4, 2, 4, 2, 2)
DMA = pltpu.SemaphoreType.DMA
ORDERS = (("x", "y", "z"), ("y", "z", "x"), ("z", "x", "y"))
SPLIT_ROWS = (False, False, False, True)


def tiles(array, bounds, grain=128):
    return [(array, s, lo * grain, hi * grain) for s, (lo, hi) in enumerate(zip(bounds[:-1], bounds[1:]))]


CHUNKS = (
    tuple(tiles(0, (0, 11, 22, 32)) + tiles(1, (0, 2, 5, 8))),
    tuple(tiles(2, (0, 15, 30, 44))),
    tuple(tiles(3, (0, 7, 14, 22), 8)),
)
UNITS = CHUNKS[0] + CHUNKS[1] + CHUNKS[2]
C1, C2, C3 = (tuple(UNITS.index(u) for u in chunk) for chunk in CHUNKS)


def where_am_i():
    dp = lax.axis_index("dp")
    seq = lax.axis_index("seq")
    return {"x": (seq // 2 % 2) * 2 + dp % 2, "y": dp // 2, "z": seq // 4, "c": seq % 2}


def device(at):
    return (at["y"] * 2 + at["x"] % 2, at["z"] * 4 + (at["x"] // 2) * 2 + at["c"])


def moved(at, axis, by):
    out = dict(at)
    out[axis] = (at[axis] + by) % RING if axis != "c" else 1 - at[axis]
    return out


def block(ref, at, whole, lo, hi, rows):
    every = slice(None)
    pick = lambda axis, value: every if axis in whole else value
    span = pl.ds(lo, hi - lo)
    return ref.at[
        pick("y", at["y"]), pick("x", at["x"] % 2), pick("z", at["z"]), pick("x", at["x"] // 2), at["c"],
        span if rows else every, every if rows else span,
    ]


def middle(lo, hi, rows):
    grain = 8 if rows else 128
    return lo + ((hi - lo) // grain // 2) * grain


def neighbours(me):
    return [moved(me, a, d) for a in "xyz" for d in (1, -1)] + [moved(me, "c", 1)]


def dot(a, b, dims=((1,), (0,))):
    return lax.dot_general(a, b, (dims, ((), ())), preferred_element_type=F32)


def by_rows(count, size, body):
    def one(k, _):
        body(pl.ds(pl.multiple_of(k * size, size), size))
        return 0
    lax.fori_loop(0, count // size, one, 0)


def columns_of(k, size):
    return pl.ds(pl.multiple_of(k * size, size), size)


def sigmoid(u):
    return 1.0 / (1.0 + jnp.exp(-u))


def rms_factor(v):
    return lax.rsqrt(jnp.mean(v * v, axis=-1, keepdims=True) + EPSILON)


class Gather:
    def __init__(self, arrays, me, send_sem, recv_sem, csend_sem, crecv_sem):
        self.arrays, self.me = arrays, me
        self.send_sem, self.recv_sem, self.csend_sem, self.crecv_sem = send_sem, recv_sem, csend_sem, crecv_sem
        self.sends = []

    def copy(self, ref, u, slot, to):
        return pltpu.make_async_remote_copy(src_ref=ref, dst_ref=ref, send_sem=self.send_sem.at[u, slot],
            recv_sem=self.recv_sem.at[u, slot], device_id=device(to), device_id_type=MESH)

    def ccopy(self, ref, u, slot):
        return pltpu.make_async_remote_copy(src_ref=ref, dst_ref=ref, send_sem=self.csend_sem.at[u, slot],
            recv_sem=self.crecv_sem.at[u, slot], device_id=device(moved(self.me, "c", 1)), device_id_type=MESH)

    def go(self, cp):
        cp.start()
        self.sends.append(cp)

    def part(self, u, at, stage, half=None):
        i, s, lo, hi = UNITS[u]
        rows = SPLIT_ROWS[i]
        mid = middle(lo, hi, rows)
        lo, hi = (lo, hi) if half is None else ((lo, mid), (mid, hi))[half]
        return block(self.arrays[i], at, ORDERS[s][:stage], lo, hi, rows)

    def axis(self, u, stage):
        return ORDERS[UNITS[u][1]][stage]

    def begin(self, units, stage):
        for u in units:
            a = self.axis(u, stage)
            mine = self.part(u, self.me, stage)
            self.go(self.copy(mine, u, 4 * stage, moved(self.me, a, 1)))
            self.go(self.copy(mine, u, 4 * stage + 1, moved(self.me, a, -1)))
            if stage == 2:
                self.go(self.ccopy(mine, u, 0))

    def relay(self, units, stage):
        for u in units:
            a = self.axis(u, stage)
            above, below = moved(self.me, a, 1), moved(self.me, a, -1)
            self.copy(self.part(u, below, stage), u, 4 * stage, below).wait_recv()
            self.go(self.copy(self.part(u, below, stage, 0), u, 4 * stage + 2, above))
            self.copy(self.part(u, above, stage), u, 4 * stage + 1, above).wait_recv()
            self.go(self.copy(self.part(u, above, stage, 1), u, 4 * stage + 3, below))
            if stage == 2:
                self.go(self.ccopy(self.part(u, below, stage), u, 1))
                self.go(self.ccopy(self.part(u, above, stage), u, 2))

    def finish(self, units, stage):
        for u in units:
            a = self.axis(u, stage)
            far = moved(self.me, a, 2)
            for half in range(2):
                self.copy(self.part(u, far, stage, half), u, 4 * stage + 2 + half, moved(self.me, a, 1)).wait_recv()
            if stage == 2:
                self.go(self.ccopy(self.part(u, far, stage), u, 3))

    def arrive(self, units):
        sib = moved(self.me, "c", 1)
        for u in units:
            for k, by in enumerate((0, -1, 1, 2)):
                self.ccopy(self.part(u, moved(sib, self.axis(u, 2), by), 2), u, k).wait_recv()

    def drain(self):
        for cp in self.sends:
            cp.wait_send()


class Scan:
    def __init__(self, local, came, going, carried, sems):
        self.me, self.dp = lax.axis_index("seq"), lax.axis_index("dp")
        self.local, self.came, self.going, self.carried = local, came, going, carried
        self.send1, self.recv1, self.send2, self.recv2 = sems

    def to(self, k):
        return (self.me + k) % N_SEQ

    def out(self, to):
        return pltpu.make_async_remote_copy(src_ref=self.local.at[to], dst_ref=self.came.at[self.me], send_sem=self.send1.at[to],
            recv_sem=self.recv1.at[self.me], device_id=(self.dp, to), device_id_type=MESH)

    def back(self, to):
        return pltpu.make_async_remote_copy(src_ref=self.going.at[to], dst_ref=self.carried.at[self.me], send_sem=self.send2.at[to],
            recv_sem=self.recv2.at[self.me], device_id=(self.dp, to), device_id_type=MESH)

    def arrival(self, ref, ssem, rsem, frm):
        return pltpu.make_async_remote_copy(src_ref=ref.at[frm], dst_ref=ref.at[frm], send_sem=ssem.at[frm],
            recv_sem=rsem.at[frm], device_id=(self.dp, self.to(1)), device_id_type=MESH)

    def each(self, body):
        def one(k, _):
            body(self.to(k))
            return 0
        lax.fori_loop(1, N_SEQ, one, 0)

    def start(self):
        self.each(lambda to: self.out(to).start())
        self.came[self.me] = self.local[self.me]

    def join(self, tags_all, decays, backward):
        self.each(lambda frm: self.arrival(self.came, self.send1, self.recv1, frm).wait_recv())
        micro, head = self.me // H, self.me % H
        fade = jnp.exp(-float(HD) * jnp.full((1, HD), decays[head], F32))
        first = lambda b: tags_all[b, pl.ds(2 * micro, 1), :]
        last = lambda b: tags_all[b, pl.ds(2 * micro + 1, 1), :]
        acc = jnp.zeros((HD, HD), F32)
        previous = None
        for b in (range(N_SEQ - 1, -1, -1) if backward else range(N_SEQ)):
            self.going[b] = acc.astype(LOW)
            if previous is None:
                acc = self.came[b].astype(F32)
            else:
                near = (last(b) == first(previous)) if backward else (first(b) == last(previous))
                acc = self.came[b].astype(F32) + jnp.where((first(b) == last(b)) & near, fade, 0.0) * acc
            previous = b
        self.carried[self.me] = self.going[self.me]
        self.each(lambda to: self.back(to).start())

    def finish(self):
        self.each(lambda frm: self.arrival(self.carried, self.send2, self.recv2, frm).wait_recv())

    def drain(self):
        def one(to):
            self.out(to).wait_send()
            self.back(to).wait_send()
        self.each(one)


def spread(row):
    across = jnp.broadcast_to(row, (HD, HD))
    return across.T, across


def row_index():
    return lax.broadcasted_iota(jnp.int32, (HD, HD), 0).astype(F32)


def column_index():
    return lax.broadcasted_iota(jnp.int32, (HD, HD), 1).astype(F32)


def pair_at(p):
    micro, head = p // H, p % H
    return micro, head, pl.ds(pl.multiple_of(micro * HD, HD), HD), pl.ds(pl.multiple_of(head * HD, HD), HD)


def transpose_into(src, dst, count):
    def one(k, _):
        at = columns_of(k, 128)
        dst[at, :] = src[:, at].T
        return 0
    lax.fori_loop(0, count // 128, one, 0)


def forward_kernel(*refs):
    (x, cot, ids, decays), small = refs[:4], refs[4:12]
    (act, tags_all, o_qkv, o_slopes, o_gate, o_mixed, o_resid, o_up, o_carried, o_in, o_output, o_wide, o_down,
     t_first, t_gated, t_second, t_product, b_branch) = refs[12:30]
    (w_in, w_output, w_up, w_flat, w_down, pre, first_in, qkv, slopes, gate, mixed, resid, up, gated, second, product,
     first_t, gated_t, second_t, product_t, carried, local, came, going, spare, tag, allowed, kept_mask, ids_down,
     send_sem, recv_sem, csend_sem, crecv_sem, tag_send, tag_recv, s1, r1, s2, r2, out_sem, pass_send, pass_recv) = refs[30:]
    me = where_am_i()
    sib = moved(me, "c", 1)
    seq, dp = lax.axis_index("seq"), lax.axis_index("dp")
    to = lambda k: (seq + k) % N_SEQ
    barrier = pltpu.get_barrier_semaphore()
    close = neighbours(me)
    for other in close:
        pl.semaphore_signal(barrier, inc=1, device_id=device(other), device_id_type=MESH)

    def greet(k, _):
        pl.semaphore_signal(barrier, inc=1, device_id=(dp, to(k)), device_id_type=MESH)
        return 0
    lax.fori_loop(1, N_SEQ, greet, 0)

    here = (me["y"], me["x"] % 2, me["z"], me["x"] // 2, me["c"])
    def place(src, target, base, width):
        n = width // 128
        spare[pl.ds(0, 8 * n), :] = src[...].astype(F32)
        for c in range(n):
            target[(*here, slice(None), pl.ds(base + c * 128, 128))] = spare[pl.ds(c, 8, stride=n), :].astype(LOW)
    for k in range(4):
        place(small[k], w_in, k * D, D)
    place(small[4], w_output, 0, D)
    place(small[5], w_up, 0, FF)
    place(small[6], w_up, FF, FF)
    w_flat[here] = small[7][...]
    tag[...] = jnp.zeros((8, HD), F32)
    for m in range(2):
        tag[2 * m:2 * m + 1, :] = jnp.broadcast_to(ids[m:m + 1, 0:1], (1, HD))
        tag[2 * m + 1:2 * m + 2, :] = jnp.broadcast_to(ids[m:m + 1, HD - 1:HD], (1, HD))
    tags_all[seq] = tag[...]
    pl.semaphore_wait(barrier, len(close) + N_SEQ - 1)

    g = Gather((w_in, w_output, w_up, w_flat), me, send_sem, recv_sem, csend_sem, crecv_sem)
    scan = Scan(local, came, going, carried, (s1, r1, s2, r2))
    g.begin(C1, 0)
    g.begin(C2, 0)
    g.begin(C3, 0)

    kept, passed = [], []
    def keep(src, dst):
        cp = pltpu.make_async_copy(src, dst, out_sem.at[len(kept)])
        cp.start()
        kept.append(cp)
    def hand(mine, theirs, dst):
        keep(mine, dst.at[me["c"]])
        k = len(passed)
        cp = pltpu.make_async_remote_copy(src_ref=theirs, dst_ref=dst.at[me["c"]], send_sem=pass_send.at[k],
            recv_sem=pass_recv.at[k], device_id=device(sib), device_id_type=MESH)
        cp.start()
        passed.append((cp, dst))

    def tag_copy(other):
        return pltpu.make_async_remote_copy(src_ref=tag, dst_ref=tags_all.at[seq], send_sem=tag_send.at[other],
            recv_sem=tag_recv.at[seq], device_id=(dp, other), device_id_type=MESH)
    scan.each(lambda other: tag_copy(other).start())

    def norm_in(rows):
        v = x[rows, :].astype(F32)
        first_in[rows, :] = (v * rms_factor(v)).astype(LOW)
    by_rows(ROWS, 32, norm_in)
    g.relay(C1, 0)
    g.relay(C2, 0)
    g.relay(C3, 0)
    for m in range(2):
        down, across = spread(ids[m:m + 1, :])
        ids_down[m] = down
        allowed[m] = jnp.where((down == across) & (row_index() >= column_index()), 1.0, 0.0)
        kept_mask[m] = jnp.where(down == jnp.broadcast_to(ids[m:m + 1, HD - 1:HD], (HD, HD)), 1.0, 0.0)
    half = lambda c: cot.at[:, pl.ds(pl.multiple_of(c * 512, 512), 512)]
    hand(half(me["c"]), half(sib["c"]), b_branch)
    g.finish(C1, 0)
    g.begin(C1, 1)
    g.finish(C2, 0)
    g.begin(C2, 1)
    g.finish(C3, 0)
    g.begin(C3, 1)
    g.relay(C1, 1)
    g.relay(C2, 1)
    g.relay(C3, 1)
    g.finish(C1, 1)
    g.begin(C1, 2)
    g.finish(C2, 1)
    g.finish(C3, 1)
    transpose_into(first_in, first_t, D)
    hand(first_t, first_t, t_first)
    g.relay(C1, 2)
    g.begin(C2, 2)
    g.finish(C1, 2)
    g.arrive(C1)
    keep(w_in, o_in)
    keep(w_output, o_output)

    m_in = w_in.reshape(D, 4 * D)
    def project(k, _):
        cols = columns_of(k, 512)
        pre[:, cols] = dot(first_in[...], m_in[:, cols])
        return 0
    lax.fori_loop(0, 8, project, 0)
    g.relay(C2, 2)
    g.begin(C3, 2)

    def rows_of_heads(rows):
        for k in range(2):
            u = pre[rows, k * D:(k + 1) * D]
            s = sigmoid(u)
            qkv[rows, k * D:(k + 1) * D] = (u * s).astype(LOW)
            slopes[rows, k * D:(k + 1) * D] = (s * (1.0 + u * (1.0 - s))).astype(LOW)
        qkv[rows, 2 * D:3 * D] = pre[rows, 2 * D:3 * D].astype(LOW)
        gate[rows, :] = pre[rows, 3 * D:4 * D].astype(LOW)
    by_rows(ROWS, 16, rows_of_heads)
    keep(qkv, o_qkv)
    keep(slopes, o_slopes)
    keep(gate, o_gate)

    def states(p, _):
        micro, head, rows, _ = pair_at(p)
        keeping = jnp.exp((row_index() - (HD - 1.0)) * decays[head]) * kept_mask[micro]
        held = (qkv[rows, head_of(head, 1)].astype(F32) * keeping).astype(LOW)
        local[p] = dot(held, qkv[rows, head_of(head, 2)], ((0,), (0,))).astype(LOW)
        return 0
    lax.fori_loop(0, 2 * H, states, 0)
    scan.start()
    g.finish(C2, 2)

    def within(p, _):
        micro, head, rows, cols = pair_at(p)
        mask = allowed[micro] * jnp.exp(jnp.minimum(column_index() - row_index(), 0.0) * decays[head])
        weighted = (dot(qkv[rows, head_of(head, 0)], qkv[rows, head_of(head, 1)], ((1,), (1,))) * mask).astype(LOW)
        mixed[rows, cols] = dot(weighted, qkv[rows, head_of(head, 2)])
        return 0
    lax.fori_loop(0, 2 * H, within, 0)
    scan.each(lambda frm: pltpu.make_async_remote_copy(src_ref=tag, dst_ref=tags_all.at[frm], send_sem=tag_send.at[frm],
        recv_sem=tag_recv.at[frm], device_id=(dp, to(1)), device_id_type=MESH).wait_recv())
    scan.join(tags_all, decays, False)
    g.relay(C3, 2)
    scan.finish()
    keep(carried, o_carried)

    def crossing(p, _):
        micro, head, rows, cols = pair_at(p)
        boundary = jnp.where(seq > 0, tags_all[jnp.maximum(seq - 1, 0), pl.ds(2 * micro + 1, 1), :], -1.0)
        reaching = jnp.where(ids_down[micro] == boundary, jnp.exp(-(row_index() + 1.0) * decays[head]), 0.0)
        mixed[rows, cols] += dot(qkv[rows, head_of(head, 0)], carried[p]) * reaching
        return 0
    lax.fori_loop(0, 2 * H, crossing, 0)
    keep(mixed, o_mixed)

    def gate_rows(rows):
        v = mixed[rows, :]
        gated[rows, :] = (v * rms_factor(v) * pre[rows, 3 * D:4 * D]).astype(LOW)
    by_rows(ROWS, 16, gate_rows)
    m_output = w_output.reshape(D, D)
    def output(k, _):
        cols = columns_of(k, 512)
        resid[:, cols] = x[:, cols].astype(F32) + dot(gated[...], m_output[:, cols])
        return 0
    lax.fori_loop(0, 2, output, 0)
    keep(resid, o_resid)
    def norm_second(rows):
        v = resid[rows, :]
        second[rows, :] = (v * rms_factor(v)).astype(LOW)
    by_rows(ROWS, 32, norm_second)
    g.finish(C3, 2)
    g.arrive(C2)
    keep(w_up, o_wide)
    m_up = w_up.reshape(D, 2 * FF)
    def widen(k, _):
        cols, more = columns_of(k, 256), pl.ds(pl.multiple_of(k * 256 + FF, 256), 256)
        left = dot(second[...], m_up[:, cols])
        right = dot(second[...], m_up[:, more])
        up[:, cols] = left.astype(LOW)
        up[:, more] = right.astype(LOW)
        product[:, cols] = (left * right).astype(LOW)
        return 0
    lax.fori_loop(0, 11, widen, 0)
    keep(up, o_up)
    transpose_into(product, product_t, FF)
    hand(product_t, product_t, t_product)
    transpose_into(gated, gated_t, D)
    hand(gated_t, gated_t, t_gated)
    transpose_into(second, second_t, D)
    hand(second_t, second_t, t_second)
    g.arrive(C3)
    flat = w_flat.reshape(128 * 176, 128)
    def arrange(k, _):
        spare[...] = flat[pl.ds(pl.multiple_of(k * 1408, 1408), 1408), :].astype(F32)
        for c in range(8):
            w_down[pl.ds(pl.multiple_of(k * 176, 176), 176), c * 128:(c + 1) * 128] = spare[pl.ds(c, 176, stride=8), :].astype(LOW)
        return 0
    lax.fori_loop(0, 16, arrange, 0)
    keep(w_down, o_down)
    def last(k, _):
        cols = columns_of(k, 512)
        act[:, cols] = (resid[:, cols] + dot(product[...], w_down[:, cols])).astype(LOW)
        return 0
    lax.fori_loop(0, 2, last, 0)
    for cp in kept:
        cp.wait()
    for k, (cp, dst) in enumerate(passed):
        cp.wait_send()
        there = dst.at[sib["c"]]
        pltpu.make_async_remote_copy(src_ref=there, dst_ref=there, send_sem=pass_send.at[k], recv_sem=pass_recv.at[k],
            device_id=device(sib), device_id_type=MESH).wait_recv()
    scan.each(lambda other: tag_copy(other).wait_send())
    scan.drain()
    g.drain()


def forward(x, cot, ids, decays, pieces):
    v = pl.BlockSpec(memory_space=pltpu.VMEM)
    anywhere = pl.BlockSpec(memory_space=pl.ANY)
    sds = jax.ShapeDtypeStruct
    n = len(UNITS)
    outs = [sds((ROWS, D), LOW), sds((N_SEQ, 8, HD), F32), sds((ROWS, 3 * D), LOW), sds((ROWS, 2 * D), LOW), sds((ROWS, D), LOW),
        sds((ROWS, D), F32), sds((ROWS, D), F32), sds((ROWS, 2 * FF), LOW), sds((N_SEQ, HD, HD), LOW),
        sds(OWNERS + (8, 4 * D), LOW), sds(OWNERS + (8, D), LOW), sds(OWNERS + (8, 2 * FF), LOW), sds((FF, D), LOW),
        sds((2, D, ROWS), LOW), sds((2, D, ROWS), LOW), sds((2, D, ROWS), LOW), sds((2, FF, ROWS), LOW), sds((2, ROWS, D // 2), LOW)]
    vm = pltpu.VMEM
    scratch = [vm(OWNERS + (8, 4 * D), LOW), vm(OWNERS + (8, D), LOW), vm(OWNERS + (8, 2 * FF), LOW), vm(OWNERS + (176, 128), LOW),
        vm((FF, D), LOW), vm((ROWS, 4 * D), F32), vm((ROWS, D), LOW), vm((ROWS, 3 * D), LOW), vm((ROWS, 2 * D), LOW), vm((ROWS, D), LOW),
        vm((ROWS, D), F32), vm((ROWS, D), F32), vm((ROWS, 2 * FF), LOW), vm((ROWS, D), LOW), vm((ROWS, D), LOW), vm((ROWS, FF), LOW),
        vm((D, ROWS), LOW), vm((D, ROWS), LOW), vm((D, ROWS), LOW), vm((FF, ROWS), LOW)] + [vm((N_SEQ, HD, HD), LOW)] * 4 + [
        vm((1408, 128), F32), vm((8, HD), F32)] + [vm((2, HD, HD), F32)] * 3 + [
        DMA((n, 12)), DMA((n, 12)), DMA((n, 4)), DMA((n, 4))] + [DMA((N_SEQ,))] * 6 + [DMA((20,)), DMA((5,)), DMA((5,))]
    return pl.pallas_call(
        forward_kernel, out_shape=outs,
        in_specs=[v, v, v, pl.BlockSpec(memory_space=pltpu.SMEM)] + [v] * 8,
        out_specs=[v] * 2 + [anywhere] * 16,
        scratch_shapes=scratch,
        compiler_params=pltpu.CompilerParams(collective_id=0, has_side_effects=True, vmem_limit_bytes=60 << 20),
        name="gather_and_forward",
    )(x, cot, ids, decays, *pieces)


def head_of(head, part):
    return pl.ds(pl.multiple_of(part * D + head * HD, HD), HD)


DOWN, WIDE, OUTPUT, INPUT = range(4)
HELD = ((88, 256), (16, FF), (16, D // 2), (16, 2 * D))
BACK_UNITS = tuple(tiles(DOWN, (0, 3, 7, 11), 8) + tiles(WIDE, (0, 7, 14, 22)) + tiles(OUTPUT, (0, 2, 4)) + tiles(INPUT, (0, 5, 10, 16)))
BACK_OF = [tuple(u for u, unit in enumerate(BACK_UNITS) if unit[0] == i) for i in range(4)]
BACK_ORDERS = tuple(order[::-1] for order in ORDERS)
DIMS = (("y", 4), ("x", 2), ("z", 4), ("x", 2))


def live_dims(fixed):
    return tuple(n for a, n in DIMS if a not in fixed)


def part_of(ref, at, fixed, gone, lo, hi, rows, lead=()):
    every = slice(None)
    idx = []
    for k, (a, n) in enumerate(DIMS):
        if a in gone:
            continue
        if a in fixed:
            idx.append((at["x"] % 2 if k == 1 else at["x"] // 2) if a == "x" else at[a])
        else:
            idx.append(every)
    span = pl.ds(lo, hi - lo)
    return ref.at[(*lead, *idx, span if rows else every, every if rows else span)]


def accumulate(dst, srcs, dims, out=None):
    target = dst if out is None else out
    def one(k, _):
        idx, rest = [], k
        for d in dims[::-1]:
            idx.append(rest % d)
            rest = rest // d
        at = tuple(idx[::-1]) if dims else ...
        total = dst[at].astype(F32)
        for s in srcs:
            total = total + s[at].astype(F32)
        target[at] = total.astype(target.dtype)
        return 0
    n = 1
    for d in dims:
        n *= d
    if n == 1:
        one(0, 0)
    else:
        lax.fori_loop(0, n, one, 0)


class Scatter:
    def __init__(self, held, slots, final, me, send_sem, recv_sem):
        self.held, self.slots, self.final, self.me = held, slots, final, me
        self.send_sem, self.recv_sem = send_sem, recv_sem
        self.sends = []

    def spans(self, u):
        i, s, lo, hi = BACK_UNITS[u]
        return self.held[i], BACK_ORDERS[s], i == DOWN, lo, middle(lo, hi, i == DOWN), hi

    def slot(self, u, stage, k, lo, hi):
        _, order, rows, base, _, _ = self.spans(u)
        return part_of(self.slots[stage][u], self.me, (), order[:stage + 1], lo - base, hi - base, rows, (k,))

    def send(self, src, dst, u, stage, k, to):
        cp = pltpu.make_async_remote_copy(src_ref=src, dst_ref=dst, send_sem=self.send_sem.at[u, stage, k],
            recv_sem=self.recv_sem.at[u, stage, k], device_id=device(to), device_id_type=MESH)
        cp.start()
        self.sends.append(cp)

    def got(self, ref, u, stage, k):
        pltpu.make_async_remote_copy(src_ref=ref, dst_ref=ref, send_sem=self.send_sem.at[u, stage, k],
            recv_sem=self.recv_sem.at[u, stage, k], device_id=device(moved(self.me, "c", 1)), device_id_type=MESH).wait_recv()

    def far(self, units, stage):
        for u in units:
            held, order, rows, lo, mid, hi = self.spans(u)
            at = moved(self.me, order[stage], 2)
            fixed = order[:stage + 1]
            self.send(part_of(held, at, fixed, (), lo, mid, rows), self.slot(u, stage, 0, lo, mid), u, stage, 0, moved(self.me, order[stage], 1))
            self.send(part_of(held, at, fixed, (), mid, hi, rows), self.slot(u, stage, 0, mid, hi), u, stage, 1, moved(self.me, order[stage], -1))

    def turn(self, units, stage):
        for u in units:
            held, order, rows, lo, mid, hi = self.spans(u)
            fixed = order[:stage + 1]
            for k, (by, a, b) in enumerate(((1, lo, mid), (-1, mid, hi))):
                to = moved(self.me, order[stage], by)
                came = self.slot(u, stage, 0, a, b)
                self.got(came, u, stage, k)
                accumulate(part_of(held, to, fixed, (), a, b, rows), [came], live_dims(fixed))
                self.send(part_of(held, to, fixed, (), lo, hi, rows), self.slot(u, stage, 1 + k, lo, hi), u, stage, 2 + k, to)

    def land(self, units, stage):
        for u in units:
            held, order, rows, lo, mid, hi = self.spans(u)
            fixed = order[:stage + 1]
            came = [self.slot(u, stage, 1 + k, lo, hi) for k in range(2)]
            for k in range(2):
                self.got(came[k], u, stage, 2 + k)
            mine = part_of(held, self.me, fixed, (), lo, hi, rows)
            if stage < 2:
                accumulate(mine, came, live_dims(fixed))
            else:
                span = pl.ds(lo, hi - lo)
                accumulate(mine, came, (), self.final[BACK_UNITS[u][0]].at[(span, slice(None)) if rows else (slice(None), span)])
        if stage < 2:
            self.far(units, stage + 1)

    def drain(self):
        for cp in self.sends:
            cp.wait_send()


def norm_back(upstream, normed, factor):
    return factor * (upstream - normed * jnp.mean(upstream * normed, axis=-1, keepdims=True))


def backward_kernel(*refs):
    (ids, tags_all, decays, h_x, h_cot, h_qkv, h_slopes, h_gate, h_mixed, h_resid, h_up, h_carried, w_in, w_output, w_up, w_down,
     t_first, t_gated, t_second, t_product, b_branch) = refs[:21]
    input_grad, grads = refs[21], refs[22:30]
    refs = refs[30:]
    n = len(BACK_UNITS)
    held, refs = refs[:4], refs[4:]
    slots = [refs[k * n:(k + 1) * n] for k in range(3)]
    refs = refs[3 * n:]
    final, theirs, refs = refs[:4], refs[4:7], refs[7:]
    (quarters, regroup, wbuf, product_t, lhs_a, lhs_b, branch, cot, d_up, up_sib, d_attn, attn_sib, pre_sib,
     up, qkv, slopes, gate, mixed, resid, x, d_resid, work, d_mixed, carried, local, came, going, reverse, ids_down, allowed,
     load_sem, wsem, send_sem, recv_sem, s1, r1, s2, r2, pass_send, pass_recv, end_send, end_recv, q_send, q_recv) = refs
    me = where_am_i()
    sib = moved(me, "c", 1)
    core, other_core = me["c"], sib["c"]
    seq, dp = lax.axis_index("seq"), lax.axis_index("dp")
    to = lambda k: (seq + k) % N_SEQ
    barrier = pltpu.get_barrier_semaphore()
    close = neighbours(me)
    for other in close:
        pl.semaphore_signal(barrier, inc=1, device_id=device(other), device_id_type=MESH)

    def greet(k, _):
        pl.semaphore_signal(barrier, inc=1, device_id=(dp, to(k)), device_id_type=MESH)
        return 0
    lax.fori_loop(1, N_SEQ, greet, 0)

    loads = {}
    def load(name, src, dst):
        cp = pltpu.make_async_copy(src, dst, load_sem.at[len(loads)])
        cp.start()
        loads[name] = cp
    load("product", t_product, product_t)
    load("branch", b_branch, branch)
    load("cot", h_cot, cot)

    phases = ((w_down, 11, 0, D), (w_up, 4, 0, FF), (w_up, 4, FF, FF), (w_output, 4, 0, D), (w_in, 4, 0, 2 * D), (w_in, 4, 2 * D, 2 * D))
    first = [sum(p[1] for p in phases[:k]) for k in range(len(phases))]
    def piece(phase, k):
        w, _, col, width = phases[phase]
        slot = (first[phase] + k) % 2
        row = pl.multiple_of(k * 256, 256)
        return pltpu.make_async_copy(w.at[pl.ds(row, 256), pl.ds(col, width)], wbuf.at[slot, :, pl.ds(0, width)], wsem.at[slot])
    def stream(phase, compute):
        count, width = phases[phase][1], phases[phase][3]
        def one(k, _):
            piece(phase, k).wait()
            @pl.when(k + 1 < count)
            def _():
                piece(phase, k + 1).start()
            if phase + 1 < len(phases):
                @pl.when(k + 1 == count)
                def _():
                    piece(phase + 1, 0).start()
            compute(k, wbuf.at[(first[phase] + k) % 2, :, pl.ds(0, width)])
            return 0
        lax.fori_loop(0, count, one, 0)
    piece(0, 0).start()
    load("up", h_up, up)
    load("second", t_second, lhs_a)
    load("resid", h_resid, resid)
    load("gated", t_gated, lhs_b)
    load("mixed", h_mixed, mixed)
    load("gate", h_gate, gate)
    load("qkv", h_qkv, qkv)
    load("slopes", h_slopes, slopes)
    load("carried", h_carried, carried)
    load("x", h_x, x)
    pl.semaphore_wait(barrier, len(close) + N_SEQ - 1)

    rs = Scatter(held, slots, final, me, send_sem, recv_sem)
    scan = Scan(local, came, going, reverse, (s1, r1, s2, r2))
    passed = []
    def hand(src, dst):
        k = len(passed)
        cp = pltpu.make_async_remote_copy(src_ref=src, dst_ref=dst, send_sem=pass_send.at[k], recv_sem=pass_recv.at[k],
            device_id=device(sib), device_id_type=MESH)
        cp.start()
        passed.append(cp)
        return cp

    loads["product"].wait()
    loads["branch"].wait()
    def down_rows(k, _):
        rows = pl.ds(pl.multiple_of(k * 352, 32), 352)
        for j in range(2):
            cols = slice(j * 256, (j + 1) * 256)
            total = dot(product_t[0, rows, :], branch[0, :, cols]) + dot(product_t[1, rows, :], branch[1, :, cols])
            for i in range(4):
                held[DOWN][k // 2, k % 2, i, j] = total[i * 88:(i + 1) * 88].astype(LOW)
        return 0
    lax.fori_loop(0, 8, down_rows, 0)
    rs.far(BACK_OF[DOWN], 0)

    loads["cot"].wait()
    loads["up"].wait()
    def up_back(k, w):
        cols, more = columns_of(k, 256), pl.ds(pl.multiple_of(k * 256 + FF, 256), 256)
        d_product = dot(cot[...], w[...], ((1,), (1,)))
        d_up[:, cols] = (d_product * up[:, more].astype(F32)).astype(LOW)
        d_up[:, more] = (d_product * up[:, cols].astype(F32)).astype(LOW)
    stream(0, up_back)
    side = lambda c, width: pl.ds(pl.multiple_of(c * width, width), width)
    hand(d_up.at[:, side(other_core, FF)], up_sib)
    rs.turn(BACK_OF[DOWN], 0)
    def second_left(k, w):
        work[:, columns_of(k, 256)] = dot(d_up[:, 0:FF], w[...], ((1,), (1,)))
    stream(1, second_left)
    def second_right(k, w):
        work[:, columns_of(k, 256)] += dot(d_up[:, FF:2 * FF], w[...], ((1,), (1,)))
    stream(2, second_right)
    rs.land(BACK_OF[DOWN], 0)

    loads["resid"].wait()
    def resid_back(rows):
        v = resid[rows, :]
        factor = rms_factor(v)
        total = cot[rows, :].astype(F32) + norm_back(work[rows, :], v * factor, factor)
        d_resid[rows, :] = total
        d_attn[rows, :] = total.astype(LOW)
    by_rows(ROWS, 16, resid_back)
    hand(d_attn.at[:, side(other_core, D // 2)], attn_sib)
    rs.turn(BACK_OF[DOWN], 1)
    def gated_back(k, w):
        work[:, columns_of(k, 256)] = dot(d_attn[...], w[...], ((1,), (1,)))
    stream(3, gated_back)
    loads["mixed"].wait()
    loads["gate"].wait()
    d_gate = resid
    def mixed_back(rows):
        v = mixed[rows, :]
        factor = rms_factor(v)
        normed = v * factor
        g = work[rows, :]
        d_gate[rows, :] = g * normed
        d_mixed[rows, :] = norm_back(g * gate[rows, :].astype(F32), normed, factor).astype(LOW)
    by_rows(ROWS, 16, mixed_back)
    loads["qkv"].wait()
    for m in range(2):
        below, across = spread(ids[m:m + 1, :])
        ids_down[m] = below
        allowed[m] = jnp.where((below == across) & (row_index() >= column_index()), 1.0, 0.0)
    def back_states(p, _):
        micro, head, rows, cols = pair_at(p)
        start = ids[pl.ds(micro, 1), 0:1]
        opening = jnp.where(ids_down[micro] == start, jnp.exp(-(row_index() + 1.0) * decays[head]), 0.0)
        opened = (qkv[rows, head_of(head, 0)].astype(F32) * opening).astype(LOW)
        local[p] = dot(opened, d_mixed[rows, cols], ((0,), (0,))).astype(LOW)
        return 0
    lax.fori_loop(0, 2 * H, back_states, 0)
    scan.start()
    rs.land(BACK_OF[DOWN], 1)
    rs.turn(BACK_OF[DOWN], 2)

    def grad_half(i, lhs, own, base, sibling, units):
        out = held[i].reshape(D, HELD[i][1])
        for u in units:
            _, _, lo, hi = BACK_UNITS[u]
            a = lo
            while a < hi:
                wide = min(256, hi - a)
                mine = own[:, pl.ds(pl.multiple_of(base + a, 128), wide)]
                total = dot(lhs[core], mine) + dot(lhs[other_core], sibling[:, a:a + wide])
                out[:, a:a + wide] = total.astype(LOW)
                a += wide
            rs.far((u,), 0)

    loads["second"].wait()
    passed[0].wait_recv()
    grad_half(WIDE, lhs_a, d_up, core * FF, up_sib, BACK_OF[WIDE])
    load("first", t_first, lhs_a)
    rs.land(BACK_OF[DOWN], 2)
    loads["gated"].wait()
    passed[1].wait_recv()
    grad_half(OUTPUT, lhs_b, d_attn, core * (D // 2), attn_sib, BACK_OF[OUTPUT])
    scan.join(tags_all, decays, True)
    rs.turn(BACK_OF[WIDE], 0)

    passed[0].wait_send()
    loads["slopes"].wait()
    loads["carried"].wait()
    d_pre = d_up.at[:, 0:4 * D]
    def pair_back(p, _):
        micro, head, rows, cols = pair_at(p)
        q, k, v = (qkv[rows, head_of(head, part)] for part in range(3))
        dm = d_mixed[rows, cols]
        mask = allowed[micro] * jnp.exp(jnp.minimum(column_index() - row_index(), 0.0) * decays[head])
        weighted = (dot(q, k, ((1,), (1,))) * mask).astype(LOW)
        d_scores = (dot(dm, v, ((1,), (1,))) * mask).astype(LOW)
        boundary = jnp.where(seq > 0, tags_all[jnp.maximum(seq - 1, 0), pl.ds(2 * micro + 1, 1), :], -1.0)
        reaching = jnp.where(ids_down[micro] == boundary, jnp.exp(-(row_index() + 1.0) * decays[head]), 0.0)
        d_q = dot(d_scores, k) + dot(dm, carried[p], ((1,), (1,))) * reaching
        d_pre[rows, head_of(head, 0)] = (d_q * slopes[rows, head_of(head, 0)].astype(F32)).astype(LOW)
        work[rows, cols] = dot(d_scores, q, ((0,), (0,)))
        mixed[rows, cols] = dot(weighted, dm, ((0,), (0,)))
        return 0
    lax.fori_loop(0, 2 * H, pair_back, 0)
    def gate_out(rows):
        d_pre[rows, 3 * D:4 * D] = d_gate[rows, :].astype(LOW)
    by_rows(ROWS, 16, gate_out)
    rs.land(BACK_OF[WIDE], 0)
    rs.turn(BACK_OF[OUTPUT], 0)
    scan.finish()
    def pair_close(p, _):
        micro, head, rows, cols = pair_at(p)
        after = jnp.where(seq < N_SEQ - 1, tags_all[jnp.minimum(seq + 1, N_SEQ - 1), pl.ds(2 * micro, 1), :], -1.0)
        closing = jnp.where(ids_down[micro] == after, jnp.exp((row_index() - (HD - 1.0)) * decays[head]), 0.0)
        d_k = work[rows, cols] + dot(qkv[rows, head_of(head, 2)], reverse[p], ((1,), (1,))) * closing
        d_v = mixed[rows, cols] + dot(qkv[rows, head_of(head, 1)], reverse[p]) * closing
        d_pre[rows, head_of(head, 1)] = (d_k * slopes[rows, head_of(head, 1)].astype(F32)).astype(LOW)
        d_pre[rows, head_of(head, 2)] = d_v.astype(LOW)
        return 0
    lax.fori_loop(0, 2 * H, pair_close, 0)
    hand(d_pre.at[:, side(other_core, 2 * D)], pre_sib)
    rs.turn(BACK_OF[WIDE], 1)
    rs.land(BACK_OF[OUTPUT], 0)
    loads["first"].wait()
    passed[2].wait_recv()
    grad_half(INPUT, lhs_a, d_pre, core * 2 * D, pre_sib, BACK_OF[INPUT])
    rs.land(BACK_OF[WIDE], 1)
    rs.turn(BACK_OF[OUTPUT], 1)
    def first_left(k, w):
        work[:, columns_of(k, 256)] = dot(d_pre[:, 0:2 * D], w[...], ((1,), (1,)))
    stream(4, first_left)
    rs.turn(BACK_OF[INPUT], 0)
    rs.turn(BACK_OF[WIDE], 2)
    rs.land(BACK_OF[OUTPUT], 1)
    def first_right(k, w):
        work[:, columns_of(k, 256)] += dot(d_pre[:, 2 * D:4 * D], w[...], ((1,), (1,)))
    stream(5, first_right)
    rs.land(BACK_OF[INPUT], 0)
    rs.land(BACK_OF[WIDE], 2)
    rs.turn(BACK_OF[OUTPUT], 2)
    loads["x"].wait()
    def input_back(rows):
        v = x[rows, :].astype(F32)
        factor = rms_factor(v)
        input_grad[rows, :] = d_resid[rows, :] + norm_back(work[rows, :], v * factor, factor)
    by_rows(ROWS, 16, input_back)
    rs.turn(BACK_OF[INPUT], 1)
    rs.land(BACK_OF[OUTPUT], 2)

    place = me["x"] // 2 * 2 + core
    def owner(j):
        return (dp, me["z"] * 4 + j)
    for j in range(4):
        quarters[j, 0:22, :] = final[DOWN][j * 22:(j + 1) * 22, :]
    def quarter(k):
        j = (place + k) % 4
        return pltpu.make_async_remote_copy(src_ref=quarters.at[j], dst_ref=regroup.at[place], send_sem=q_send.at[j],
            recv_sem=q_recv.at[place], device_id=owner(j), device_id_type=MESH)
    for k in range(1, 4):
        quarter(k).start()
    regroup[place] = quarters[place]
    ends = []
    def swap(i):
        k = len(ends)
        cp = pltpu.make_async_remote_copy(src_ref=final[i].at[side(other_core, 8), :], dst_ref=theirs[i - 1], send_sem=end_send.at[k],
            recv_sem=end_recv.at[k], device_id=device(sib), device_id_type=MESH)
        cp.start()
        ends.append(cp)
    def give(i, outs):
        ends[i - 1].wait_recv()
        mine, came = final[i][side(core, 8), :], theirs[i - 1][...]
        both = (jnp.where(core == 0, mine, came), jnp.where(core == 0, came, mine))
        width = HELD[i][1]
        n = len(outs) // 2
        for k, out in enumerate(outs):
            tiles_out = width // 128 if n == 0 else width // 128 // n
            for c in range(tiles_out):
                a = ((k % n) * tiles_out + c) * 128
                out[pl.ds(c, 8, stride=tiles_out), :] = both[k // n][:, a:a + 128]
    swap(WIDE)
    swap(OUTPUT)
    rs.land(BACK_OF[INPUT], 1)
    for k in range(1, 4):
        j = (place + k) % 4
        pltpu.make_async_remote_copy(src_ref=regroup.at[j], dst_ref=regroup.at[j], send_sem=q_send.at[j],
            recv_sem=q_recv.at[j], device_id=owner((place + 1) % 4), device_id_type=MESH).wait_recv()
    for j in range(4):
        for k in range(2):
            t = (j % 2) * 4 + (j // 2) * 2 + k
            grads[7][pl.ds(t, 22, stride=8), :] = regroup[j, 0:22, k * 128:(k + 1) * 128]
    give(WIDE, grads[5:7])
    ends[OUTPUT - 1].wait_recv()
    mine, came = final[OUTPUT][side(core, 8), :], theirs[OUTPUT - 1][...]
    both = (jnp.where(core == 0, mine, came), jnp.where(core == 0, came, mine))
    for c in range(8):
        grads[4][pl.ds(c, 8, stride=8), :] = both[c // 4][:, (c % 4) * 128:(c % 4 + 1) * 128]
    rs.turn(BACK_OF[INPUT], 2)
    rs.land(BACK_OF[INPUT], 2)
    swap(INPUT)
    give(INPUT, grads[0:4])
    for cp in ends:
        cp.wait_send()
    for k in range(1, 4):
        quarter(k).wait_send()
    passed[1].wait_send()
    passed[2].wait_send()
    scan.drain()
    rs.drain()


def backward(ids, tags_all, decays, arrays):
    v = pl.BlockSpec(memory_space=pltpu.VMEM)
    anywhere = pl.BlockSpec(memory_space=pl.ANY)
    sds = jax.ShapeDtypeStruct
    vm = pltpu.VMEM
    n = len(BACK_UNITS)
    scratch = [vm(live_dims(()) + tail, LOW) for tail in HELD]
    for stage in range(3):
        for i, s, lo, hi in BACK_UNITS:
            tail = (hi - lo, 256) if i == DOWN else (HELD[i][0], hi - lo)
            scratch.append(vm((3,) + live_dims(BACK_ORDERS[s][:stage + 1]) + tail, LOW))
    scratch += [vm(tail, F32) for tail in HELD] + [vm((8, tail[1]), F32) for tail in HELD[1:]]
    full = lambda width, kind=LOW: vm((ROWS, width), kind)
    scratch += [vm((4, 24, 256), F32), vm((4, 24, 256), F32), vm((2, 256, FF), LOW), vm((2, FF, ROWS), LOW),
        vm((2, D, ROWS), LOW), vm((2, D, ROWS), LOW), vm((2, ROWS, D // 2), LOW), full(D), full(2 * FF), full(FF), full(D), full(D // 2),
        full(2 * D), full(2 * FF), full(3 * D), full(2 * D), full(D), full(D, F32), full(D, F32), full(D), full(D, F32), full(D, F32), full(D)]
    scratch += [vm((N_SEQ, HD, HD), LOW)] * 5 + [vm((2, HD, HD), F32)] * 2
    scratch += [DMA((16,)), DMA((2,)), DMA((n, 3, 4)), DMA((n, 3, 4))] + [DMA((N_SEQ,))] * 4 + [DMA((3,))] * 4 + [DMA((4,))] * 2
    return pl.pallas_call(
        backward_kernel,
        out_shape=[sds((ROWS, D), F32)] + [sds((64, 128), F32)] * 5 + [sds((176, 128), F32)] * 3,
        in_specs=[v, v, pl.BlockSpec(memory_space=pltpu.SMEM)] + [anywhere] * len(arrays),
        out_specs=[v] * 9,
        scratch_shapes=scratch,
        compiler_params=pltpu.CompilerParams(collective_id=1, has_side_effects=True, vmem_limit_bytes=60 << 20),
        name="backward_and_scatter",
    )(ids, tags_all, decays, *arrays)


def on_device(hidden_in, seg_ids, decay_rates, grad_out, *weights):
    x, cot = hidden_in.reshape(ROWS, D), grad_out.reshape(ROWS, D)
    ids = seg_ids.reshape(2, HD).astype(F32)
    (act, tags_all, qkv, slopes, gate, mixed, resid, up, carried, w_in, w_output, w_up, w_down, t_first, t_gated, t_second,
     t_product, b_branch) = forward(x, cot, ids, decay_rates, [w.reshape(-1, 128) for w in weights])
    input_grad, *grads = backward(ids, tags_all, decay_rates, [
        x, cot, qkv, slopes, gate, mixed, resid, up, carried, w_in.reshape(D, 4 * D), w_output.reshape(D, D),
        w_up.reshape(D, 2 * FF), w_down, t_first, t_gated, t_second, t_product, b_branch])
    return (act.reshape(hidden_in.shape), input_grad.reshape(hidden_in.shape), *(g.reshape(-1) for g in grads))


def solution(mesh):
    tokens = P(None, "dp", "seq", None)
    flat = P(("dp", "seq"))
    return jax.shard_map(
        on_device, mesh=mesh,
        in_specs=(tokens, P(None, "dp", "seq"), P(), tokens) + (flat,) * 8,
        out_specs=(tokens, tokens) + (flat,) * 8,
        check_vma=False,
    )
```

```python
import functools
import jax, jax.numpy as jnp
from jax import lax
from jax.experimental import pallas as pl
from jax.experimental.pallas import tpu as pltpu
from jax.sharding import PartitionSpec as P

MESH = pl.DeviceIdType.MESH
RING = 4
D = 1024
H = 8
HD = 128
FF = 2816
ROWS = 256
N_SEQ = 16
EPSILON = 1e-06
LOW = jnp.bfloat16
F32 = jnp.float32
OWNERS = (4, 2, 4, 2, 2)
DMA = pltpu.SemaphoreType.DMA
ORDERS = (("x", "y", "z"), ("y", "z", "x"), ("z", "x", "y"))
SPLIT_ROWS = (False, False, False, True)


def tiles(array, bounds, grain=128):
    return [(array, s, lo * grain, hi * grain) for s, (lo, hi) in enumerate(zip(bounds[:-1], bounds[1:]))]


CHUNKS = (
    tuple(tiles(0, (0, 10, 20, 32))),
    tuple(tiles(1, (0, 4, 8)) + tiles(2, (0, 15, 30, 44))),
    tuple(tiles(3, (0, 7, 14, 22), 8)),
)
UNITS = CHUNKS[0] + CHUNKS[1] + CHUNKS[2]
C1, C2, C3 = (tuple(UNITS.index(u) for u in chunk) for chunk in CHUNKS)
C2_FIRST = C2[:2]


def where_am_i():
    dp = lax.axis_index("dp")
    seq = lax.axis_index("seq")
    return {"x": (seq // 2 % 2) * 2 + dp % 2, "y": dp // 2, "z": seq // 4, "c": seq % 2}


def device(at):
    return (at["y"] * 2 + at["x"] % 2, at["z"] * 4 + (at["x"] // 2) * 2 + at["c"])


def moved(at, axis, by):
    out = dict(at)
    out[axis] = (at[axis] + by) % RING if axis != "c" else 1 - at[axis]
    return out


def block(ref, at, whole, lo, hi, rows):
    every = slice(None)
    pick = lambda axis, value: every if axis in whole else value
    span = pl.ds(lo, hi - lo)
    return ref.at[
        pick("y", at["y"]), pick("x", at["x"] % 2), pick("z", at["z"]), pick("x", at["x"] // 2), at["c"],
        span if rows else every, every if rows else span,
    ]


def middle(lo, hi, rows):
    grain = 8 if rows else 128
    return lo + ((hi - lo) // grain // 2) * grain


def neighbours(me):
    return [moved(me, a, d) for a in "xyz" for d in (1, -1)] + [moved(me, "c", 1)]


def dot(a, b, dims=((1,), (0,))):
    return lax.dot_general(a, b, (dims, ((), ())), preferred_element_type=F32)


def by_rows(count, size, body):
    def one(k, _):
        body(pl.ds(pl.multiple_of(k * size, size), size))
        return 0
    lax.fori_loop(0, count // size, one, 0)


def columns_of(k, size):
    return pl.ds(pl.multiple_of(k * size, size), size)


def sigmoid(u):
    return 1.0 / (1.0 + jnp.exp(-u))


def rms_factor(v):
    return lax.rsqrt(jnp.mean(v * v, axis=-1, keepdims=True) + EPSILON)


class Gather:
    def __init__(self, arrays, me, send_sem, recv_sem, csend_sem, crecv_sem):
        self.arrays, self.me = arrays, me
        self.send_sem, self.recv_sem, self.csend_sem, self.crecv_sem = send_sem, recv_sem, csend_sem, crecv_sem
        self.sends = []

    def copy(self, ref, u, slot, to):
        return pltpu.make_async_remote_copy(src_ref=ref, dst_ref=ref, send_sem=self.send_sem.at[u, slot],
            recv_sem=self.recv_sem.at[u, slot], device_id=device(to), device_id_type=MESH)

    def ccopy(self, ref, u, slot):
        return pltpu.make_async_remote_copy(src_ref=ref, dst_ref=ref, send_sem=self.csend_sem.at[u, slot],
            recv_sem=self.crecv_sem.at[u, slot], device_id=device(moved(self.me, "c", 1)), device_id_type=MESH)

    def go(self, cp):
        cp.start()
        self.sends.append(cp)

    def part(self, u, at, stage, half=None):
        i, s, lo, hi = UNITS[u]
        rows = SPLIT_ROWS[i]
        mid = middle(lo, hi, rows)
        lo, hi = (lo, hi) if half is None else ((lo, mid), (mid, hi))[half]
        return block(self.arrays[i], at, ORDERS[s][:stage], lo, hi, rows)

    def axis(self, u, stage):
        return ORDERS[UNITS[u][1]][stage]

    def begin(self, units, stage):
        for u in units:
            a = self.axis(u, stage)
            for k, (half, by) in enumerate(((0, 1), (1, -1), (1, 1), (0, -1))):
                self.go(self.copy(self.part(u, self.me, stage, half), u, 6 * stage + k, moved(self.me, a, by)))
            if stage == 2:
                self.go(self.ccopy(self.part(u, self.me, stage), u, 0))

    def relay(self, units, stage):
        for u in units:
            a = self.axis(u, stage)
            for half, by in ((0, 1), (1, -1)):
                first = self.part(u, moved(self.me, a, -by), stage, half)
                self.copy(first, u, 6 * stage + half, moved(self.me, a, by)).wait_recv()
                self.go(self.copy(first, u, 6 * stage + 4 + half, moved(self.me, a, by)))

    def finish(self, units, stage):
        for u in units:
            a = self.axis(u, stage)
            for k, by, half in ((2, -1, 1), (3, 1, 0), (4, 2, 0), (5, 2, 1)):
                self.copy(self.part(u, moved(self.me, a, by), stage, half), u, 6 * stage + k, moved(self.me, a, 1)).wait_recv()
            if stage == 2:
                for k, by in enumerate((-1, 1, 2)):
                    self.go(self.ccopy(self.part(u, moved(self.me, a, by), stage), u, 1 + k))

    def advance(self, units, stage):
        for u in units:
            self.finish((u,), stage)
            self.begin((u,), stage + 1)

    def arrive(self, units):
        sib = moved(self.me, "c", 1)
        for u in units:
            for k, by in enumerate((0, -1, 1, 2)):
                self.ccopy(self.part(u, moved(sib, self.axis(u, 2), by), 2), u, k).wait_recv()

    def drain(self):
        for cp in self.sends:
            cp.wait_send()


class Scan:
    def __init__(self, local, came, going, carried, sems):
        self.me, self.dp = lax.axis_index("seq"), lax.axis_index("dp")
        self.local, self.came, self.going, self.carried = local, came, going, carried
        self.send1, self.recv1, self.send2, self.recv2 = sems

    def to(self, k):
        return (self.me + k) % N_SEQ

    def out(self, to):
        return pltpu.make_async_remote_copy(src_ref=self.local.at[to], dst_ref=self.came.at[self.me], send_sem=self.send1.at[to],
            recv_sem=self.recv1.at[self.me], device_id=(self.dp, to), device_id_type=MESH)

    def back(self, to):
        return pltpu.make_async_remote_copy(src_ref=self.going.at[to], dst_ref=self.carried.at[self.me], send_sem=self.send2.at[to],
            recv_sem=self.recv2.at[self.me], device_id=(self.dp, to), device_id_type=MESH)

    def arrival(self, ref, ssem, rsem, frm):
        return pltpu.make_async_remote_copy(src_ref=ref.at[frm], dst_ref=ref.at[frm], send_sem=ssem.at[frm],
            recv_sem=rsem.at[frm], device_id=(self.dp, self.to(1)), device_id_type=MESH)

    def each(self, body):
        def one(k, _):
            body(self.to(k))
            return 0
        lax.fori_loop(1, N_SEQ, one, 0)

    def start(self):
        self.each(lambda to: self.out(to).start())
        self.came[self.me] = self.local[self.me]

    def join(self, tags_all, decays, backward):
        self.each(lambda frm: self.arrival(self.came, self.send1, self.recv1, frm).wait_recv())
        micro, head = self.me // H, self.me % H
        fade = jnp.exp(-float(HD) * jnp.full((1, HD), decays[head], F32))
        first = lambda b: tags_all[b, pl.ds(2 * micro, 1), :]
        last = lambda b: tags_all[b, pl.ds(2 * micro + 1, 1), :]
        acc = jnp.zeros((HD, HD), F32)
        previous = None
        for b in (range(N_SEQ - 1, -1, -1) if backward else range(N_SEQ)):
            self.going[b] = acc.astype(LOW)
            if previous is None:
                acc = self.came[b].astype(F32)
            else:
                near = (last(b) == first(previous)) if backward else (first(b) == last(previous))
                acc = self.came[b].astype(F32) + jnp.where((first(b) == last(b)) & near, fade, 0.0) * acc
            previous = b
        self.carried[self.me] = self.going[self.me]
        self.each(lambda to: self.back(to).start())

    def finish(self):
        self.each(lambda frm: self.arrival(self.carried, self.send2, self.recv2, frm).wait_recv())

    def drain(self):
        def one(to):
            self.out(to).wait_send()
            self.back(to).wait_send()
        self.each(one)


def spread(row):
    across = jnp.broadcast_to(row, (HD, HD))
    return across.T, across


def row_index():
    return lax.broadcasted_iota(jnp.int32, (HD, HD), 0).astype(F32)


def column_index():
    return lax.broadcasted_iota(jnp.int32, (HD, HD), 1).astype(F32)


def pair_at(p):
    micro, head = p // H, p % H
    return micro, head, pl.ds(pl.multiple_of(micro * HD, HD), HD), pl.ds(pl.multiple_of(head * HD, HD), HD)


def transpose_into(src, dst, count):
    def one(k, _):
        at = columns_of(k, 128)
        dst[at, :] = src[:, at].T
        return 0
    lax.fori_loop(0, count // 128, one, 0)


def forward_kernel(*refs):
    (x, cot, ids, decays), small = refs[:4], refs[4:12]
    (act, tags_all, o_qkv, o_slopes, o_gate, o_mixed, o_resid, o_up, o_carried, o_in, o_output, o_wide, o_down,
     t_first, t_gated, t_second, t_product, b_branch) = refs[12:30]
    (w_in, w_output, w_up, w_flat, w_down, pre, first_in, qkv, slopes, gate, mixed, resid, up, gated, second, product,
     first_t, gated_t, second_t, product_t, carried, local, came, going, spare, tag, allowed, kept_mask, ids_down,
     send_sem, recv_sem, csend_sem, crecv_sem, tag_send, tag_recv, s1, r1, s2, r2, out_sem, pass_send, pass_recv) = refs[30:]
    me = where_am_i()
    sib = moved(me, "c", 1)
    seq, dp = lax.axis_index("seq"), lax.axis_index("dp")
    to = lambda k: (seq + k) % N_SEQ
    barrier = pltpu.get_barrier_semaphore()
    close = neighbours(me)
    for other in close:
        pl.semaphore_signal(barrier, inc=1, device_id=device(other), device_id_type=MESH)

    def greet(k, _):
        pl.semaphore_signal(barrier, inc=1, device_id=(dp, to(k)), device_id_type=MESH)
        return 0
    lax.fori_loop(1, N_SEQ, greet, 0)

    here = (me["y"], me["x"] % 2, me["z"], me["x"] // 2, me["c"])
    def place(src, target, base, width):
        n = width // 128
        spare[pl.ds(0, 8 * n), :] = src[...].astype(F32)
        for c in range(n):
            target[(*here, slice(None), pl.ds(base + c * 128, 128))] = spare[pl.ds(c, 8, stride=n), :].astype(LOW)
    for k in range(4):
        place(small[k], w_in, k * D, D)
    place(small[4], w_output, 0, D)
    place(small[5], w_up, 0, FF)
    place(small[6], w_up, FF, FF)
    w_flat[here] = small[7][...]
    tag[...] = jnp.zeros((8, HD), F32)
    for m in range(2):
        tag[2 * m:2 * m + 1, :] = jnp.broadcast_to(ids[m:m + 1, 0:1], (1, HD))
        tag[2 * m + 1:2 * m + 2, :] = jnp.broadcast_to(ids[m:m + 1, HD - 1:HD], (1, HD))
    tags_all[seq] = tag[...]
    pl.semaphore_wait(barrier, len(close) + N_SEQ - 1)

    g = Gather((w_in, w_output, w_up, w_flat), me, send_sem, recv_sem, csend_sem, crecv_sem)
    scan = Scan(local, came, going, carried, (s1, r1, s2, r2))
    g.begin(C1, 0)
    g.begin(C2, 0)
    g.begin(C3, 0)

    kept, passed = [], []
    def keep(src, dst):
        cp = pltpu.make_async_copy(src, dst, out_sem.at[len(kept)])
        cp.start()
        kept.append(cp)
    def hand(mine, theirs, dst):
        keep(mine, dst.at[me["c"]])
        k = len(passed)
        cp = pltpu.make_async_remote_copy(src_ref=theirs, dst_ref=dst.at[me["c"]], send_sem=pass_send.at[k],
            recv_sem=pass_recv.at[k], device_id=device(sib), device_id_type=MESH)
        cp.start()
        passed.append((cp, dst))

    def tag_copy(other):
        return pltpu.make_async_remote_copy(src_ref=tag, dst_ref=tags_all.at[seq], send_sem=tag_send.at[other],
            recv_sem=tag_recv.at[seq], device_id=(dp, other), device_id_type=MESH)
    scan.each(lambda other: tag_copy(other).start())

    def norm_in(rows):
        v = x[rows, :].astype(F32)
        first_in[rows, :] = (v * rms_factor(v)).astype(LOW)
    by_rows(ROWS, 32, norm_in)
    g.relay(C1, 0)
    g.relay(C2, 0)
    g.relay(C3, 0)
    g.advance(C1, 0)
    for m in range(2):
        down, across = spread(ids[m:m + 1, :])
        ids_down[m] = down
        allowed[m] = jnp.where((down == across) & (row_index() >= column_index()), 1.0, 0.0)
        kept_mask[m] = jnp.where(down == jnp.broadcast_to(ids[m:m + 1, HD - 1:HD], (HD, HD)), 1.0, 0.0)
    g.relay(C1, 1)
    g.advance(C2, 0)
    g.advance(C1, 1)
    g.advance(C3, 0)
    half = lambda c: cot.at[:, pl.ds(pl.multiple_of(c * 512, 512), 512)]
    hand(half(me["c"]), half(sib["c"]), b_branch)
    transpose_into(first_in, first_t, D)
    hand(first_t, first_t, t_first)
    g.relay(C2, 1)
    g.relay(C1, 2)
    g.relay(C3, 1)
    g.advance(C2, 1)
    g.finish(C1, 2)
    g.arrive(C1)
    keep(w_in, o_in)

    m_in = w_in.reshape(D, 4 * D)
    def project(k, _):
        cols = columns_of(k, 512)
        pre[:, cols] = dot(first_in[...], m_in[:, cols])
        return 0
    lax.fori_loop(0, 8, project, 0)
    g.relay(C2, 2)
    g.advance(C3, 1)

    def rows_of_heads(rows):
        for k in range(2):
            u = pre[rows, k * D:(k + 1) * D]
            s = sigmoid(u)
            qkv[rows, k * D:(k + 1) * D] = (u * s).astype(LOW)
            slopes[rows, k * D:(k + 1) * D] = (s * (1.0 + u * (1.0 - s))).astype(LOW)
        qkv[rows, 2 * D:3 * D] = pre[rows, 2 * D:3 * D].astype(LOW)
        gate[rows, :] = pre[rows, 3 * D:4 * D].astype(LOW)
    by_rows(ROWS, 16, rows_of_heads)
    keep(qkv, o_qkv)
    keep(slopes, o_slopes)
    keep(gate, o_gate)

    def states(p, _):
        micro, head, rows, _ = pair_at(p)
        keeping = jnp.exp((row_index() - (HD - 1.0)) * decays[head]) * kept_mask[micro]
        held = (qkv[rows, head_of(head, 1)].astype(F32) * keeping).astype(LOW)
        local[p] = dot(held, qkv[rows, head_of(head, 2)], ((0,), (0,))).astype(LOW)
        return 0
    lax.fori_loop(0, 2 * H, states, 0)
    scan.start()

    def within(p, _):
        micro, head, rows, cols = pair_at(p)
        mask = allowed[micro] * jnp.exp(jnp.minimum(column_index() - row_index(), 0.0) * decays[head])
        weighted = (dot(qkv[rows, head_of(head, 0)], qkv[rows, head_of(head, 1)], ((1,), (1,))) * mask).astype(LOW)
        mixed[rows, cols] = dot(weighted, qkv[rows, head_of(head, 2)])
        return 0
    lax.fori_loop(0, 2 * H, within, 0)
    scan.each(lambda frm: pltpu.make_async_remote_copy(src_ref=tag, dst_ref=tags_all.at[frm], send_sem=tag_send.at[frm],
        recv_sem=tag_recv.at[frm], device_id=(dp, to(1)), device_id_type=MESH).wait_recv())
    scan.join(tags_all, decays, False)
    g.finish(C2, 2)
    g.relay(C3, 2)
    g.arrive(C2_FIRST)
    keep(w_output, o_output)
    scan.finish()
    keep(carried, o_carried)

    def crossing(p, _):
        micro, head, rows, cols = pair_at(p)
        boundary = jnp.where(seq > 0, tags_all[jnp.maximum(seq - 1, 0), pl.ds(2 * micro + 1, 1), :], -1.0)
        reaching = jnp.where(ids_down[micro] == boundary, jnp.exp(-(row_index() + 1.0) * decays[head]), 0.0)
        mixed[rows, cols] += dot(qkv[rows, head_of(head, 0)], carried[p]) * reaching
        return 0
    lax.fori_loop(0, 2 * H, crossing, 0)
    keep(mixed, o_mixed)

    def gate_rows(rows):
        v = mixed[rows, :]
        gated[rows, :] = (v * rms_factor(v) * pre[rows, 3 * D:4 * D]).astype(LOW)
    by_rows(ROWS, 16, gate_rows)
    m_output = w_output.reshape(D, D)
    def output(k, _):
        cols = columns_of(k, 512)
        resid[:, cols] = x[:, cols].astype(F32) + dot(gated[...], m_output[:, cols])
        for c in range(4):
            at = columns_of(k * 4 + c, 128)
            gated_t[at, :] = gated[:, at].T
        return 0
    lax.fori_loop(0, 2, output, 0)
    keep(resid, o_resid)
    def norm_second(rows):
        v = resid[rows, :]
        second[rows, :] = (v * rms_factor(v)).astype(LOW)
    by_rows(ROWS, 32, norm_second)
    hand(gated_t, gated_t, t_gated)
    g.finish(C3, 2)
    g.arrive(C2[2:])
    keep(w_up, o_wide)
    m_up = w_up.reshape(D, 2 * FF)
    def widen(k, _):
        cols, more = columns_of(k, 256), pl.ds(pl.multiple_of(k * 256 + FF, 256), 256)
        left = dot(second[...], m_up[:, cols])
        right = dot(second[...], m_up[:, more])
        up[:, cols] = left.astype(LOW)
        up[:, more] = right.astype(LOW)
        both = (left * right).astype(LOW)
        product[:, cols] = both
        product_t[cols, :] = both.T
        return 0
    lax.fori_loop(0, 11, widen, 0)
    keep(up, o_up)
    hand(product_t, product_t, t_product)
    g.arrive(C3)
    flat = w_flat.reshape(128 * 176, 128)
    def arrange(k, _):
        spare[...] = flat[pl.ds(pl.multiple_of(k * 1408, 1408), 1408), :].astype(F32)
        for c in range(8):
            w_down[pl.ds(pl.multiple_of(k * 176, 176), 176), c * 128:(c + 1) * 128] = spare[pl.ds(c, 176, stride=8), :].astype(LOW)
        return 0
    lax.fori_loop(0, 16, arrange, 0)
    keep(w_down, o_down)
    def last(k, _):
        cols = columns_of(k, 512)
        act[:, cols] = (resid[:, cols] + dot(product[...], w_down[:, cols])).astype(LOW)
        for c in range(4):
            at = columns_of(k * 4 + c, 128)
            second_t[at, :] = second[:, at].T
        return 0
    lax.fori_loop(0, 2, last, 0)
    hand(second_t, second_t, t_second)
    for cp in kept:
        cp.wait()
    for k, (cp, dst) in enumerate(passed):
        cp.wait_send()
        there = dst.at[sib["c"]]
        pltpu.make_async_remote_copy(src_ref=there, dst_ref=there, send_sem=pass_send.at[k], recv_sem=pass_recv.at[k],
            device_id=device(sib), device_id_type=MESH).wait_recv()
    scan.each(lambda other: tag_copy(other).wait_send())
    scan.drain()
    g.drain()


def forward(x, cot, ids, decays, pieces):
    v = pl.BlockSpec(memory_space=pltpu.VMEM)
    anywhere = pl.BlockSpec(memory_space=pl.ANY)
    sds = jax.ShapeDtypeStruct
    n = len(UNITS)
    outs = [sds((ROWS, D), LOW), sds((N_SEQ, 8, HD), F32), sds((ROWS, 3 * D), LOW), sds((ROWS, 2 * D), LOW), sds((ROWS, D), LOW),
        sds((ROWS, D), F32), sds((ROWS, D), F32), sds((ROWS, 2 * FF), LOW), sds((N_SEQ, HD, HD), LOW),
        sds(OWNERS + (8, 4 * D), LOW), sds(OWNERS + (8, D), LOW), sds(OWNERS + (8, 2 * FF), LOW), sds((FF, D), LOW),
        sds((2, D, ROWS), LOW), sds((2, D, ROWS), LOW), sds((2, D, ROWS), LOW), sds((2, FF, ROWS), LOW), sds((2, ROWS, D // 2), LOW)]
    vm = pltpu.VMEM
    scratch = [vm(OWNERS + (8, 4 * D), LOW), vm(OWNERS + (8, D), LOW), vm(OWNERS + (8, 2 * FF), LOW), vm(OWNERS + (176, 128), LOW),
        vm((FF, D), LOW), vm((ROWS, 4 * D), F32), vm((ROWS, D), LOW), vm((ROWS, 3 * D), LOW), vm((ROWS, 2 * D), LOW), vm((ROWS, D), LOW),
        vm((ROWS, D), F32), vm((ROWS, D), F32), vm((ROWS, 2 * FF), LOW), vm((ROWS, D), LOW), vm((ROWS, D), LOW), vm((ROWS, FF), LOW),
        vm((D, ROWS), LOW), vm((D, ROWS), LOW), vm((D, ROWS), LOW), vm((FF, ROWS), LOW)] + [vm((N_SEQ, HD, HD), LOW)] * 4 + [
        vm((1408, 128), F32), vm((8, HD), F32)] + [vm((2, HD, HD), F32)] * 3 + [
        DMA((n, 18)), DMA((n, 18)), DMA((n, 4)), DMA((n, 4))] + [DMA((N_SEQ,))] * 6 + [DMA((20,)), DMA((5,)), DMA((5,))]
    return pl.pallas_call(
        forward_kernel, out_shape=outs,
        in_specs=[v, v, v, pl.BlockSpec(memory_space=pltpu.SMEM)] + [v] * 8,
        out_specs=[v] * 2 + [anywhere] * 16,
        scratch_shapes=scratch,
        compiler_params=pltpu.CompilerParams(collective_id=0, has_side_effects=True, vmem_limit_bytes=60 << 20),
        name="gather_and_forward",
    )(x, cot, ids, decays, *pieces)


def head_of(head, part):
    return pl.ds(pl.multiple_of(part * D + head * HD, HD), HD)


DOWN, WIDE, OUTPUT, INPUT = range(4)
HELD = ((88, 256), (16, FF), (16, D // 2), (16, 2 * D))
GROUPS = (
    tiles(DOWN, (0, 3, 7, 11), 8),
    tiles(WIDE, (0, 7, 14, 22)),
    [(OUTPUT, 0, 0, 256), (OUTPUT, 1, 256, 512)],
    [(INPUT, 1, 1536, 1792), (INPUT, 2, 1792, 2048)],
    [(INPUT, 2, 0, 256), (INPUT, 0, 256, 512)],
    [(INPUT, 0, 512, 896), (INPUT, 1, 896, 1280), (INPUT, 2, 1280, 1536)],
)
BACK_UNITS = tuple(unit for group in GROUPS for unit in group)
G_DOWN, G_WIDE, G_OUTPUT, G_GATE, G_QUERY, G_VALUE = (tuple(BACK_UNITS.index(unit) for unit in group) for group in GROUPS)
BACK_ORDERS = tuple(order[::-1] for order in ORDERS)
DIMS = (("y", 4), ("x", 2), ("z", 4), ("x", 2))


def live_dims(fixed):
    return tuple(n for a, n in DIMS if a not in fixed)


def part_of(ref, at, fixed, gone, lo, hi, rows, lead=()):
    every = slice(None)
    idx = []
    for k, (a, n) in enumerate(DIMS):
        if a in gone:
            continue
        if a in fixed:
            idx.append((at["x"] % 2 if k == 1 else at["x"] // 2) if a == "x" else at[a])
        else:
            idx.append(every)
    span = pl.ds(lo, hi - lo)
    return ref.at[(*lead, *idx, span if rows else every, every if rows else span)]


def accumulate(dst, srcs, dims, out=None):
    target = dst if out is None else out
    def one(k, _):
        idx, rest = [], k
        for d in dims[::-1]:
            idx.append(rest % d)
            rest = rest // d
        at = tuple(idx[::-1]) if dims else ...
        total = dst[at].astype(F32)
        for s in srcs:
            total = total + s[at].astype(F32)
        target[at] = total.astype(target.dtype)
        return 0
    n = 1
    for d in dims:
        n *= d
    if n == 1:
        one(0, 0)
    else:
        lax.fori_loop(0, n, one, 0)


class Scatter:
    def __init__(self, held, slots, final, me, send_sem, recv_sem):
        self.held, self.slots, self.final, self.me = held, slots, final, me
        self.send_sem, self.recv_sem = send_sem, recv_sem
        self.sends = []

    def spans(self, u):
        i, s, lo, hi = BACK_UNITS[u]
        return self.held[i], BACK_ORDERS[s], i == DOWN, lo, middle(lo, hi, i == DOWN), hi

    def slot(self, u, stage, k, lo, hi):
        _, order, rows, base, _, _ = self.spans(u)
        return part_of(self.slots[stage][u], self.me, (), order[:stage + 1], lo - base, hi - base, rows, (k,))

    def send(self, src, dst, u, stage, k, to):
        cp = pltpu.make_async_remote_copy(src_ref=src, dst_ref=dst, send_sem=self.send_sem.at[u, stage, k],
            recv_sem=self.recv_sem.at[u, stage, k], device_id=device(to), device_id_type=MESH)
        cp.start()
        self.sends.append(cp)

    def got(self, ref, u, stage, k):
        pltpu.make_async_remote_copy(src_ref=ref, dst_ref=ref, send_sem=self.send_sem.at[u, stage, k],
            recv_sem=self.recv_sem.at[u, stage, k], device_id=device(moved(self.me, "c", 1)), device_id_type=MESH).wait_recv()

    def far(self, units, stage):
        for u in units:
            held, order, rows, lo, mid, hi = self.spans(u)
            axis, fixed = order[stage], order[:stage + 1]
            above, below, across = (moved(self.me, axis, by) for by in (1, -1, 2))
            mine = lambda at, a, b: part_of(held, at, fixed, (), a, b, rows)
            if stage == 2:
                for k, at in enumerate((across, above, below)):
                    self.send(mine(at, lo, hi), self.slot(u, stage, k, lo, hi), u, stage, k, at)
                continue
            self.send(mine(across, lo, mid), self.slot(u, stage, 0, lo, mid), u, stage, 0, above)
            self.send(mine(across, mid, hi), self.slot(u, stage, 0, mid, hi), u, stage, 1, below)
            self.send(mine(above, mid, hi), self.slot(u, stage, 1, mid, hi), u, stage, 2, above)
            self.send(mine(below, lo, mid), self.slot(u, stage, 2, lo, mid), u, stage, 3, below)

    def turn(self, units, stage):
        for u in units:
            held, order, rows, lo, mid, hi = self.spans(u)
            fixed = order[:stage + 1]
            for k, (by, a, b) in enumerate(((1, lo, mid), (-1, mid, hi))):
                to = moved(self.me, order[stage], by)
                came = self.slot(u, stage, 0, a, b)
                self.got(came, u, stage, k)
                sums = part_of(held, to, fixed, (), a, b, rows)
                accumulate(sums, [came], live_dims(fixed))
                self.send(sums, self.slot(u, stage, 1 + k, a, b), u, stage, 4 + k, to)

    def land(self, units, stage):
        for u in units:
            held, order, rows, lo, mid, hi = self.spans(u)
            fixed = order[:stage + 1]
            mine = part_of(held, self.me, fixed, (), lo, hi, rows)
            if stage == 2:
                came = [self.slot(u, stage, k, lo, hi) for k in range(3)]
                for k in range(3):
                    self.got(came[k], u, stage, k)
                span = pl.ds(lo, hi - lo)
                accumulate(mine, came, (), self.final[BACK_UNITS[u][0]].at[(span, slice(None)) if rows else (slice(None), span)])
                continue
            for k, (a, b) in ((2, (mid, hi)), (3, (lo, mid)), (4, (lo, mid)), (5, (mid, hi))):
                self.got(self.slot(u, stage, 1 + k % 2, a, b), u, stage, k)
            accumulate(mine, [self.slot(u, stage, 1 + k, lo, hi) for k in range(2)], live_dims(fixed))
            self.far((u,), stage + 1)

    def drain(self):
        for cp in self.sends:
            cp.wait_send()


def norm_back(upstream, normed, factor):
    return factor * (upstream - normed * jnp.mean(upstream * normed, axis=-1, keepdims=True))


def backward_kernel(*refs):
    (ids, tags_all, decays, h_x, h_cot, h_qkv, h_slopes, h_gate, h_mixed, h_resid, h_up, h_carried, w_in, w_output, w_up, w_down,
     t_first, t_gated, t_second, t_product, b_branch) = refs[:21]
    input_grad, grads = refs[21], refs[22:30]
    refs = refs[30:]
    n = len(BACK_UNITS)
    held, refs = refs[:4], refs[4:]
    slots = [refs[k * n:(k + 1) * n] for k in range(3)]
    refs = refs[3 * n:]
    final, theirs, refs = refs[:4], refs[4:7], refs[7:]
    (quarters, regroup, wbuf, product_t, lhs_a, lhs_b, branch, cot, d_up, up_sib, d_attn, attn_sib, pre_sib,
     up, qkv, slopes, gate, mixed, resid, x, work, d_mixed, carried, local, came, going, reverse, ids_down, allowed,
     load_sem, wsem, send_sem, recv_sem, s1, r1, s2, r2, pass_send, pass_recv, end_send, end_recv, q_send, q_recv) = refs
    me = where_am_i()
    sib = moved(me, "c", 1)
    core, other_core = me["c"], sib["c"]
    seq, dp = lax.axis_index("seq"), lax.axis_index("dp")
    to = lambda k: (seq + k) % N_SEQ
    barrier = pltpu.get_barrier_semaphore()
    close = neighbours(me) + [moved(me, a, 2) for a in "xyz"]
    for other in close:
        pl.semaphore_signal(barrier, inc=1, device_id=device(other), device_id_type=MESH)

    def greet(k, _):
        pl.semaphore_signal(barrier, inc=1, device_id=(dp, to(k)), device_id_type=MESH)
        return 0
    lax.fori_loop(1, N_SEQ, greet, 0)

    loads = {}
    def load(name, src, dst):
        cp = pltpu.make_async_copy(src, dst, load_sem.at[len(loads)])
        cp.start()
        loads[name] = cp
    load("product", t_product, product_t)
    load("branch", b_branch, branch)
    load("cot", h_cot, cot)

    phases = ((w_down, 11, 0, D), (w_up, 4, 0, FF), (w_up, 4, FF, FF), (w_output, 4, 0, D),
        (w_in, 4, 3 * D, D), (w_in, 4, 0, 2 * D), (w_in, 4, 2 * D, D))
    first = [sum(p[1] for p in phases[:k]) for k in range(len(phases))]
    def piece(phase, k):
        w, _, col, width = phases[phase]
        slot = (first[phase] + k) % 3
        row = pl.multiple_of(k * 256, 256)
        return pltpu.make_async_copy(w.at[pl.ds(row, 256), pl.ds(col, width)], wbuf.at[slot, :, pl.ds(0, width)], wsem.at[slot])
    def stream(phase, compute):
        count, width = phases[phase][1], phases[phase][3]
        def one(k, _):
            @pl.when(k + 2 < count)
            def _():
                piece(phase, k + 2).start()
            if phase + 1 < len(phases):
                @pl.when(k + 2 >= count)
                def _():
                    piece(phase + 1, k + 2 - count).start()
            piece(phase, k).wait()
            compute(k, wbuf.at[(first[phase] + k) % 3, :, pl.ds(0, width)])
            return 0
        lax.fori_loop(0, count, one, 0)
    piece(0, 0).start()
    piece(0, 1).start()
    load("up", h_up, up)
    load("resid", h_resid, resid)
    load("mixed", h_mixed, mixed)
    load("gate", h_gate, gate)
    load("qkv", h_qkv, qkv)
    load("second", t_second, lhs_a)
    load("gated", t_gated, lhs_b)
    load("carried", h_carried, carried)
    load("slopes", h_slopes, slopes)
    load("x", h_x, x)
    for m in range(2):
        below, across = spread(ids[m:m + 1, :])
        ids_down[m] = below
        allowed[m] = jnp.where((below == across) & (row_index() >= column_index()), 1.0, 0.0)
    pl.semaphore_wait(barrier, len(close) + N_SEQ - 1)

    rs = Scatter(held, slots, final, me, send_sem, recv_sem)
    scan = Scan(local, came, going, reverse, (s1, r1, s2, r2))
    passed = []
    def hand(src, dst):
        k = len(passed)
        cp = pltpu.make_async_remote_copy(src_ref=src, dst_ref=dst, send_sem=pass_send.at[k], recv_sem=pass_recv.at[k],
            device_id=device(sib), device_id_type=MESH)
        cp.start()
        passed.append(cp)
        return cp

    loads["product"].wait()
    loads["branch"].wait()
    def down_rows(k, _):
        rows = pl.ds(pl.multiple_of(k * 352, 32), 352)
        for j in range(2):
            cols = slice(j * 256, (j + 1) * 256)
            total = dot(product_t[0, rows, :], branch[0, :, cols]) + dot(product_t[1, rows, :], branch[1, :, cols])
            for i in range(4):
                held[DOWN][k // 2, k % 2, i, j] = total[i * 88:(i + 1) * 88].astype(LOW)
        return 0
    lax.fori_loop(0, 8, down_rows, 0)
    rs.far(G_DOWN, 0)

    loads["cot"].wait()
    loads["up"].wait()
    def up_back(k, w):
        cols, more = columns_of(k, 256), pl.ds(pl.multiple_of(k * 256 + FF, 256), 256)
        d_product = dot(cot[...], w[...], ((1,), (1,)))
        d_up[:, cols] = (d_product * up[:, more].astype(F32)).astype(LOW)
        d_up[:, more] = (d_product * up[:, cols].astype(F32)).astype(LOW)
    stream(0, up_back)
    side = lambda c, width, base=0: pl.ds(pl.multiple_of(c * width + base, 128), width)
    h_wide = hand(d_up.at[:, side(other_core, FF)], up_sib)
    def second_left(k, w):
        work[:, columns_of(k, 256)] = dot(d_up[:, 0:FF], w[...], ((1,), (1,)))
    stream(1, second_left)
    rs.turn(G_DOWN, 0)

    def grad_half(i, lhs, own, base, shift, sibling, units):
        out = held[i].reshape(D, HELD[i][1])
        for u in units:
            _, _, lo, hi = BACK_UNITS[u]
            a = lo
            while a < hi:
                wide = min(256, hi - a)
                mine = own[:, pl.ds(pl.multiple_of(base + (a - shift), 128), wide)]
                total = dot(lhs[core], mine) + dot(lhs[other_core], sibling[:, a:a + wide])
                out[:, a:a + wide] = total.astype(LOW)
                a += wide
            rs.far((u,), 0)

    loads["second"].wait()
    h_wide.wait_recv()
    grad_half(WIDE, lhs_a, d_up, core * FF, 0, up_sib, G_WIDE)
    load("first", t_first, lhs_a)
    rs.land(G_DOWN, 0)
    def second_right(k, w):
        work[:, columns_of(k, 256)] += dot(d_up[:, FF:2 * FF], w[...], ((1,), (1,)))
    stream(2, second_right)

    loads["resid"].wait()
    def resid_back(rows):
        v = resid[rows, :]
        factor = rms_factor(v)
        total = cot[rows, :].astype(F32) + norm_back(work[rows, :], v * factor, factor)
        resid[rows, :] = total
        d_attn[rows, :] = total.astype(LOW)
    by_rows(ROWS, 16, resid_back)
    h_attn = hand(d_attn.at[:, side(other_core, D // 2)], attn_sib)
    rs.turn(G_DOWN, 1)
    rs.turn(G_WIDE, 0)
    def gated_back(k, w):
        work[:, columns_of(k, 256)] = dot(d_attn[...], w[...], ((1,), (1,)))
    stream(3, gated_back)
    loads["mixed"].wait()
    loads["gate"].wait()
    def mixed_back(rows):
        v = mixed[rows, :]
        factor = rms_factor(v)
        normed = v * factor
        g = work[rows, :]
        d_mixed[rows, :] = norm_back(g * gate[rows, :].astype(F32), normed, factor).astype(LOW)
        gate[rows, :] = (g * normed).astype(LOW)
    by_rows(ROWS, 16, mixed_back)
    h_gate_out = hand(gate.at[:, side(other_core, D // 2)], pre_sib.at[:, pl.ds(1536, 512)])
    loads["qkv"].wait()
    def back_states(p, _):
        micro, head, rows, cols = pair_at(p)
        start = ids[pl.ds(micro, 1), 0:1]
        opening = jnp.where(ids_down[micro] == start, jnp.exp(-(row_index() + 1.0) * decays[head]), 0.0)
        opened = (qkv[rows, head_of(head, 0)].astype(F32) * opening).astype(LOW)
        local[p] = dot(opened, d_mixed[rows, cols], ((0,), (0,))).astype(LOW)
        return 0
    lax.fori_loop(0, 2 * H, back_states, 0)
    scan.start()
    rs.land(G_DOWN, 1)
    loads["gated"].wait()
    h_attn.wait_recv()
    grad_half(OUTPUT, lhs_b, d_attn, core * (D // 2), 0, attn_sib, G_OUTPUT)
    loads["first"].wait()
    h_gate_out.wait_recv()
    grad_half(INPUT, lhs_a, gate, core * (D // 2), 1536, pre_sib, G_GATE)
    rs.land(G_WIDE, 0)
    scan.join(tags_all, decays, True)

    h_wide.wait_send()
    loads["slopes"].wait()
    loads["carried"].wait()
    d_pre = d_up.at[:, 0:3 * D]
    def pair_back(p, _):
        micro, head, rows, cols = pair_at(p)
        q, k, v = (qkv[rows, head_of(head, part)] for part in range(3))
        dm = d_mixed[rows, cols]
        mask = allowed[micro] * jnp.exp(jnp.minimum(column_index() - row_index(), 0.0) * decays[head])
        weighted = (dot(q, k, ((1,), (1,))) * mask).astype(LOW)
        d_scores = (dot(dm, v, ((1,), (1,))) * mask).astype(LOW)
        boundary = jnp.where(seq > 0, tags_all[jnp.maximum(seq - 1, 0), pl.ds(2 * micro + 1, 1), :], -1.0)
        reaching = jnp.where(ids_down[micro] == boundary, jnp.exp(-(row_index() + 1.0) * decays[head]), 0.0)
        d_q = dot(d_scores, k) + dot(dm, carried[p], ((1,), (1,))) * reaching
        d_pre[rows, head_of(head, 0)] = (d_q * slopes[rows, head_of(head, 0)].astype(F32)).astype(LOW)
        work[rows, cols] = dot(d_scores, q, ((0,), (0,)))
        mixed[rows, cols] = dot(weighted, dm, ((0,), (0,)))
        return 0
    lax.fori_loop(0, 2 * H, pair_back, 0)
    h_query = hand(d_pre.at[:, side(other_core, D // 2)], pre_sib.at[:, pl.ds(0, 512)])
    rs.turn(G_OUTPUT, 0)
    rs.turn(G_GATE, 0)
    rs.land(G_DOWN, 2)
    rs.turn(G_WIDE, 1)
    h_query.wait_recv()
    grad_half(INPUT, lhs_a, d_pre, core * (D // 2), 0, pre_sib, G_QUERY)
    scan.finish()
    def pair_close(p, _):
        micro, head, rows, cols = pair_at(p)
        after = jnp.where(seq < N_SEQ - 1, tags_all[jnp.minimum(seq + 1, N_SEQ - 1), pl.ds(2 * micro, 1), :], -1.0)
        closing = jnp.where(ids_down[micro] == after, jnp.exp((row_index() - (HD - 1.0)) * decays[head]), 0.0)
        d_k = work[rows, cols] + dot(qkv[rows, head_of(head, 2)], reverse[p], ((1,), (1,))) * closing
        d_v = mixed[rows, cols] + dot(qkv[rows, head_of(head, 1)], reverse[p]) * closing
        d_pre[rows, head_of(head, 1)] = (d_k * slopes[rows, head_of(head, 1)].astype(F32)).astype(LOW)
        d_pre[rows, head_of(head, 2)] = d_v.astype(LOW)
        return 0
    lax.fori_loop(0, 2 * H, pair_close, 0)
    h_key = hand(d_pre.at[:, side(other_core, D // 2, D)], pre_sib.at[:, pl.ds(512, 512)])
    h_value = hand(d_pre.at[:, side(other_core, D // 2, 2 * D)], pre_sib.at[:, pl.ds(1024, 512)])
    rs.land(G_OUTPUT, 0)
    rs.land(G_GATE, 0)
    h_key.wait_recv()
    h_value.wait_recv()
    out = held[INPUT].reshape(D, 2 * D)
    for u in G_VALUE:
        _, _, lo, hi = BACK_UNITS[u]
        a = lo
        while a < hi:
            part, within = a // 512, a % 512
            wide = min(256, hi - a, 512 - within)
            mine = d_pre[:, pl.ds(pl.multiple_of(part * D + core * 512 + within, 128), wide)]
            out[:, a:a + wide] = (dot(lhs_a[core], mine) + dot(lhs_a[other_core], pre_sib[:, a:a + wide])).astype(LOW)
            a += wide
        rs.far((u,), 0)
    rs.turn(G_QUERY, 0)
    rs.land(G_WIDE, 1)
    def first_gate(k, w):
        work[:, columns_of(k, 256)] = dot(gate[...], w[...], ((1,), (1,)))
    stream(4, first_gate)
    rs.turn(G_VALUE, 0)
    rs.turn(G_OUTPUT, 1)
    rs.turn(G_GATE, 1)
    rs.land(G_QUERY, 0)
    def first_keys(k, w):
        work[:, columns_of(k, 256)] += dot(d_pre[:, 0:2 * D], w[...], ((1,), (1,)))
    stream(5, first_keys)
    rs.land(G_VALUE, 0)
    rs.land(G_OUTPUT, 1)
    rs.land(G_GATE, 1)
    rs.turn(G_QUERY, 1)
    rs.land(G_WIDE, 2)
    def first_values(k, w):
        work[:, columns_of(k, 256)] += dot(d_pre[:, 2 * D:3 * D], w[...], ((1,), (1,)))
    stream(6, first_values)
    rs.turn(G_VALUE, 1)
    rs.land(G_QUERY, 1)
    loads["x"].wait()
    def input_back(rows):
        v = x[rows, :].astype(F32)
        factor = rms_factor(v)
        input_grad[rows, :] = resid[rows, :] + norm_back(work[rows, :], v * factor, factor)
    by_rows(ROWS, 16, input_back)
    rs.land(G_OUTPUT, 2)
    rs.land(G_VALUE, 1)

    place = me["x"] // 2 * 2 + core
    def owner(j):
        return (dp, me["z"] * 4 + j)
    for j in range(4):
        quarters[j, 0:22, :] = final[DOWN][j * 22:(j + 1) * 22, :]
    def quarter(k):
        j = (place + k) % 4
        return pltpu.make_async_remote_copy(src_ref=quarters.at[j], dst_ref=regroup.at[place], send_sem=q_send.at[j],
            recv_sem=q_recv.at[place], device_id=owner(j), device_id_type=MESH)
    for k in range(1, 4):
        quarter(k).start()
    regroup[place] = quarters[place]
    ends = {}
    def swap(i):
        cp = pltpu.make_async_remote_copy(src_ref=final[i].at[pl.ds(pl.multiple_of(other_core * 8, 8), 8), :], dst_ref=theirs[i - 1],
            send_sem=end_send.at[i - 1], recv_sem=end_recv.at[i - 1], device_id=device(sib), device_id_type=MESH)
        cp.start()
        ends[i] = cp
    def give(i, outs, part):
        ends[i].wait_recv()
        mine, came = final[i][pl.ds(pl.multiple_of(core * 8, 8), 8), :], theirs[i - 1][...]
        both = (jnp.where(core == 0, mine, came), jnp.where(core == 0, came, mine))
        n = part // 128
        for k, out in enumerate(outs):
            for c in range(2 * n):
                out[pl.ds(c, 8, stride=2 * n), :] = both[c // n][:, k * part + (c % n) * 128:k * part + (c % n + 1) * 128]
    swap(WIDE)
    swap(OUTPUT)
    for k in range(1, 4):
        j = (place + k) % 4
        pltpu.make_async_remote_copy(src_ref=regroup.at[j], dst_ref=regroup.at[j], send_sem=q_send.at[j],
            recv_sem=q_recv.at[j], device_id=owner((place + 1) % 4), device_id_type=MESH).wait_recv()
    for j in range(4):
        for k in range(2):
            t = (j % 2) * 4 + (j // 2) * 2 + k
            grads[7][pl.ds(t, 22, stride=8), :] = regroup[j, 0:22, k * 128:(k + 1) * 128]
    ends[WIDE].wait_recv()
    mine, came = final[WIDE][pl.ds(pl.multiple_of(core * 8, 8), 8), :], theirs[WIDE - 1][...]
    for k, both in enumerate((jnp.where(core == 0, mine, came), jnp.where(core == 0, came, mine))):
        for c in range(22):
            grads[5 + k][pl.ds(c, 8, stride=22), :] = both[:, c * 128:(c + 1) * 128]
    give(OUTPUT, grads[4:5], 512)
    rs.land(G_GATE, 2)
    rs.land(G_QUERY, 2)
    rs.land(G_VALUE, 2)
    swap(INPUT)
    give(INPUT, grads[0:4], 512)
    for cp in ends.values():
        cp.wait_send()
    for k in range(1, 4):
        quarter(k).wait_send()
    for cp in passed[1:]:
        cp.wait_send()
    scan.drain()
    rs.drain()


def backward(ids, tags_all, decays, arrays):
    v = pl.BlockSpec(memory_space=pltpu.VMEM)
    anywhere = pl.BlockSpec(memory_space=pl.ANY)
    sds = jax.ShapeDtypeStruct
    vm = pltpu.VMEM
    n = len(BACK_UNITS)
    scratch = [vm(live_dims(()) + tail, LOW) for tail in HELD]
    for stage in range(3):
        for i, s, lo, hi in BACK_UNITS:
            tail = (hi - lo, 256) if i == DOWN else (HELD[i][0], hi - lo)
            scratch.append(vm((3,) + live_dims(BACK_ORDERS[s][:stage + 1]) + tail, LOW))
    scratch += [vm(tail, F32) for tail in HELD] + [vm((8, tail[1]), F32) for tail in HELD[1:]]
    full = lambda width, kind=LOW: vm((ROWS, width), kind)
    scratch += [vm((4, 24, 256), F32), vm((4, 24, 256), F32), vm((3, 256, FF), LOW), vm((2, FF, ROWS), LOW),
        vm((2, D, ROWS), LOW), vm((2, D, ROWS), LOW), vm((2, ROWS, D // 2), LOW), full(D), full(2 * FF), full(FF), full(D), full(D // 2),
        full(2 * D), full(2 * FF), full(3 * D), full(2 * D), full(D), full(D, F32), full(D, F32), full(D), full(D, F32), full(D)]
    scratch += [vm((N_SEQ, HD, HD), LOW)] * 5 + [vm((2, HD, HD), F32)] * 2
    scratch += [DMA((16,)), DMA((3,)), DMA((n, 3, 6)), DMA((n, 3, 6))] + [DMA((N_SEQ,))] * 4 + [DMA((6,))] * 2 + [DMA((3,))] * 2 + [DMA((4,))] * 2
    return pl.pallas_call(
        backward_kernel,
        out_shape=[sds((ROWS, D), F32)] + [sds((64, 128), F32)] * 5 + [sds((176, 128), F32)] * 3,
        in_specs=[v, v, pl.BlockSpec(memory_space=pltpu.SMEM)] + [anywhere] * len(arrays),
        out_specs=[v] * 9,
        scratch_shapes=scratch,
        compiler_params=pltpu.CompilerParams(collective_id=1, has_side_effects=True, vmem_limit_bytes=60 << 20),
        name="backward_and_scatter",
    )(ids, tags_all, decays, *arrays)


def copy_kernel(*refs):
    n = len(refs) // 3
    sems = refs[-1]
    into = [pltpu.make_async_copy(refs[k], refs[2 * n + k], sems.at[0, k]) for k in range(n)]
    out = [pltpu.make_async_copy(refs[2 * n + k], refs[n + k], sems.at[1, k]) for k in range(n)]
    for cp in into:
        cp.start()
    for a, b in zip(into, out):
        a.wait()
        b.start()
    for cp in out:
        cp.wait()


def hand_out(arrays):
    anywhere = pl.BlockSpec(memory_space=pl.ANY)
    return pl.pallas_call(
        copy_kernel, out_shape=[jax.ShapeDtypeStruct(a.shape, a.dtype) for a in arrays],
        in_specs=[anywhere] * len(arrays), out_specs=[anywhere] * len(arrays),
        scratch_shapes=[pltpu.VMEM(a.shape, a.dtype) for a in arrays] + [DMA((2, len(arrays)))], name="hand_out",
    )(*arrays)


def on_device(hidden_in, seg_ids, decay_rates, grad_out, *weights):
    x, cot = hidden_in.reshape(ROWS, D), grad_out.reshape(ROWS, D)
    ids = seg_ids.reshape(2, HD).astype(F32)
    (act, tags_all, qkv, slopes, gate, mixed, resid, up, carried, w_in, w_output, w_up, w_down, t_first, t_gated, t_second,
     t_product, b_branch) = forward(x, cot, ids, decay_rates, [w.reshape(-1, 128) for w in weights])
    input_grad, *grads = backward(ids, tags_all, decay_rates, [
        x, cot, qkv, slopes, gate, mixed, resid, up, carried, w_in.reshape(D, 4 * D), w_output.reshape(D, D),
        w_up.reshape(D, 2 * FF), w_down, t_first, t_gated, t_second, t_product, b_branch])
    act, input_grad, *grads = hand_out([act, input_grad, *grads])
    return (act.reshape(hidden_in.shape), input_grad.reshape(hidden_in.shape), *(g.reshape(-1) for g in grads))


def solution(mesh):
    tokens = P(None, "dp", "seq", None)
    flat = P(("dp", "seq"))
    return jax.shard_map(
        on_device, mesh=mesh,
        in_specs=(tokens, P(None, "dp", "seq"), P(), tokens) + (flat,) * 8,
        out_specs=(tokens, tokens) + (flat,) * 8,
        check_vma=False,
    )
```

```python
import functools
import jax, jax.numpy as jnp
from jax import lax
from jax.experimental import pallas as pl
from jax.experimental.pallas import tpu as pltpu
from jax.sharding import PartitionSpec as P

MESH = pl.DeviceIdType.MESH
RING = 4
D = 1024
H = 8
HD = 128
FF = 2816
ROWS = 256
N_SEQ = 16
EPSILON = 1e-06
LOW = jnp.bfloat16
F32 = jnp.float32
OWNERS = (4, 2, 4, 2, 2)
DMA = pltpu.SemaphoreType.DMA
ORDERS = (("x", "y", "z"), ("y", "z", "x"), ("z", "x", "y"))
SPLIT_ROWS = (False, False, False, True)


def tiles(array, bounds, grain=128):
    return [(array, s, lo * grain, hi * grain) for s, (lo, hi) in enumerate(zip(bounds[:-1], bounds[1:]))]


CHUNKS = (
    tuple(tiles(0, (0, 10, 20, 32))),
    tuple(tiles(1, (0, 4, 8)) + tiles(2, (0, 15, 30, 44))),
    tuple(tiles(3, (0, 7, 14, 22), 8)),
)
UNITS = CHUNKS[0] + CHUNKS[1] + CHUNKS[2]
C1, C2, C3 = (tuple(UNITS.index(u) for u in chunk) for chunk in CHUNKS)
C2_FIRST = C2[:2]


def where_am_i():
    dp = lax.axis_index("dp")
    seq = lax.axis_index("seq")
    return {"x": (seq // 2 % 2) * 2 + dp % 2, "y": dp // 2, "z": seq // 4, "c": seq % 2}


def device(at):
    return (at["y"] * 2 + at["x"] % 2, at["z"] * 4 + (at["x"] // 2) * 2 + at["c"])


def moved(at, axis, by):
    out = dict(at)
    out[axis] = (at[axis] + by) % RING if axis != "c" else 1 - at[axis]
    return out


def block(ref, at, whole, lo, hi, rows):
    every = slice(None)
    pick = lambda axis, value: every if axis in whole else value
    span = pl.ds(lo, hi - lo)
    return ref.at[
        pick("y", at["y"]), pick("x", at["x"] % 2), pick("z", at["z"]), pick("x", at["x"] // 2), at["c"],
        span if rows else every, every if rows else span,
    ]


def middle(lo, hi, rows):
    grain = 8 if rows else 128
    return lo + ((hi - lo) // grain // 2) * grain


def neighbours(me):
    return [moved(me, a, d) for a in "xyz" for d in (1, -1)] + [moved(me, "c", 1)]


def dot(a, b, dims=((1,), (0,))):
    return lax.dot_general(a, b, (dims, ((), ())), preferred_element_type=F32)


def by_rows(count, size, body):
    def one(k, _):
        body(pl.ds(pl.multiple_of(k * size, size), size))
        return 0
    lax.fori_loop(0, count // size, one, 0)


def columns_of(k, size):
    return pl.ds(pl.multiple_of(k * size, size), size)


def sigmoid(u):
    return 1.0 / (1.0 + jnp.exp(-u))


def rms_factor(v):
    return lax.rsqrt(jnp.mean(v * v, axis=-1, keepdims=True) + EPSILON)


class Gather:
    def __init__(self, arrays, me, send_sem, recv_sem, csend_sem, crecv_sem):
        self.arrays, self.me = arrays, me
        self.send_sem, self.recv_sem, self.csend_sem, self.crecv_sem = send_sem, recv_sem, csend_sem, crecv_sem
        self.sends = []

    def copy(self, ref, u, slot, to):
        return pltpu.make_async_remote_copy(src_ref=ref, dst_ref=ref, send_sem=self.send_sem.at[u, slot],
            recv_sem=self.recv_sem.at[u, slot], device_id=device(to), device_id_type=MESH)

    def ccopy(self, ref, u, slot):
        return pltpu.make_async_remote_copy(src_ref=ref, dst_ref=ref, send_sem=self.csend_sem.at[u, slot],
            recv_sem=self.crecv_sem.at[u, slot], device_id=device(moved(self.me, "c", 1)), device_id_type=MESH)

    def go(self, cp):
        cp.start()
        self.sends.append(cp)

    def part(self, u, at, stage, half=None):
        i, s, lo, hi = UNITS[u]
        rows = SPLIT_ROWS[i]
        mid = middle(lo, hi, rows)
        lo, hi = (lo, hi) if half is None else ((lo, mid), (mid, hi))[half]
        return block(self.arrays[i], at, ORDERS[s][:stage], lo, hi, rows)

    def axis(self, u, stage):
        return ORDERS[UNITS[u][1]][stage]

    def begin(self, units, stage):
        for u in units:
            a = self.axis(u, stage)
            for k, (half, by) in enumerate(((0, 1), (1, -1), (1, 1), (0, -1))):
                self.go(self.copy(self.part(u, self.me, stage, half), u, 6 * stage + k, moved(self.me, a, by)))
            if stage == 2:
                self.go(self.ccopy(self.part(u, self.me, stage), u, 0))

    def relay(self, units, stage):
        for u in units:
            a = self.axis(u, stage)
            for half, by in ((0, 1), (1, -1)):
                first = self.part(u, moved(self.me, a, -by), stage, half)
                self.copy(first, u, 6 * stage + half, moved(self.me, a, by)).wait_recv()
                self.go(self.copy(first, u, 6 * stage + 4 + half, moved(self.me, a, by)))

    def finish(self, units, stage):
        for u in units:
            a = self.axis(u, stage)
            for k, by, half in ((2, -1, 1), (3, 1, 0), (4, 2, 0), (5, 2, 1)):
                self.copy(self.part(u, moved(self.me, a, by), stage, half), u, 6 * stage + k, moved(self.me, a, 1)).wait_recv()
            if stage == 2:
                for k, by in enumerate((-1, 1, 2)):
                    self.go(self.ccopy(self.part(u, moved(self.me, a, by), stage), u, 1 + k))

    def advance(self, units, stage):
        for u in units:
            self.finish((u,), stage)
            self.begin((u,), stage + 1)

    def arrive(self, units):
        sib = moved(self.me, "c", 1)
        for u in units:
            for k, by in enumerate((0, -1, 1, 2)):
                self.ccopy(self.part(u, moved(sib, self.axis(u, 2), by), 2), u, k).wait_recv()

    def drain(self):
        for cp in self.sends:
            cp.wait_send()


class Scan:
    def __init__(self, local, came, going, carried, sems):
        self.me, self.dp = lax.axis_index("seq"), lax.axis_index("dp")
        self.local, self.came, self.going, self.carried = local, came, going, carried
        self.send1, self.recv1, self.send2, self.recv2 = sems

    def to(self, k):
        return (self.me + k) % N_SEQ

    def out(self, to):
        return pltpu.make_async_remote_copy(src_ref=self.local.at[to], dst_ref=self.came.at[self.me], send_sem=self.send1.at[to],
            recv_sem=self.recv1.at[self.me], device_id=(self.dp, to), device_id_type=MESH)

    def back(self, to):
        return pltpu.make_async_remote_copy(src_ref=self.going.at[to], dst_ref=self.carried.at[self.me], send_sem=self.send2.at[to],
            recv_sem=self.recv2.at[self.me], device_id=(self.dp, to), device_id_type=MESH)

    def arrival(self, ref, ssem, rsem, frm):
        return pltpu.make_async_remote_copy(src_ref=ref.at[frm], dst_ref=ref.at[frm], send_sem=ssem.at[frm],
            recv_sem=rsem.at[frm], device_id=(self.dp, self.to(1)), device_id_type=MESH)

    def each(self, body):
        def one(k, _):
            body(self.to(k))
            return 0
        lax.fori_loop(1, N_SEQ, one, 0)

    def start(self):
        self.each(lambda to: self.out(to).start())
        self.came[self.me] = self.local[self.me]

    def join(self, tags_all, decays, backward):
        self.each(lambda frm: self.arrival(self.came, self.send1, self.recv1, frm).wait_recv())
        micro, head = self.me // H, self.me % H
        fade = jnp.exp(-float(HD) * jnp.full((1, HD), decays[head], F32))
        first = lambda b: tags_all[b, pl.ds(2 * micro, 1), :]
        last = lambda b: tags_all[b, pl.ds(2 * micro + 1, 1), :]
        acc = jnp.zeros((HD, HD), F32)
        previous = None
        for b in (range(N_SEQ - 1, -1, -1) if backward else range(N_SEQ)):
            self.going[b] = acc.astype(LOW)
            if previous is None:
                acc = self.came[b].astype(F32)
            else:
                near = (last(b) == first(previous)) if backward else (first(b) == last(previous))
                acc = self.came[b].astype(F32) + jnp.where((first(b) == last(b)) & near, fade, 0.0) * acc
            previous = b
        self.carried[self.me] = self.going[self.me]
        self.each(lambda to: self.back(to).start())

    def finish(self):
        self.each(lambda frm: self.arrival(self.carried, self.send2, self.recv2, frm).wait_recv())

    def drain(self):
        def one(to):
            self.out(to).wait_send()
            self.back(to).wait_send()
        self.each(one)


def spread(row):
    across = jnp.broadcast_to(row, (HD, HD))
    return across.T, across


def row_index():
    return lax.broadcasted_iota(jnp.int32, (HD, HD), 0).astype(F32)


def column_index():
    return lax.broadcasted_iota(jnp.int32, (HD, HD), 1).astype(F32)


def each_pair(body, together=4):
    def some(k, _):
        for i in range(together):
            body(k * together + i, 0)
        return 0
    lax.fori_loop(0, 2 * H // together, some, 0)


def pair_at(p):
    micro, head = p // H, p % H
    return micro, head, pl.ds(pl.multiple_of(micro * HD, HD), HD), pl.ds(pl.multiple_of(head * HD, HD), HD)


def transpose_into(src, dst, count):
    def one(k, _):
        at = columns_of(k, 128)
        dst[at, :] = src[:, at].T
        return 0
    lax.fori_loop(0, count // 128, one, 0)


def forward_kernel(*refs):
    (x, cot, ids, decays), small = refs[:4], refs[4:12]
    (act, tags_all, o_qkv, o_slopes, o_gate, o_mixed, o_resid, o_up, o_carried, o_in, o_output, o_wide, o_down,
     t_first, t_gated, t_second, t_product, b_branch) = refs[12:30]
    (w_in, w_output, w_up, w_flat, w_down, pre, first_in, qkv, slopes, gate, mixed, resid, up, gated, second, product,
     first_t, gated_t, second_t, product_t, carried, local, came, going, spare, tag, allowed, kept_mask, ids_down,
     send_sem, recv_sem, csend_sem, crecv_sem, tag_send, tag_recv, s1, r1, s2, r2, out_sem, pass_send, pass_recv) = refs[30:]
    me = where_am_i()
    sib = moved(me, "c", 1)
    seq, dp = lax.axis_index("seq"), lax.axis_index("dp")
    to = lambda k: (seq + k) % N_SEQ
    barrier = pltpu.get_barrier_semaphore()
    close = neighbours(me)
    for other in close:
        pl.semaphore_signal(barrier, inc=1, device_id=device(other), device_id_type=MESH)

    def greet(k, _):
        pl.semaphore_signal(barrier, inc=1, device_id=(dp, to(k)), device_id_type=MESH)
        return 0
    lax.fori_loop(1, N_SEQ, greet, 0)

    here = (me["y"], me["x"] % 2, me["z"], me["x"] // 2, me["c"])
    def place(src, target, base, width):
        n = width // 128
        spare[pl.ds(0, 8 * n), :] = src[...].astype(F32)
        for c in range(n):
            target[(*here, slice(None), pl.ds(base + c * 128, 128))] = spare[pl.ds(c, 8, stride=n), :].astype(LOW)
    for k in range(4):
        place(small[k], w_in, k * D, D)
    place(small[4], w_output, 0, D)
    place(small[5], w_up, 0, FF)
    place(small[6], w_up, FF, FF)
    w_flat[here] = small[7][...]
    tag[...] = jnp.zeros((8, HD), F32)
    for m in range(2):
        tag[2 * m:2 * m + 1, :] = jnp.broadcast_to(ids[m:m + 1, 0:1], (1, HD))
        tag[2 * m + 1:2 * m + 2, :] = jnp.broadcast_to(ids[m:m + 1, HD - 1:HD], (1, HD))
    tags_all[seq] = tag[...]
    pl.semaphore_wait(barrier, len(close) + N_SEQ - 1)

    g = Gather((w_in, w_output, w_up, w_flat), me, send_sem, recv_sem, csend_sem, crecv_sem)
    scan = Scan(local, came, going, carried, (s1, r1, s2, r2))
    g.begin(C1, 0)
    g.begin(C2, 0)
    g.begin(C3, 0)

    kept, passed = [], []
    def keep(src, dst):
        cp = pltpu.make_async_copy(src, dst, out_sem.at[len(kept)])
        cp.start()
        kept.append(cp)
    def hand(mine, theirs, dst):
        keep(mine, dst.at[me["c"]])
        k = len(passed)
        cp = pltpu.make_async_remote_copy(src_ref=theirs, dst_ref=dst.at[me["c"]], send_sem=pass_send.at[k],
            recv_sem=pass_recv.at[k], device_id=device(sib), device_id_type=MESH)
        cp.start()
        passed.append((cp, dst))

    def tag_copy(other):
        return pltpu.make_async_remote_copy(src_ref=tag, dst_ref=tags_all.at[seq], send_sem=tag_send.at[other],
            recv_sem=tag_recv.at[seq], device_id=(dp, other), device_id_type=MESH)
    scan.each(lambda other: tag_copy(other).start())

    def norm_in(rows):
        v = x[rows, :].astype(F32)
        first_in[rows, :] = (v * rms_factor(v)).astype(LOW)
    by_rows(ROWS, 32, norm_in)
    g.relay(C1, 0)
    g.relay(C2, 0)
    g.relay(C3, 0)
    g.advance(C1, 0)
    for m in range(2):
        down, across = spread(ids[m:m + 1, :])
        ids_down[m] = down
        allowed[m] = jnp.where((down == across) & (row_index() >= column_index()), 1.0, 0.0)
        kept_mask[m] = jnp.where(down == jnp.broadcast_to(ids[m:m + 1, HD - 1:HD], (HD, HD)), 1.0, 0.0)
    g.relay(C1, 1)
    g.advance(C2, 0)
    g.advance(C1, 1)
    g.advance(C3, 0)
    half = lambda c: cot.at[:, pl.ds(pl.multiple_of(c * 512, 512), 512)]
    hand(half(me["c"]), half(sib["c"]), b_branch)
    transpose_into(first_in, first_t, D)
    hand(first_t, first_t, t_first)
    g.relay(C2, 1)
    g.relay(C1, 2)
    g.relay(C3, 1)
    g.advance(C2, 1)
    g.finish(C1, 2)
    g.arrive(C1)
    keep(w_in, o_in)

    m_in = w_in.reshape(D, 4 * D)
    def project(k, _):
        cols = columns_of(k, 512)
        pre[:, cols] = dot(first_in[...], m_in[:, cols])
        return 0
    lax.fori_loop(0, 8, project, 0)
    g.relay(C2, 2)
    g.advance(C3, 1)

    def rows_of_heads(rows):
        for k in range(2):
            u = pre[rows, k * D:(k + 1) * D]
            s = sigmoid(u)
            qkv[rows, k * D:(k + 1) * D] = (u * s).astype(LOW)
            slopes[rows, k * D:(k + 1) * D] = (s * (1.0 + u * (1.0 - s))).astype(LOW)
        qkv[rows, 2 * D:3 * D] = pre[rows, 2 * D:3 * D].astype(LOW)
        gate[rows, :] = pre[rows, 3 * D:4 * D].astype(LOW)
    by_rows(ROWS, 32, rows_of_heads)
    keep(qkv, o_qkv)
    keep(slopes, o_slopes)
    keep(gate, o_gate)

    def states(p, _):
        micro, head, rows, _ = pair_at(p)
        keeping = jnp.exp((row_index() - (HD - 1.0)) * decays[head]) * kept_mask[micro]
        held = (qkv[rows, head_of(head, 1)].astype(F32) * keeping).astype(LOW)
        local[p] = dot(held, qkv[rows, head_of(head, 2)], ((0,), (0,))).astype(LOW)
        return 0
    each_pair(states)
    scan.start()

    def within(p, _):
        micro, head, rows, cols = pair_at(p)
        mask = allowed[micro] * jnp.exp(jnp.minimum(column_index() - row_index(), 0.0) * decays[head])
        weighted = (dot(qkv[rows, head_of(head, 0)], qkv[rows, head_of(head, 1)], ((1,), (1,))) * mask).astype(LOW)
        mixed[rows, cols] = dot(weighted, qkv[rows, head_of(head, 2)])
        return 0
    each_pair(within)
    scan.each(lambda frm: pltpu.make_async_remote_copy(src_ref=tag, dst_ref=tags_all.at[frm], send_sem=tag_send.at[frm],
        recv_sem=tag_recv.at[frm], device_id=(dp, to(1)), device_id_type=MESH).wait_recv())
    scan.join(tags_all, decays, False)
    g.finish(C2, 2)
    g.relay(C3, 2)
    g.arrive(C2_FIRST)
    keep(w_output, o_output)
    scan.finish()
    keep(carried, o_carried)

    def crossing(p, _):
        micro, head, rows, cols = pair_at(p)
        boundary = jnp.where(seq > 0, tags_all[jnp.maximum(seq - 1, 0), pl.ds(2 * micro + 1, 1), :], -1.0)
        reaching = jnp.where(ids_down[micro] == boundary, jnp.exp(-(row_index() + 1.0) * decays[head]), 0.0)
        mixed[rows, cols] += dot(qkv[rows, head_of(head, 0)], carried[p]) * reaching
        return 0
    each_pair(crossing)
    keep(mixed, o_mixed)

    def gate_rows(rows):
        v = mixed[rows, :]
        gated[rows, :] = (v * rms_factor(v) * pre[rows, 3 * D:4 * D]).astype(LOW)
    by_rows(ROWS, 32, gate_rows)
    m_output = w_output.reshape(D, D)
    def output(k, _):
        cols = columns_of(k, 512)
        resid[:, cols] = x[:, cols].astype(F32) + dot(gated[...], m_output[:, cols])
        for c in range(4):
            at = columns_of(k * 4 + c, 128)
            gated_t[at, :] = gated[:, at].T
        return 0
    lax.fori_loop(0, 2, output, 0)
    keep(resid, o_resid)
    def norm_second(rows):
        v = resid[rows, :]
        second[rows, :] = (v * rms_factor(v)).astype(LOW)
    by_rows(ROWS, 32, norm_second)
    hand(gated_t, gated_t, t_gated)
    g.finish(C3, 2)
    g.arrive(C2[2:])
    keep(w_up, o_wide)
    m_up = w_up.reshape(D, 2 * FF)
    def widen(k, _):
        cols, more = columns_of(k, 256), pl.ds(pl.multiple_of(k * 256 + FF, 256), 256)
        left = dot(second[...], m_up[:, cols])
        right = dot(second[...], m_up[:, more])
        up[:, cols] = left.astype(LOW)
        up[:, more] = right.astype(LOW)
        both = (left * right).astype(LOW)
        product[:, cols] = both
        product_t[cols, :] = both.T
        return 0
    lax.fori_loop(0, 11, widen, 0)
    keep(up, o_up)
    hand(product_t, product_t, t_product)
    g.arrive(C3)
    flat = w_flat.reshape(128 * 176, 128)
    def arrange(k, _):
        spare[...] = flat[pl.ds(pl.multiple_of(k * 1408, 1408), 1408), :].astype(F32)
        for c in range(8):
            w_down[pl.ds(pl.multiple_of(k * 176, 176), 176), c * 128:(c + 1) * 128] = spare[pl.ds(c, 176, stride=8), :].astype(LOW)
        return 0
    lax.fori_loop(0, 16, arrange, 0)
    keep(w_down, o_down)
    def last(k, _):
        cols = columns_of(k, 512)
        act[:, cols] = (resid[:, cols] + dot(product[...], w_down[:, cols])).astype(LOW)
        for c in range(4):
            at = columns_of(k * 4 + c, 128)
            second_t[at, :] = second[:, at].T
        return 0
    lax.fori_loop(0, 2, last, 0)
    hand(second_t, second_t, t_second)
    for cp in kept:
        cp.wait()
    for k, (cp, dst) in enumerate(passed):
        cp.wait_send()
        there = dst.at[sib["c"]]
        pltpu.make_async_remote_copy(src_ref=there, dst_ref=there, send_sem=pass_send.at[k], recv_sem=pass_recv.at[k],
            device_id=device(sib), device_id_type=MESH).wait_recv()
    scan.each(lambda other: tag_copy(other).wait_send())
    scan.drain()
    g.drain()


def forward(x, cot, ids, decays, pieces):
    v = pl.BlockSpec(memory_space=pltpu.VMEM)
    anywhere = pl.BlockSpec(memory_space=pl.ANY)
    sds = jax.ShapeDtypeStruct
    n = len(UNITS)
    outs = [sds((ROWS, D), LOW), sds((N_SEQ, 8, HD), F32), sds((ROWS, 3 * D), LOW), sds((ROWS, 2 * D), LOW), sds((ROWS, D), LOW),
        sds((ROWS, D), F32), sds((ROWS, D), F32), sds((ROWS, 2 * FF), LOW), sds((N_SEQ, HD, HD), LOW),
        sds(OWNERS + (8, 4 * D), LOW), sds(OWNERS + (8, D), LOW), sds(OWNERS + (8, 2 * FF), LOW), sds((FF, D), LOW),
        sds((2, D, ROWS), LOW), sds((2, D, ROWS), LOW), sds((2, D, ROWS), LOW), sds((2, FF, ROWS), LOW), sds((2, ROWS, D // 2), LOW)]
    vm = pltpu.VMEM
    scratch = [vm(OWNERS + (8, 4 * D), LOW), vm(OWNERS + (8, D), LOW), vm(OWNERS + (8, 2 * FF), LOW), vm(OWNERS + (176, 128), LOW),
        vm((FF, D), LOW), vm((ROWS, 4 * D), F32), vm((ROWS, D), LOW), vm((ROWS, 3 * D), LOW), vm((ROWS, 2 * D), LOW), vm((ROWS, D), LOW),
        vm((ROWS, D), F32), vm((ROWS, D), F32), vm((ROWS, 2 * FF), LOW), vm((ROWS, D), LOW), vm((ROWS, D), LOW), vm((ROWS, FF), LOW),
        vm((D, ROWS), LOW), vm((D, ROWS), LOW), vm((D, ROWS), LOW), vm((FF, ROWS), LOW)] + [vm((N_SEQ, HD, HD), LOW)] * 4 + [
        vm((1408, 128), F32), vm((8, HD), F32)] + [vm((2, HD, HD), F32)] * 3 + [
        DMA((n, 18)), DMA((n, 18)), DMA((n, 4)), DMA((n, 4))] + [DMA((N_SEQ,))] * 6 + [DMA((20,)), DMA((5,)), DMA((5,))]
    return pl.pallas_call(
        forward_kernel, out_shape=outs,
        in_specs=[v, v, v, pl.BlockSpec(memory_space=pltpu.SMEM)] + [v] * 8,
        out_specs=[v] * 2 + [anywhere] * 16,
        scratch_shapes=scratch,
        compiler_params=pltpu.CompilerParams(collective_id=0, has_side_effects=True, vmem_limit_bytes=60 << 20),
        name="gather_and_forward",
    )(x, cot, ids, decays, *pieces)


def head_of(head, part):
    return pl.ds(pl.multiple_of(part * D + head * HD, HD), HD)


DOWN, WIDE, OUTPUT, INPUT = range(4)
HELD = ((88, 256), (16, FF), (16, D // 2), (16, 2 * D))
GROUPS = (
    tiles(DOWN, (0, 3, 7, 11), 8),
    tiles(WIDE, (0, 7, 14, 22)),
    [(OUTPUT, 0, 0, 256), (OUTPUT, 1, 256, 512)],
    [(INPUT, 1, 1536, 1792), (INPUT, 2, 1792, 2048)],
    [(INPUT, 2, 0, 256), (INPUT, 0, 256, 512)],
    [(INPUT, 0, 512, 896), (INPUT, 1, 896, 1280), (INPUT, 2, 1280, 1536)],
)
BACK_UNITS = tuple(unit for group in GROUPS for unit in group)
G_DOWN, G_WIDE, G_OUTPUT, G_GATE, G_QUERY, G_VALUE = (tuple(BACK_UNITS.index(unit) for unit in group) for group in GROUPS)
BACK_ORDERS = tuple(order[::-1] for order in ORDERS)
DIMS = (("y", 4), ("x", 2), ("z", 4), ("x", 2))


def live_dims(fixed):
    return tuple(n for a, n in DIMS if a not in fixed)


def part_of(ref, at, fixed, gone, lo, hi, rows, lead=()):
    every = slice(None)
    idx = []
    for k, (a, n) in enumerate(DIMS):
        if a in gone:
            continue
        if a in fixed:
            idx.append((at["x"] % 2 if k == 1 else at["x"] // 2) if a == "x" else at[a])
        else:
            idx.append(every)
    span = pl.ds(lo, hi - lo)
    return ref.at[(*lead, *idx, span if rows else every, every if rows else span)]


def accumulate(dst, srcs, dims, out=None):
    target = dst if out is None else out
    rows, width = dst.shape[-2:]
    most = max(1, 64 // max(1, rows * width // 1024))
    cut, inner = len(dims), 1
    while cut > 0 and inner * dims[cut - 1] <= most:
        cut -= 1
        inner *= dims[cut]
    near = [()]
    for d in dims[cut:]:
        near = [at + (i,) for at in near for i in range(d)]
    def group(lead):
        places = [lead + at if dims else ... for at in near]
        totals = []
        for at in places:
            total = dst[at].astype(F32)
            for s in srcs:
                total = total + s[at].astype(F32)
            totals.append(total.astype(target.dtype))
        for at, total in zip(places, totals):
            target[at] = total
    count = 1
    for d in dims[:cut]:
        count *= d
    def one(k, _):
        idx, rest = [], k
        for m, d in enumerate(dims[:cut][::-1]):
            last = m == cut - 1
            idx.append(rest if last else rest % d)
            rest = rest if last else rest // d
        group(tuple(idx[::-1]))
        return 0
    if count == 1:
        group((0,) * cut)
    else:
        lax.fori_loop(0, count, one, 0)


class Scatter:
    def __init__(self, held, slots, final, me, send_sem, recv_sem):
        self.held, self.slots, self.final, self.me = held, slots, final, me
        self.send_sem, self.recv_sem = send_sem, recv_sem
        self.sends = []

    def spans(self, u):
        i, s, lo, hi = BACK_UNITS[u]
        return self.held[i], BACK_ORDERS[s], i == DOWN, lo, middle(lo, hi, i == DOWN), hi

    def slot(self, u, stage, k, lo, hi):
        _, order, rows, base, _, _ = self.spans(u)
        return part_of(self.slots[stage][u], self.me, (), order[:stage + 1], lo - base, hi - base, rows, (k,))

    def send(self, src, dst, u, stage, k, to):
        cp = pltpu.make_async_remote_copy(src_ref=src, dst_ref=dst, send_sem=self.send_sem.at[u, stage, k],
            recv_sem=self.recv_sem.at[u, stage, k], device_id=device(to), device_id_type=MESH)
        cp.start()
        self.sends.append(cp)

    def got(self, ref, u, stage, k):
        pltpu.make_async_remote_copy(src_ref=ref, dst_ref=ref, send_sem=self.send_sem.at[u, stage, k],
            recv_sem=self.recv_sem.at[u, stage, k], device_id=device(moved(self.me, "c", 1)), device_id_type=MESH).wait_recv()

    def far(self, units, stage):
        for u in units:
            held, order, rows, lo, mid, hi = self.spans(u)
            axis, fixed = order[stage], order[:stage + 1]
            above, below, across = (moved(self.me, axis, by) for by in (1, -1, 2))
            mine = lambda at, a, b: part_of(held, at, fixed, (), a, b, rows)
            if stage > 0:
                for k, at in enumerate((across, above, below)):
                    self.send(mine(at, lo, hi), self.slot(u, stage, k, lo, hi), u, stage, k, at)
                continue
            self.send(mine(across, lo, mid), self.slot(u, stage, 0, lo, mid), u, stage, 0, above)
            self.send(mine(across, mid, hi), self.slot(u, stage, 0, mid, hi), u, stage, 1, below)
            self.send(mine(above, mid, hi), self.slot(u, stage, 1, mid, hi), u, stage, 2, above)
            self.send(mine(below, lo, mid), self.slot(u, stage, 2, lo, mid), u, stage, 3, below)

    def turn(self, units, stage):
        for u in units:
            held, order, rows, lo, mid, hi = self.spans(u)
            fixed = order[:stage + 1]
            for k, (by, a, b) in enumerate(((1, lo, mid), (-1, mid, hi))):
                to = moved(self.me, order[stage], by)
                came = self.slot(u, stage, 0, a, b)
                self.got(came, u, stage, k)
                sums = part_of(held, to, fixed, (), a, b, rows)
                accumulate(sums, [came], live_dims(fixed))
                self.send(sums, self.slot(u, stage, 1 + k, a, b), u, stage, 4 + k, to)

    def land(self, units, stage):
        for u in units:
            held, order, rows, lo, mid, hi = self.spans(u)
            fixed = order[:stage + 1]
            mine = part_of(held, self.me, fixed, (), lo, hi, rows)
            if stage > 0:
                came = [self.slot(u, stage, k, lo, hi) for k in range(3)]
                for k in range(3):
                    self.got(came[k], u, stage, k)
                span = pl.ds(lo, hi - lo)
                if stage == 2:
                    accumulate(mine, came, (), self.final[BACK_UNITS[u][0]].at[(span, slice(None)) if rows else (slice(None), span)])
                else:
                    accumulate(mine, came, live_dims(fixed))
                    self.far((u,), 2)
                continue
            for k, (a, b) in ((2, (mid, hi)), (3, (lo, mid)), (4, (lo, mid)), (5, (mid, hi))):
                self.got(self.slot(u, stage, 1 + k % 2, a, b), u, stage, k)
            accumulate(mine, [self.slot(u, stage, 1 + k, lo, hi) for k in range(2)], live_dims(fixed))
            self.far((u,), stage + 1)

    def drain(self):
        for cp in self.sends:
            cp.wait_send()


def norm_back(upstream, normed, factor):
    return factor * (upstream - normed * jnp.mean(upstream * normed, axis=-1, keepdims=True))


def backward_kernel(*refs):
    (h_ids, h_tags, decays, h_x, h_cot, h_qkv, h_slopes, h_gate, h_mixed, h_resid, h_up, h_carried, w_in, w_output, w_up, w_down,
     t_first, t_gated, t_second, t_product, b_branch) = refs[:21]
    o_input, o_grads = refs[21], refs[22:30]
    refs = refs[30:]
    input_grad, grads, ids, tags_all, refs = refs[0], refs[1:9], refs[9], refs[10], refs[11:]
    n = len(BACK_UNITS)
    held, refs = refs[:4], refs[4:]
    slots = [refs[k * n:(k + 1) * n] for k in range(3)]
    refs = refs[3 * n:]
    final, theirs, refs = refs[:4], refs[4:7], refs[7:]
    (quarters, regroup, wbuf, product_t, lhs_a, lhs_b, branch, cot, d_up, up_sib, d_attn, attn_sib, pre_sib,
     up, qkv, slopes, gate, mixed, resid, x, work, d_mixed, carried, local, came, going, reverse, ids_down, allowed,
     load_sem, wsem, send_sem, recv_sem, s1, r1, s2, r2, pass_send, pass_recv, end_send, end_recv, q_send, q_recv, out_sem) = refs
    me = where_am_i()
    sib = moved(me, "c", 1)
    core, other_core = me["c"], sib["c"]
    seq, dp = lax.axis_index("seq"), lax.axis_index("dp")
    to = lambda k: (seq + k) % N_SEQ
    barrier = pltpu.get_barrier_semaphore()
    close = neighbours(me) + [moved(me, a, 2) for a in "xyz"]
    for other in close:
        pl.semaphore_signal(barrier, inc=1, device_id=device(other), device_id_type=MESH)

    def greet(k, _):
        pl.semaphore_signal(barrier, inc=1, device_id=(dp, to(k)), device_id_type=MESH)
        return 0
    lax.fori_loop(1, N_SEQ, greet, 0)

    loads = {}
    def load(name, src, dst):
        cp = pltpu.make_async_copy(src, dst, load_sem.at[len(loads)])
        cp.start()
        loads[name] = cp
    load("ids", h_ids, ids)
    load("tags", h_tags, tags_all)
    load("product", t_product, product_t)
    load("branch", b_branch, branch)
    load("cot", h_cot, cot)

    phases = ((w_down, 11, 0, D), (w_up, 4, 0, FF), (w_up, 4, FF, FF), (w_output, 4, 0, D),
        (w_in, 4, 3 * D, D), (w_in, 4, 0, 2 * D), (w_in, 4, 2 * D, D))
    first = [sum(p[1] for p in phases[:k]) for k in range(len(phases))]
    def piece(phase, k):
        w, _, col, width = phases[phase]
        slot = (first[phase] + k) % 3
        row = pl.multiple_of(k * 256, 256)
        return pltpu.make_async_copy(w.at[pl.ds(row, 256), pl.ds(col, width)], wbuf.at[slot, :, pl.ds(0, width)], wsem.at[slot])
    def stream(phase, compute):
        count, width = phases[phase][1], phases[phase][3]
        def one(k, _):
            @pl.when(k + 2 < count)
            def _():
                piece(phase, k + 2).start()
            if phase + 1 < len(phases):
                @pl.when(k + 2 >= count)
                def _():
                    piece(phase + 1, k + 2 - count).start()
            piece(phase, k).wait()
            compute(k, wbuf.at[(first[phase] + k) % 3, :, pl.ds(0, width)])
            return 0
        lax.fori_loop(0, count, one, 0)
    piece(0, 0).start()
    piece(0, 1).start()
    load("up", h_up, up)
    load("resid", h_resid, resid)
    load("mixed", h_mixed, mixed)
    load("gate", h_gate, gate)
    load("qkv", h_qkv, qkv)
    load("second", t_second, lhs_a)
    load("gated", t_gated, lhs_b)
    load("carried", h_carried, carried)
    load("slopes", h_slopes, slopes)
    load("x", h_x, x)
    kept = []
    def keep(src, dst):
        cp = pltpu.make_async_copy(src, dst, out_sem.at[len(kept)])
        cp.start()
        kept.append(cp)
    loads["ids"].wait()
    loads["tags"].wait()
    for m in range(2):
        below, across = spread(ids[m:m + 1, :])
        ids_down[m] = below
        allowed[m] = jnp.where((below == across) & (row_index() >= column_index()), 1.0, 0.0)
    pl.semaphore_wait(barrier, len(close) + N_SEQ - 1)

    rs = Scatter(held, slots, final, me, send_sem, recv_sem)
    scan = Scan(local, came, going, reverse, (s1, r1, s2, r2))
    passed = []
    def hand(src, dst):
        k = len(passed)
        cp = pltpu.make_async_remote_copy(src_ref=src, dst_ref=dst, send_sem=pass_send.at[k], recv_sem=pass_recv.at[k],
            device_id=device(sib), device_id_type=MESH)
        cp.start()
        passed.append(cp)
        return cp

    loads["product"].wait()
    loads["branch"].wait()
    def down_rows(k, _):
        rows = pl.ds(pl.multiple_of(k * 352, 32), 352)
        for j in range(2):
            cols = slice(j * 256, (j + 1) * 256)
            total = dot(product_t[0, rows, :], branch[0, :, cols]) + dot(product_t[1, rows, :], branch[1, :, cols])
            for i in range(4):
                held[DOWN][k // 2, k % 2, i, j] = total[i * 88:(i + 1) * 88].astype(LOW)
        return 0
    lax.fori_loop(0, 8, down_rows, 0)
    rs.far(G_DOWN, 0)

    loads["cot"].wait()
    loads["up"].wait()
    def up_back(k, w):
        cols, more = columns_of(k, 256), pl.ds(pl.multiple_of(k * 256 + FF, 256), 256)
        d_product = dot(cot[...], w[...], ((1,), (1,)))
        d_up[:, cols] = (d_product * up[:, more].astype(F32)).astype(LOW)
        d_up[:, more] = (d_product * up[:, cols].astype(F32)).astype(LOW)
    stream(0, up_back)
    side = lambda c, width, base=0: pl.ds(pl.multiple_of(c * width + base, 128), width)
    h_wide = hand(d_up.at[:, side(other_core, FF)], up_sib)
    def second_left(k, w):
        work[:, columns_of(k, 256)] = dot(d_up[:, 0:FF], w[...], ((1,), (1,)))
    stream(1, second_left)

    def grad_half(i, lhs, own, base, shift, sibling, units):
        out = held[i].reshape(D, HELD[i][1])
        for u in units:
            _, _, lo, hi = BACK_UNITS[u]
            a = lo
            while a < hi:
                wide = min(256, hi - a)
                mine = own[:, pl.ds(pl.multiple_of(base + (a - shift), 128), wide)]
                total = dot(lhs[core], mine) + dot(lhs[other_core], sibling[:, a:a + wide])
                out[:, a:a + wide] = total.astype(LOW)
                a += wide
            rs.far((u,), 0)

    loads["second"].wait()
    h_wide.wait_recv()
    grad_half(WIDE, lhs_a, d_up, core * FF, 0, up_sib, G_WIDE)
    load("first", t_first, lhs_a)
    def second_right(k, w):
        work[:, columns_of(k, 256)] += dot(d_up[:, FF:2 * FF], w[...], ((1,), (1,)))
    stream(2, second_right)
    rs.turn(G_DOWN, 0)

    loads["resid"].wait()
    def resid_back(rows):
        v = resid[rows, :]
        factor = rms_factor(v)
        total = cot[rows, :].astype(F32) + norm_back(work[rows, :], v * factor, factor)
        resid[rows, :] = total
        d_attn[rows, :] = total.astype(LOW)
    by_rows(ROWS, 32, resid_back)
    h_attn = hand(d_attn.at[:, side(other_core, D // 2)], attn_sib)
    def gated_back(k, w):
        work[:, columns_of(k, 256)] = dot(d_attn[...], w[...], ((1,), (1,)))
    stream(3, gated_back)
    loads["mixed"].wait()
    loads["gate"].wait()
    def mixed_back(rows):
        v = mixed[rows, :]
        factor = rms_factor(v)
        normed = v * factor
        g = work[rows, :]
        d_mixed[rows, :] = norm_back(g * gate[rows, :].astype(F32), normed, factor).astype(LOW)
        gate[rows, :] = (g * normed).astype(LOW)
    by_rows(ROWS, 32, mixed_back)
    h_gate_out = hand(gate.at[:, side(other_core, D // 2)], pre_sib.at[:, pl.ds(1536, 512)])
    loads["qkv"].wait()
    def back_states(p, _):
        micro, head, rows, cols = pair_at(p)
        start = ids[pl.ds(micro, 1), 0:1]
        opening = jnp.where(ids_down[micro] == start, jnp.exp(-(row_index() + 1.0) * decays[head]), 0.0)
        opened = (qkv[rows, head_of(head, 0)].astype(F32) * opening).astype(LOW)
        local[p] = dot(opened, d_mixed[rows, cols], ((0,), (0,))).astype(LOW)
        return 0
    each_pair(back_states)
    scan.start()
    loads["gated"].wait()
    h_attn.wait_recv()
    grad_half(OUTPUT, lhs_b, d_attn, core * (D // 2), 0, attn_sib, G_OUTPUT)
    loads["first"].wait()
    h_gate_out.wait_recv()
    grad_half(INPUT, lhs_a, gate, core * (D // 2), 1536, pre_sib, G_GATE)
    rs.turn(G_WIDE, 0)
    rs.land(G_DOWN, 0)
    scan.join(tags_all, decays, True)

    h_wide.wait_send()
    loads["slopes"].wait()
    loads["carried"].wait()
    d_pre = d_up.at[:, 0:3 * D]
    def pair_back(p, _):
        micro, head, rows, cols = pair_at(p)
        q, k, v = (qkv[rows, head_of(head, part)] for part in range(3))
        dm = d_mixed[rows, cols]
        mask = allowed[micro] * jnp.exp(jnp.minimum(column_index() - row_index(), 0.0) * decays[head])
        weighted = (dot(q, k, ((1,), (1,))) * mask).astype(LOW)
        d_scores = (dot(dm, v, ((1,), (1,))) * mask).astype(LOW)
        boundary = jnp.where(seq > 0, tags_all[jnp.maximum(seq - 1, 0), pl.ds(2 * micro + 1, 1), :], -1.0)
        reaching = jnp.where(ids_down[micro] == boundary, jnp.exp(-(row_index() + 1.0) * decays[head]), 0.0)
        d_q = dot(d_scores, k) + dot(dm, carried[p], ((1,), (1,))) * reaching
        d_pre[rows, head_of(head, 0)] = (d_q * slopes[rows, head_of(head, 0)].astype(F32)).astype(LOW)
        work[rows, cols] = dot(d_scores, q, ((0,), (0,)))
        mixed[rows, cols] = dot(weighted, dm, ((0,), (0,)))
        return 0
    each_pair(pair_back)
    h_query = hand(d_pre.at[:, side(other_core, D // 2)], pre_sib.at[:, pl.ds(0, 512)])
    h_query.wait_recv()
    grad_half(INPUT, lhs_a, d_pre, core * (D // 2), 0, pre_sib, G_QUERY)
    scan.finish()
    def pair_close(p, _):
        micro, head, rows, cols = pair_at(p)
        after = jnp.where(seq < N_SEQ - 1, tags_all[jnp.minimum(seq + 1, N_SEQ - 1), pl.ds(2 * micro, 1), :], -1.0)
        closing = jnp.where(ids_down[micro] == after, jnp.exp((row_index() - (HD - 1.0)) * decays[head]), 0.0)
        d_k = work[rows, cols] + dot(qkv[rows, head_of(head, 2)], reverse[p], ((1,), (1,))) * closing
        d_v = mixed[rows, cols] + dot(qkv[rows, head_of(head, 1)], reverse[p]) * closing
        d_pre[rows, head_of(head, 1)] = (d_k * slopes[rows, head_of(head, 1)].astype(F32)).astype(LOW)
        d_pre[rows, head_of(head, 2)] = d_v.astype(LOW)
        return 0
    each_pair(pair_close)
    h_key = hand(d_pre.at[:, side(other_core, D // 2, D)], pre_sib.at[:, pl.ds(512, 512)])
    h_value = hand(d_pre.at[:, side(other_core, D // 2, 2 * D)], pre_sib.at[:, pl.ds(1024, 512)])
    rs.land(G_WIDE, 0)
    rs.land(G_DOWN, 1)
    h_key.wait_recv()
    h_value.wait_recv()
    out = held[INPUT].reshape(D, 2 * D)
    for u in G_VALUE:
        _, _, lo, hi = BACK_UNITS[u]
        a = lo
        while a < hi:
            part, within = a // 512, a % 512
            wide = min(256, hi - a, 512 - within)
            mine = d_pre[:, pl.ds(pl.multiple_of(part * D + core * 512 + within, 128), wide)]
            out[:, a:a + wide] = (dot(lhs_a[core], mine) + dot(lhs_a[other_core], pre_sib[:, a:a + wide])).astype(LOW)
            a += wide
        rs.far((u,), 0)
    rs.turn(G_OUTPUT, 0)
    rs.turn(G_GATE, 0)
    rs.turn(G_QUERY, 0)
    def first_gate(k, w):
        work[:, columns_of(k, 256)] = dot(gate[...], w[...], ((1,), (1,)))
    stream(4, first_gate)
    rs.turn(G_VALUE, 0)
    rs.land(G_OUTPUT, 0)
    rs.land(G_GATE, 0)
    rs.land(G_QUERY, 0)
    rs.land(G_WIDE, 1)
    rs.land(G_DOWN, 2)
    def first_keys(k, w):
        work[:, columns_of(k, 256)] += dot(d_pre[:, 0:2 * D], w[...], ((1,), (1,)))
    stream(5, first_keys)
    rs.land(G_VALUE, 0)
    rs.land(G_OUTPUT, 1)
    rs.land(G_GATE, 1)
    rs.land(G_QUERY, 1)
    def first_values(k, w):
        work[:, columns_of(k, 256)] += dot(d_pre[:, 2 * D:3 * D], w[...], ((1,), (1,)))
    stream(6, first_values)
    rs.land(G_VALUE, 1)
    rs.land(G_WIDE, 2)
    loads["x"].wait()
    def input_back(rows):
        v = x[rows, :].astype(F32)
        factor = rms_factor(v)
        input_grad[rows, :] = resid[rows, :] + norm_back(work[rows, :], v * factor, factor)
    by_rows(ROWS, 32, input_back)
    keep(input_grad, o_input)

    rs.land(G_OUTPUT, 2)
    place = me["x"] // 2 * 2 + core
    def owner(j):
        return (dp, me["z"] * 4 + j)
    for j in range(4):
        quarters[j, 0:22, :] = final[DOWN][j * 22:(j + 1) * 22, :]
    def quarter(k):
        j = (place + k) % 4
        return pltpu.make_async_remote_copy(src_ref=quarters.at[j], dst_ref=regroup.at[place], send_sem=q_send.at[j],
            recv_sem=q_recv.at[place], device_id=owner(j), device_id_type=MESH)
    for k in range(1, 4):
        quarter(k).start()
    regroup[place] = quarters[place]
    ends = {}
    def swap(i):
        cp = pltpu.make_async_remote_copy(src_ref=final[i].at[pl.ds(pl.multiple_of(other_core * 8, 8), 8), :], dst_ref=theirs[i - 1],
            send_sem=end_send.at[i - 1], recv_sem=end_recv.at[i - 1], device_id=device(sib), device_id_type=MESH)
        cp.start()
        ends[i] = cp
    def give(i, outs, part):
        ends[i].wait_recv()
        mine, came = final[i][pl.ds(pl.multiple_of(core * 8, 8), 8), :], theirs[i - 1][...]
        both = (jnp.where(core == 0, mine, came), jnp.where(core == 0, came, mine))
        n = part // 128
        for k, out in enumerate(outs):
            for c in range(2 * n):
                out[pl.ds(c, 8, stride=2 * n), :] = both[c // n][:, k * part + (c % n) * 128:k * part + (c % n + 1) * 128]
    swap(WIDE)
    swap(OUTPUT)
    for k in range(1, 4):
        j = (place + k) % 4
        pltpu.make_async_remote_copy(src_ref=regroup.at[j], dst_ref=regroup.at[j], send_sem=q_send.at[j],
            recv_sem=q_recv.at[j], device_id=owner((place + 1) % 4), device_id_type=MESH).wait_recv()
    for j in range(4):
        for k in range(2):
            t = (j % 2) * 4 + (j // 2) * 2 + k
            grads[7][pl.ds(t, 22, stride=8), :] = regroup[j, 0:22, k * 128:(k + 1) * 128]
    keep(grads[7], o_grads[7])
    ends[WIDE].wait_recv()
    mine, came = final[WIDE][pl.ds(pl.multiple_of(core * 8, 8), 8), :], theirs[WIDE - 1][...]
    for k, both in enumerate((jnp.where(core == 0, mine, came), jnp.where(core == 0, came, mine))):
        for c in range(22):
            grads[5 + k][pl.ds(c, 8, stride=22), :] = both[:, c * 128:(c + 1) * 128]
        keep(grads[5 + k], o_grads[5 + k])
    give(OUTPUT, grads[4:5], 512)
    keep(grads[4], o_grads[4])
    rs.land(G_GATE, 2)
    rs.land(G_QUERY, 2)
    rs.land(G_VALUE, 2)
    swap(INPUT)
    give(INPUT, grads[0:4], 512)
    for k in range(4):
        keep(grads[k], o_grads[k])
    for cp in kept:
        cp.wait()
    for cp in ends.values():
        cp.wait_send()
    for k in range(1, 4):
        quarter(k).wait_send()
    for cp in passed[1:]:
        cp.wait_send()
    scan.drain()
    rs.drain()


def backward(ids, tags_all, decays, arrays):
    anywhere = pl.BlockSpec(memory_space=pl.ANY)
    sds = jax.ShapeDtypeStruct
    vm = pltpu.VMEM
    n = len(BACK_UNITS)
    scratch = [vm((ROWS, D), F32)] + [vm((64, 128), F32)] * 5 + [vm((176, 128), F32)] * 3 + [vm((2, HD), F32), vm((N_SEQ, 8, HD), F32)]
    scratch += [vm(live_dims(()) + tail, LOW) for tail in HELD]
    for stage in range(3):
        for i, s, lo, hi in BACK_UNITS:
            tail = (hi - lo, 256) if i == DOWN else (HELD[i][0], hi - lo)
            scratch.append(vm((3,) + live_dims(BACK_ORDERS[s][:stage + 1]) + tail, LOW))
    scratch += [vm(tail, F32) for tail in HELD] + [vm((8, tail[1]), F32) for tail in HELD[1:]]
    full = lambda width, kind=LOW: vm((ROWS, width), kind)
    scratch += [vm((4, 24, 256), F32), vm((4, 24, 256), F32), vm((3, 256, FF), LOW), vm((2, FF, ROWS), LOW),
        vm((2, D, ROWS), LOW), vm((2, D, ROWS), LOW), vm((2, ROWS, D // 2), LOW), full(D), full(2 * FF), full(FF), full(D), full(D // 2),
        full(2 * D), full(2 * FF), full(3 * D), full(2 * D), full(D), full(D, F32), full(D, F32), full(D), full(D, F32), full(D)]
    scratch += [vm((N_SEQ, HD, HD), LOW)] * 5 + [vm((2, HD, HD), F32)] * 2
    scratch += [DMA((16,)), DMA((3,)), DMA((n, 3, 6)), DMA((n, 3, 6))] + [DMA((N_SEQ,))] * 4 + [DMA((6,))] * 2 + [DMA((3,))] * 2 + [DMA((4,))] * 2 + [DMA((9,))]
    return pl.pallas_call(
        backward_kernel,
        out_shape=[sds((ROWS, D), F32)] + [sds((64, 128), F32)] * 5 + [sds((176, 128), F32)] * 3,
        in_specs=[anywhere] * 2 + [pl.BlockSpec(memory_space=pltpu.SMEM)] + [anywhere] * len(arrays),
        out_specs=[anywhere] * 9,
        scratch_shapes=scratch,
        compiler_params=pltpu.CompilerParams(collective_id=1, has_side_effects=True, vmem_limit_bytes=60 << 20),
        name="backward_and_scatter",
    )(ids, tags_all, decays, *arrays)


def copy_kernel(*refs):
    n = len(refs) // 3
    sems = refs[-1]
    into = [pltpu.make_async_copy(refs[k], refs[2 * n + k], sems.at[0, k]) for k in range(n)]
    out = [pltpu.make_async_copy(refs[2 * n + k], refs[n + k], sems.at[1, k]) for k in range(n)]
    for cp in into:
        cp.start()
    for a, b in zip(into, out):
        a.wait()
        b.start()
    for cp in out:
        cp.wait()


def hand_out(arrays):
    anywhere = pl.BlockSpec(memory_space=pl.ANY)
    return pl.pallas_call(
        copy_kernel, out_shape=[jax.ShapeDtypeStruct(a.shape, a.dtype) for a in arrays],
        in_specs=[anywhere] * len(arrays), out_specs=[anywhere] * len(arrays),
        scratch_shapes=[pltpu.VMEM(a.shape, a.dtype) for a in arrays] + [DMA((2, len(arrays)))], name="hand_out",
    )(*arrays)


def on_device(hidden_in, seg_ids, decay_rates, grad_out, *weights):
    x, cot = hidden_in.reshape(ROWS, D), grad_out.reshape(ROWS, D)
    ids = seg_ids.reshape(2, HD).astype(F32)
    (act, tags_all, qkv, slopes, gate, mixed, resid, up, carried, w_in, w_output, w_up, w_down, t_first, t_gated, t_second,
     t_product, b_branch) = forward(x, cot, ids, decay_rates, [w.reshape(-1, 128) for w in weights])
    input_grad, *grads = backward(ids, tags_all, decay_rates, [
        x, cot, qkv, slopes, gate, mixed, resid, up, carried, w_in.reshape(D, 4 * D), w_output.reshape(D, D),
        w_up.reshape(D, 2 * FF), w_down, t_first, t_gated, t_second, t_product, b_branch])
    act, input_grad, *grads = hand_out([act, input_grad, *grads])
    return (act.reshape(hidden_in.shape), input_grad.reshape(hidden_in.shape), *(g.reshape(-1) for g in grads))


def solution(mesh):
    tokens = P(None, "dp", "seq", None)
    flat = P(("dp", "seq"))
    return jax.shard_map(
        on_device, mesh=mesh,
        in_specs=(tokens, P(None, "dp", "seq"), P(), tokens) + (flat,) * 8,
        out_specs=(tokens, tokens) + (flat,) * 8,
        check_vma=False,
    )
```

```python
import functools
import jax, jax.numpy as jnp
from jax import lax
from jax.experimental import pallas as pl
from jax.experimental.pallas import tpu as pltpu
from jax.sharding import PartitionSpec as P

MESH = pl.DeviceIdType.MESH
RING = 4
D = 1024
H = 8
HD = 128
FF = 2816
ROWS = 256
N_SEQ = 16
EPSILON = 1e-06
LOW = jnp.bfloat16
F32 = jnp.float32
OWNERS = (4, 2, 4, 2, 2)
DMA = pltpu.SemaphoreType.DMA
ORDERS = (("x", "y", "z"), ("y", "z", "x"), ("z", "x", "y"))
SPLIT_ROWS = (False, False, False, True)


def tiles(array, bounds, grain=128):
    return [(array, s, lo * grain, hi * grain) for s, (lo, hi) in enumerate(zip(bounds[:-1], bounds[1:]))]


CHUNKS = (
    tuple(tiles(0, (0, 11, 22, 32))),
    ((1, 2, 0, 1024),) + tuple(tiles(2, (0, 16, 32, 44))),
    tuple(tiles(3, (0, 8, 16, 22), 8)),
)
UNITS = CHUNKS[0] + CHUNKS[1] + CHUNKS[2]
C1, C2, C3 = (tuple(UNITS.index(u) for u in chunk) for chunk in CHUNKS)
C2_FIRST = C2[:1]


def where_am_i():
    dp = lax.axis_index("dp")
    seq = lax.axis_index("seq")
    return {"x": (seq // 2 % 2) * 2 + dp % 2, "y": dp // 2, "z": seq // 4, "c": seq % 2}


def device(at):
    return (at["y"] * 2 + at["x"] % 2, at["z"] * 4 + (at["x"] // 2) * 2 + at["c"])


def moved(at, axis, by):
    out = dict(at)
    out[axis] = (at[axis] + by) % RING if axis != "c" else 1 - at[axis]
    return out


def block(ref, at, whole, lo, hi, rows):
    every = slice(None)
    pick = lambda axis, value: every if axis in whole else value
    span = pl.ds(lo, hi - lo)
    return ref.at[
        pick("y", at["y"]), pick("x", at["x"] % 2), pick("z", at["z"]), pick("x", at["x"] // 2), at["c"],
        span if rows else every, every if rows else span,
    ]


def middle(lo, hi, rows):
    grain = 8 if rows else 128
    return lo + ((hi - lo) // grain // 2) * grain


def neighbours(me):
    return [moved(me, a, d) for a in "xyz" for d in (1, -1)] + [moved(me, "c", 1)]


def dot(a, b, dims=((1,), (0,))):
    return lax.dot_general(a, b, (dims, ((), ())), preferred_element_type=F32)


def by_rows(count, size, body):
    def one(k, _):
        body(pl.ds(pl.multiple_of(k * size, size), size))
        return 0
    lax.fori_loop(0, count // size, one, 0)


def columns_of(k, size):
    return pl.ds(pl.multiple_of(k * size, size), size)


def sigmoid(u):
    return 1.0 / (1.0 + jnp.exp(-u))


def rms_factor(v):
    return lax.rsqrt(jnp.mean(v * v, axis=-1, keepdims=True) + EPSILON)


class Gather:
    def __init__(self, arrays, me, send_sem, recv_sem, csend_sem, crecv_sem):
        self.arrays, self.me = arrays, me
        self.send_sem, self.recv_sem, self.csend_sem, self.crecv_sem = send_sem, recv_sem, csend_sem, crecv_sem
        self.sends = []

    def copy(self, ref, u, slot, to):
        return pltpu.make_async_remote_copy(src_ref=ref, dst_ref=ref, send_sem=self.send_sem.at[u, slot],
            recv_sem=self.recv_sem.at[u, slot], device_id=device(to), device_id_type=MESH)

    def ccopy(self, ref, u, slot):
        return pltpu.make_async_remote_copy(src_ref=ref, dst_ref=ref, send_sem=self.csend_sem.at[u, slot],
            recv_sem=self.crecv_sem.at[u, slot], device_id=device(moved(self.me, "c", 1)), device_id_type=MESH)

    def go(self, cp):
        cp.start()
        self.sends.append(cp)

    def part(self, u, at, stage, half=None):
        i, s, lo, hi = UNITS[u]
        rows = SPLIT_ROWS[i]
        mid = middle(lo, hi, rows)
        lo, hi = (lo, hi) if half is None else ((lo, mid), (mid, hi))[half]
        return block(self.arrays[i], at, ORDERS[s][:stage], lo, hi, rows)

    def axis(self, u, stage):
        return ORDERS[UNITS[u][1]][stage]

    def begin(self, units, stage):
        for u in units:
            a = self.axis(u, stage)
            if stage == 0:
                for k, by in enumerate((1, -1, 2)):
                    self.go(self.copy(self.part(u, self.me, stage), u, k, moved(self.me, a, by)))
                continue
            for k, (half, by) in enumerate(((0, 1), (1, -1), (1, 1), (0, -1))):
                self.go(self.copy(self.part(u, self.me, stage, half), u, 6 * stage + k, moved(self.me, a, by)))
            if stage == 2:
                self.go(self.ccopy(self.part(u, self.me, stage), u, 0))

    def relay(self, units, stage):
        for u in units:
            a = self.axis(u, stage)
            for half, by in ((0, 1), (1, -1)):
                first = self.part(u, moved(self.me, a, -by), stage, half)
                self.copy(first, u, 6 * stage + half, moved(self.me, a, by)).wait_recv()
                self.go(self.copy(first, u, 6 * stage + 4 + half, moved(self.me, a, by)))

    def finish(self, units, stage):
        for u in units:
            a = self.axis(u, stage)
            if stage == 0:
                for k, by in enumerate((-1, 1, 2)):
                    self.copy(self.part(u, moved(self.me, a, by), stage), u, k, moved(self.me, a, 1)).wait_recv()
                continue
            for k, by, half in ((2, -1, 1), (3, 1, 0), (4, 2, 0), (5, 2, 1)):
                self.copy(self.part(u, moved(self.me, a, by), stage, half), u, 6 * stage + k, moved(self.me, a, 1)).wait_recv()
            if stage == 2:
                for k, by in enumerate((-1, 1, 2)):
                    self.go(self.ccopy(self.part(u, moved(self.me, a, by), stage), u, 1 + k))

    def advance(self, units, stage):
        for u in units:
            self.finish((u,), stage)
            self.begin((u,), stage + 1)

    def arrive(self, units):
        sib = moved(self.me, "c", 1)
        for u in units:
            for k, by in enumerate((0, -1, 1, 2)):
                self.ccopy(self.part(u, moved(sib, self.axis(u, 2), by), 2), u, k).wait_recv()

    def drain(self):
        for cp in self.sends:
            cp.wait_send()


class Scan:
    def __init__(self, local, came, going, carried, sems):
        self.me, self.dp = lax.axis_index("seq"), lax.axis_index("dp")
        self.local, self.came, self.going, self.carried = local, came, going, carried
        self.send1, self.recv1, self.send2, self.recv2 = sems

    def to(self, k):
        return (self.me + k) % N_SEQ

    def out(self, to):
        return pltpu.make_async_remote_copy(src_ref=self.local.at[to], dst_ref=self.came.at[self.me], send_sem=self.send1.at[to],
            recv_sem=self.recv1.at[self.me], device_id=(self.dp, to), device_id_type=MESH)

    def back(self, to):
        return pltpu.make_async_remote_copy(src_ref=self.going.at[to], dst_ref=self.carried.at[self.me], send_sem=self.send2.at[to],
            recv_sem=self.recv2.at[self.me], device_id=(self.dp, to), device_id_type=MESH)

    def arrival(self, ref, ssem, rsem, frm):
        return pltpu.make_async_remote_copy(src_ref=ref.at[frm], dst_ref=ref.at[frm], send_sem=ssem.at[frm],
            recv_sem=rsem.at[frm], device_id=(self.dp, self.to(1)), device_id_type=MESH)

    def each(self, body):
        def one(k, _):
            body(self.to(k))
            return 0
        lax.fori_loop(1, N_SEQ, one, 0)

    def start(self):
        self.each(lambda to: self.out(to).start())
        self.came[self.me] = self.local[self.me]

    def join(self, tags_all, decays, backward):
        self.each(lambda frm: self.arrival(self.came, self.send1, self.recv1, frm).wait_recv())
        micro, head = self.me // H, self.me % H
        fade = jnp.exp(-float(HD) * jnp.full((1, HD), decays[head], F32))
        first = lambda b: tags_all[b, pl.ds(2 * micro, 1), :]
        last = lambda b: tags_all[b, pl.ds(2 * micro + 1, 1), :]
        acc = jnp.zeros((HD, HD), F32)
        previous = None
        for b in (range(N_SEQ - 1, -1, -1) if backward else range(N_SEQ)):
            self.going[b] = acc.astype(LOW)
            if previous is None:
                acc = self.came[b].astype(F32)
            else:
                near = (last(b) == first(previous)) if backward else (first(b) == last(previous))
                acc = self.came[b].astype(F32) + jnp.where((first(b) == last(b)) & near, fade, 0.0) * acc
            previous = b
        self.carried[self.me] = self.going[self.me]
        self.each(lambda to: self.back(to).start())

    def finish(self):
        self.each(lambda frm: self.arrival(self.carried, self.send2, self.recv2, frm).wait_recv())

    def drain(self):
        def one(to):
            self.out(to).wait_send()
            self.back(to).wait_send()
        self.each(one)


def spread(row):
    across = jnp.broadcast_to(row, (HD, HD))
    return across.T, across


def row_index():
    return lax.broadcasted_iota(jnp.int32, (HD, HD), 0).astype(F32)


def column_index():
    return lax.broadcasted_iota(jnp.int32, (HD, HD), 1).astype(F32)


def each_pair(body, together=4):
    def some(k, _):
        for i in range(together):
            body(k * together + i, 0)
        return 0
    lax.fori_loop(0, 2 * H // together, some, 0)


def pair_at(p):
    micro, head = p // H, p % H
    return micro, head, pl.ds(pl.multiple_of(micro * HD, HD), HD), pl.ds(pl.multiple_of(head * HD, HD), HD)


def transpose_into(src, dst, count):
    def one(k, _):
        at = columns_of(k, 128)
        dst[at, :] = src[:, at].T
        return 0
    lax.fori_loop(0, count // 128, one, 0)


def forward_kernel(*refs):
    (x, cot, whole_ids, decays), small = refs[:4], refs[4:12]
    (act, tags_all, o_qkv, o_slopes, o_gate, o_mixed, o_resid, o_up, o_carried, o_in, o_output, o_wide, o_down,
     t_first, t_gated, t_second, t_product, b_branch) = refs[12:30]
    (w_in, w_output, w_up, w_flat, w_down, pre, first_in, qkv, slopes, gate, mixed, resid, up, gated, second, product,
     first_t, gated_t, second_t, product_t, carried, local, came, going, spare, tag, allowed, kept_mask, ids_down,
     send_sem, recv_sem, csend_sem, crecv_sem, tag_send, tag_recv, s1, r1, s2, r2, out_sem, pass_send, pass_recv, ids) = refs[30:]
    me = where_am_i()
    sib = moved(me, "c", 1)
    seq, dp = lax.axis_index("seq"), lax.axis_index("dp")
    to = lambda k: (seq + k) % N_SEQ
    barrier = pltpu.get_barrier_semaphore()
    close = neighbours(me) + [moved(me, a, 2) for a in "xyz"]
    for other in close:
        pl.semaphore_signal(barrier, inc=1, device_id=device(other), device_id_type=MESH)

    def greet(k, _):
        pl.semaphore_signal(barrier, inc=1, device_id=(dp, to(k)), device_id_type=MESH)
        return 0
    lax.fori_loop(1, N_SEQ, greet, 0)

    here = (me["y"], me["x"] % 2, me["z"], me["x"] // 2, me["c"])
    def place(src, target, base, width):
        n = width // 128
        spare[pl.ds(0, 8 * n), :] = src[...].astype(F32)
        for c in range(n):
            target[(*here, slice(None), pl.ds(base + c * 128, 128))] = spare[pl.ds(c, 8, stride=n), :].astype(LOW)
    for k in range(4):
        place(small[k], w_in, k * D, D)
    place(small[4], w_output, 0, D)
    place(small[5], w_up, 0, FF)
    place(small[6], w_up, FF, FF)
    w_flat[here] = small[7][...]
    ids[...] = whole_ids[...].astype(F32)
    tag[...] = jnp.zeros((8, HD), F32)
    for m in range(2):
        tag[2 * m:2 * m + 1, :] = jnp.broadcast_to(ids[m:m + 1, 0:1], (1, HD))
        tag[2 * m + 1:2 * m + 2, :] = jnp.broadcast_to(ids[m:m + 1, HD - 1:HD], (1, HD))
    tags_all[seq] = tag[...]
    pl.semaphore_wait(barrier, len(close) + N_SEQ - 1)

    g = Gather((w_in, w_output, w_up, w_flat), me, send_sem, recv_sem, csend_sem, crecv_sem)
    scan = Scan(local, came, going, carried, (s1, r1, s2, r2))
    g.begin(C1, 0)
    g.begin(C2, 0)
    g.begin(C3, 0)

    kept, passed = [], []
    def keep(src, dst):
        cp = pltpu.make_async_copy(src, dst, out_sem.at[len(kept)])
        cp.start()
        kept.append(cp)
    def hand(mine, theirs, dst):
        keep(mine, dst.at[me["c"]])
        k = len(passed)
        cp = pltpu.make_async_remote_copy(src_ref=theirs, dst_ref=dst.at[me["c"]], send_sem=pass_send.at[k],
            recv_sem=pass_recv.at[k], device_id=device(sib), device_id_type=MESH)
        cp.start()
        passed.append((cp, dst))

    def tag_copy(other):
        return pltpu.make_async_remote_copy(src_ref=tag, dst_ref=tags_all.at[seq], send_sem=tag_send.at[other],
            recv_sem=tag_recv.at[seq], device_id=(dp, other), device_id_type=MESH)
    scan.each(lambda other: tag_copy(other).start())

    def norm_in(rows):
        v = x[rows, :].astype(F32)
        first_in[rows, :] = (v * rms_factor(v)).astype(LOW)
    by_rows(ROWS, 32, norm_in)
    g.advance(C1, 0)
    for m in range(2):
        down, across = spread(ids[m:m + 1, :])
        ids_down[m] = down
        allowed[m] = jnp.where((down == across) & (row_index() >= column_index()), 1.0, 0.0)
        kept_mask[m] = jnp.where(down == jnp.broadcast_to(ids[m:m + 1, HD - 1:HD], (HD, HD)), 1.0, 0.0)
    g.relay(C1, 1)
    g.advance(C2, 0)
    g.advance(C1, 1)
    g.advance(C3, 0)
    half = lambda c: cot.at[:, pl.ds(pl.multiple_of(c * 512, 512), 512)]
    hand(half(me["c"]), half(sib["c"]), b_branch)
    transpose_into(first_in, first_t, D)
    hand(first_t, first_t, t_first)
    g.relay(C2, 1)
    g.relay(C1, 2)
    g.relay(C3, 1)
    g.advance(C2, 1)
    g.finish(C1, 2)
    g.arrive(C1)
    keep(w_in, o_in)

    m_in = w_in.reshape(D, 4 * D)
    def project(k):
        cols = columns_of(k, 512)
        pre[:, cols] = dot(first_in[...], m_in[:, cols])
    def project_kv(k, _):
        project(k + 2)
        return 0
    lax.fori_loop(0, 4, project_kv, 0)
    def swish_rows(rows, k):
        u = pre[rows, k * D:(k + 1) * D]
        s = sigmoid(u)
        qkv[rows, k * D:(k + 1) * D] = (u * s).astype(LOW)
        slopes[rows, k * D:(k + 1) * D] = (s * (1.0 + u * (1.0 - s))).astype(LOW)
    def rows_kv(rows):
        swish_rows(rows, 1)
        qkv[rows, 2 * D:3 * D] = pre[rows, 2 * D:3 * D].astype(LOW)
    by_rows(ROWS, 32, rows_kv)

    def states(p, _):
        micro, head, rows, _ = pair_at(p)
        keeping = jnp.exp((row_index() - (HD - 1.0)) * decays[head]) * kept_mask[micro]
        held = (qkv[rows, head_of(head, 1)].astype(F32) * keeping).astype(LOW)
        local[p] = dot(held, qkv[rows, head_of(head, 2)], ((0,), (0,))).astype(LOW)
        return 0
    each_pair(states)
    scan.start()
    g.relay(C2, 2)
    g.advance(C3, 1)
    def project_qg(k, _):
        project(jnp.where(k < 2, k, k + 4))
        return 0
    lax.fori_loop(0, 4, project_qg, 0)
    def rows_qg(rows):
        swish_rows(rows, 0)
        gate[rows, :] = pre[rows, 3 * D:4 * D].astype(LOW)
    by_rows(ROWS, 32, rows_qg)
    keep(qkv, o_qkv)
    keep(slopes, o_slopes)
    keep(gate, o_gate)

    def within(p, _):
        micro, head, rows, cols = pair_at(p)
        mask = allowed[micro] * jnp.exp(jnp.minimum(column_index() - row_index(), 0.0) * decays[head])
        weighted = (dot(qkv[rows, head_of(head, 0)], qkv[rows, head_of(head, 1)], ((1,), (1,))) * mask).astype(LOW)
        mixed[rows, cols] = dot(weighted, qkv[rows, head_of(head, 2)])
        return 0
    each_pair(within)
    scan.each(lambda frm: pltpu.make_async_remote_copy(src_ref=tag, dst_ref=tags_all.at[frm], send_sem=tag_send.at[frm],
        recv_sem=tag_recv.at[frm], device_id=(dp, to(1)), device_id_type=MESH).wait_recv())
    scan.join(tags_all, decays, False)
    g.finish(C2, 2)
    g.relay(C3, 2)
    g.arrive(C2_FIRST)
    keep(w_output, o_output)
    scan.finish()
    keep(carried, o_carried)

    def crossing(p, _):
        micro, head, rows, cols = pair_at(p)
        boundary = jnp.where(seq > 0, tags_all[jnp.maximum(seq - 1, 0), pl.ds(2 * micro + 1, 1), :], -1.0)
        reaching = jnp.where(ids_down[micro] == boundary, jnp.exp(-(row_index() + 1.0) * decays[head]), 0.0)
        mixed[rows, cols] += dot(qkv[rows, head_of(head, 0)], carried[p]) * reaching
        return 0
    each_pair(crossing)
    keep(mixed, o_mixed)

    def gate_rows(rows):
        v = mixed[rows, :]
        gated[rows, :] = (v * rms_factor(v) * pre[rows, 3 * D:4 * D]).astype(LOW)
    by_rows(ROWS, 32, gate_rows)
    m_output = w_output.reshape(D, D)
    def output(k, _):
        cols = columns_of(k, 512)
        resid[:, cols] = x[:, cols].astype(F32) + dot(gated[...], m_output[:, cols])
        for c in range(4):
            at = columns_of(k * 4 + c, 128)
            gated_t[at, :] = gated[:, at].T
        return 0
    lax.fori_loop(0, 2, output, 0)
    keep(resid, o_resid)
    def norm_second(rows):
        v = resid[rows, :]
        second[rows, :] = (v * rms_factor(v)).astype(LOW)
    by_rows(ROWS, 32, norm_second)
    hand(gated_t, gated_t, t_gated)
    g.finish(C3, 2)
    g.arrive(C2[1:])
    keep(w_up, o_wide)
    m_up = w_up.reshape(D, 2 * FF)
    def widen(k, _):
        cols, more = columns_of(k, 256), pl.ds(pl.multiple_of(k * 256 + FF, 256), 256)
        left = dot(second[...], m_up[:, cols])
        right = dot(second[...], m_up[:, more])
        up[:, cols] = left.astype(LOW)
        up[:, more] = right.astype(LOW)
        both = (left * right).astype(LOW)
        product[:, cols] = both
        product_t[cols, :] = both.T
        return 0
    lax.fori_loop(0, 11, widen, 0)
    keep(up, o_up)
    hand(product_t, product_t, t_product)
    g.arrive(C3)
    flat = w_flat.reshape(128 * 176, 128)
    def arrange(k, _):
        spare[...] = flat[pl.ds(pl.multiple_of(k * 1408, 1408), 1408), :].astype(F32)
        for c in range(8):
            w_down[pl.ds(pl.multiple_of(k * 176, 176), 176), c * 128:(c + 1) * 128] = spare[pl.ds(c, 176, stride=8), :].astype(LOW)
        return 0
    for half_at in range(2):
        lax.fori_loop(8 * half_at, 8 * half_at + 8, arrange, 0)
        some = pl.ds(half_at * FF // 2, FF // 2)
        keep(w_down.at[some, :], o_down.at[some, :])
    def last(k, _):
        cols = columns_of(k, 512)
        act[:, cols] = (resid[:, cols] + dot(product[...], w_down[:, cols])).astype(LOW)
        for c in range(4):
            at = columns_of(k * 4 + c, 128)
            second_t[at, :] = second[:, at].T
        return 0
    lax.fori_loop(0, 2, last, 0)
    hand(second_t, second_t, t_second)
    for cp in kept:
        cp.wait()
    for k, (cp, dst) in enumerate(passed):
        cp.wait_send()
        there = dst.at[sib["c"]]
        pltpu.make_async_remote_copy(src_ref=there, dst_ref=there, send_sem=pass_send.at[k], recv_sem=pass_recv.at[k],
            device_id=device(sib), device_id_type=MESH).wait_recv()
    scan.each(lambda other: tag_copy(other).wait_send())
    scan.drain()
    g.drain()


def forward(x, cot, ids, decays, pieces):
    v = pl.BlockSpec(memory_space=pltpu.VMEM)
    anywhere = pl.BlockSpec(memory_space=pl.ANY)
    sds = jax.ShapeDtypeStruct
    n = len(UNITS)
    outs = [sds((ROWS, D), LOW), sds((N_SEQ, 8, HD), F32), sds((ROWS, 3 * D), LOW), sds((ROWS, 2 * D), LOW), sds((ROWS, D), LOW),
        sds((ROWS, D), F32), sds((ROWS, D), F32), sds((ROWS, 2 * FF), LOW), sds((N_SEQ, HD, HD), LOW),
        sds(OWNERS + (8, 4 * D), LOW), sds(OWNERS + (8, D), LOW), sds(OWNERS + (8, 2 * FF), LOW), sds((FF, D), LOW),
        sds((2, D, ROWS), LOW), sds((2, D, ROWS), LOW), sds((2, D, ROWS), LOW), sds((2, FF, ROWS), LOW), sds((2, ROWS, D // 2), LOW)]
    vm = pltpu.VMEM
    scratch = [vm(OWNERS + (8, 4 * D), LOW), vm(OWNERS + (8, D), LOW), vm(OWNERS + (8, 2 * FF), LOW), vm(OWNERS + (176, 128), LOW),
        vm((FF, D), LOW), vm((ROWS, 4 * D), F32), vm((ROWS, D), LOW), vm((ROWS, 3 * D), LOW), vm((ROWS, 2 * D), LOW), vm((ROWS, D), LOW),
        vm((ROWS, D), F32), vm((ROWS, D), F32), vm((ROWS, 2 * FF), LOW), vm((ROWS, D), LOW), vm((ROWS, D), LOW), vm((ROWS, FF), LOW),
        vm((D, ROWS), LOW), vm((D, ROWS), LOW), vm((D, ROWS), LOW), vm((FF, ROWS), LOW)] + [vm((N_SEQ, HD, HD), LOW)] * 4 + [
        vm((1408, 128), F32), vm((8, HD), F32)] + [vm((2, HD, HD), F32)] * 3 + [
        DMA((n, 18)), DMA((n, 18)), DMA((n, 4)), DMA((n, 4))] + [DMA((N_SEQ,))] * 6 + [DMA((20,)), DMA((5,)), DMA((5,)), vm((2, HD), F32)]
    return pl.pallas_call(
        forward_kernel, out_shape=outs,
        in_specs=[v, v, v, pl.BlockSpec(memory_space=pltpu.SMEM)] + [v] * 8,
        out_specs=[v] * 2 + [anywhere] * 16,
        scratch_shapes=scratch,
        compiler_params=pltpu.CompilerParams(collective_id=0, has_side_effects=True, vmem_limit_bytes=60 << 20),
        name="gather_and_forward",
    )(x, cot, ids, decays, *pieces)


def head_of(head, part):
    return pl.ds(pl.multiple_of(part * D + head * HD, HD), HD)


DOWN, WIDE, OUTPUT, INPUT = range(4)
HELD = ((88, 256), (16, FF), (16, D // 2), (16, 2 * D))
GROUPS = (
    tiles(DOWN, (0, 3, 7, 11), 8),
    tiles(WIDE, (0, 7, 14, 22)),
    [(OUTPUT, 0, 0, 512)],
    [(INPUT, 1, 1536, 2048)],
    [(INPUT, 2, 0, 512)],
    [(INPUT, 0, 512, 896), (INPUT, 1, 896, 1280), (INPUT, 2, 1280, 1536)],
)
BACK_UNITS = tuple(unit for group in GROUPS for unit in group)
G_DOWN, G_WIDE, G_OUTPUT, G_GATE, G_QUERY, G_VALUE = (tuple(BACK_UNITS.index(unit) for unit in group) for group in GROUPS)
BACK_ORDERS = tuple(order[::-1] for order in ORDERS)
DIMS = (("y", 4), ("x", 2), ("z", 4), ("x", 2))


def live_dims(fixed):
    return tuple(n for a, n in DIMS if a not in fixed)


def part_of(ref, at, fixed, gone, lo, hi, rows, lead=()):
    every = slice(None)
    idx = []
    for k, (a, n) in enumerate(DIMS):
        if a in gone:
            continue
        if a in fixed:
            idx.append((at["x"] % 2 if k == 1 else at["x"] // 2) if a == "x" else at[a])
        else:
            idx.append(every)
    span = pl.ds(lo, hi - lo)
    return ref.at[(*lead, *idx, span if rows else every, every if rows else span)]


def accumulate(dst, srcs, dims, out=None):
    target = dst if out is None else out
    rows, width = dst.shape[-2:]
    most = max(1, 64 // max(1, rows * width // 1024))
    cut, inner = len(dims), 1
    while cut > 0 and inner * dims[cut - 1] <= most:
        cut -= 1
        inner *= dims[cut]
    near = [()]
    for d in dims[cut:]:
        near = [at + (i,) for at in near for i in range(d)]
    def group(lead):
        places = [lead + at if dims else ... for at in near]
        totals = []
        for at in places:
            total = dst[at].astype(F32)
            for s in srcs:
                total = total + s[at].astype(F32)
            totals.append(total.astype(target.dtype))
        for at, total in zip(places, totals):
            target[at] = total
    count = 1
    for d in dims[:cut]:
        count *= d
    def one(k, _):
        idx, rest = [], k
        for m, d in enumerate(dims[:cut][::-1]):
            last = m == cut - 1
            idx.append(rest if last else rest % d)
            rest = rest if last else rest // d
        group(tuple(idx[::-1]))
        return 0
    if count == 1:
        group((0,) * cut)
    else:
        lax.fori_loop(0, count, one, 0)


class Scatter:
    def __init__(self, held, slots, final, me, send_sem, recv_sem):
        self.held, self.slots, self.final, self.me = held, slots, final, me
        self.send_sem, self.recv_sem = send_sem, recv_sem
        self.sends = []

    def spans(self, u):
        i, s, lo, hi = BACK_UNITS[u]
        return self.held[i], BACK_ORDERS[s], i == DOWN, lo, middle(lo, hi, i == DOWN), hi

    def slot(self, u, stage, k, lo, hi):
        _, order, rows, base, _, _ = self.spans(u)
        return part_of(self.slots[stage][u], self.me, (), order[:stage + 1], lo - base, hi - base, rows, (k,))

    def send(self, src, dst, u, stage, k, to):
        cp = pltpu.make_async_remote_copy(src_ref=src, dst_ref=dst, send_sem=self.send_sem.at[u, stage, k],
            recv_sem=self.recv_sem.at[u, stage, k], device_id=device(to), device_id_type=MESH)
        cp.start()
        self.sends.append(cp)

    def got(self, ref, u, stage, k):
        pltpu.make_async_remote_copy(src_ref=ref, dst_ref=ref, send_sem=self.send_sem.at[u, stage, k],
            recv_sem=self.recv_sem.at[u, stage, k], device_id=device(moved(self.me, "c", 1)), device_id_type=MESH).wait_recv()

    def far(self, units, stage):
        for u in units:
            held, order, rows, lo, mid, hi = self.spans(u)
            axis, fixed = order[stage], order[:stage + 1]
            above, below, across = (moved(self.me, axis, by) for by in (1, -1, 2))
            mine = lambda at, a, b: part_of(held, at, fixed, (), a, b, rows)
            if stage > 0:
                for k, at in enumerate((across, above, below)):
                    self.send(mine(at, lo, hi), self.slot(u, stage, k, lo, hi), u, stage, k, at)
                continue
            self.send(mine(across, lo, mid), self.slot(u, stage, 0, lo, mid), u, stage, 0, above)
            self.send(mine(across, mid, hi), self.slot(u, stage, 0, mid, hi), u, stage, 1, below)
            self.send(mine(above, mid, hi), self.slot(u, stage, 1, mid, hi), u, stage, 2, above)
            self.send(mine(below, lo, mid), self.slot(u, stage, 2, lo, mid), u, stage, 3, below)

    def turn(self, units, stage):
        for u in units:
            held, order, rows, lo, mid, hi = self.spans(u)
            fixed = order[:stage + 1]
            for k, (by, a, b) in enumerate(((1, lo, mid), (-1, mid, hi))):
                to = moved(self.me, order[stage], by)
                came = self.slot(u, stage, 0, a, b)
                self.got(came, u, stage, k)
                sums = part_of(held, to, fixed, (), a, b, rows)
                accumulate(sums, [came], live_dims(fixed))
                self.send(sums, self.slot(u, stage, 1 + k, a, b), u, stage, 4 + k, to)

    def land(self, units, stage):
        for u in units:
            held, order, rows, lo, mid, hi = self.spans(u)
            fixed = order[:stage + 1]
            mine = part_of(held, self.me, fixed, (), lo, hi, rows)
            if stage > 0:
                came = [self.slot(u, stage, k, lo, hi) for k in range(3)]
                for k in range(3):
                    self.got(came[k], u, stage, k)
                span = pl.ds(lo, hi - lo)
                if stage == 2:
                    accumulate(mine, came, (), self.final[BACK_UNITS[u][0]].at[(span, slice(None)) if rows else (slice(None), span)])
                else:
                    accumulate(mine, came, live_dims(fixed))
                    self.far((u,), 2)
                continue
            for k, (a, b) in ((2, (mid, hi)), (3, (lo, mid)), (4, (lo, mid)), (5, (mid, hi))):
                self.got(self.slot(u, stage, 1 + k % 2, a, b), u, stage, k)
            accumulate(mine, [self.slot(u, stage, 1 + k, lo, hi) for k in range(2)], live_dims(fixed))
            self.far((u,), stage + 1)

    def drain(self):
        for cp in self.sends:
            cp.wait_send()


def norm_back(upstream, normed, factor):
    return factor * (upstream - normed * jnp.mean(upstream * normed, axis=-1, keepdims=True))


def backward_kernel(*refs):
    (whole_ids, h_tags, decays, h_x, h_cot, h_qkv, h_slopes, h_gate, h_mixed, h_resid, h_up, h_carried, w_in, w_output, w_up, w_down,
     t_first, t_gated, t_second, t_product, b_branch) = refs[:21]
    o_input, o_grads = refs[21], refs[22:30]
    refs = refs[30:]
    input_grad, grads, ids, tags_all, refs = refs[0], refs[1:9], refs[9], refs[10], refs[11:]
    n = len(BACK_UNITS)
    held, refs = refs[:4], refs[4:]
    slots = [refs[k * n:(k + 1) * n] for k in range(3)]
    refs = refs[3 * n:]
    final, theirs, refs = refs[:4], refs[4:7], refs[7:]
    (quarters, regroup, wbuf, product_t, lhs_a, lhs_b, branch, cot, d_up, up_sib, d_attn, attn_sib, pre_sib,
     up, qkv, slopes, gate, mixed, resid, x, work, d_mixed, carried, local, came, going, reverse, ids_down, allowed,
     load_sem, wsem, send_sem, recv_sem, s1, r1, s2, r2, pass_send, pass_recv, end_send, end_recv, q_send, q_recv, out_sem) = refs
    me = where_am_i()
    sib = moved(me, "c", 1)
    core, other_core = me["c"], sib["c"]
    seq, dp = lax.axis_index("seq"), lax.axis_index("dp")
    to = lambda k: (seq + k) % N_SEQ
    barrier = pltpu.get_barrier_semaphore()
    close = neighbours(me) + [moved(me, a, 2) for a in "xyz"]
    for other in close:
        pl.semaphore_signal(barrier, inc=1, device_id=device(other), device_id_type=MESH)

    def greet(k, _):
        pl.semaphore_signal(barrier, inc=1, device_id=(dp, to(k)), device_id_type=MESH)
        return 0
    lax.fori_loop(1, N_SEQ, greet, 0)

    loads = {}
    def load(name, src, dst):
        cp = pltpu.make_async_copy(src, dst, load_sem.at[len(loads)])
        cp.start()
        loads[name] = cp
    ids[...] = whole_ids[...].astype(F32)
    load("tags", h_tags, tags_all)
    load("product", t_product, product_t)
    load("branch", b_branch, branch)
    load("cot", h_cot, cot)

    phases = ((w_down, 11, 0, D), (w_up, 4, 0, FF), (w_up, 4, FF, FF), (w_output, 4, 0, D),
        (w_in, 4, 3 * D, D), (w_in, 4, 0, 2 * D), (w_in, 4, 2 * D, D))
    first = [sum(p[1] for p in phases[:k]) for k in range(len(phases))]
    def piece(phase, k):
        w, _, col, width = phases[phase]
        slot = (first[phase] + k) % 3
        row = pl.multiple_of(k * 256, 256)
        return pltpu.make_async_copy(w.at[pl.ds(row, 256), pl.ds(col, width)], wbuf.at[slot, :, pl.ds(0, width)], wsem.at[slot])
    def stream(phase, compute):
        count, width = phases[phase][1], phases[phase][3]
        def one(k, _):
            @pl.when(k + 2 < count)
            def _():
                piece(phase, k + 2).start()
            if phase + 1 < len(phases):
                @pl.when(k + 2 >= count)
                def _():
                    piece(phase + 1, k + 2 - count).start()
            piece(phase, k).wait()
            compute(k, wbuf.at[(first[phase] + k) % 3, :, pl.ds(0, width)])
            return 0
        lax.fori_loop(0, count, one, 0)
    piece(0, 0).start()
    piece(0, 1).start()
    load("up", h_up, up)
    kept = []
    def keep(src, dst):
        cp = pltpu.make_async_copy(src, dst, out_sem.at[len(kept)])
        cp.start()
        kept.append(cp)
    loads["tags"].wait()
    for m in range(2):
        below, across = spread(ids[m:m + 1, :])
        ids_down[m] = below
        allowed[m] = jnp.where((below == across) & (row_index() >= column_index()), 1.0, 0.0)
    rs = Scatter(held, slots, final, me, send_sem, recv_sem)
    scan = Scan(local, came, going, reverse, (s1, r1, s2, r2))
    passed = []
    def hand(src, dst):
        k = len(passed)
        cp = pltpu.make_async_remote_copy(src_ref=src, dst_ref=dst, send_sem=pass_send.at[k], recv_sem=pass_recv.at[k],
            device_id=device(sib), device_id_type=MESH)
        cp.start()
        passed.append(cp)
        return cp

    loads["product"].wait()
    loads["branch"].wait()
    def down_rows(k, _):
        rows = pl.ds(pl.multiple_of(k * 352, 32), 352)
        for j in range(2):
            cols = slice(j * 256, (j + 1) * 256)
            total = dot(product_t[0, rows, :], branch[0, :, cols]) + dot(product_t[1, rows, :], branch[1, :, cols])
            for i in range(4):
                held[DOWN][k // 2, k % 2, i, j] = total[i * 88:(i + 1) * 88].astype(LOW)
        return 0
    lax.fori_loop(0, 8, down_rows, 0)
    pl.semaphore_wait(barrier, len(close) + N_SEQ - 1)
    rs.far(G_DOWN, 0)
    load("second", t_second, lhs_a)

    loads["cot"].wait()
    loads["up"].wait()
    def up_back(k, w):
        cols, more = columns_of(k, 256), pl.ds(pl.multiple_of(k * 256 + FF, 256), 256)
        d_product = dot(cot[...], w[...], ((1,), (1,)))
        d_up[:, cols] = (d_product * up[:, more].astype(F32)).astype(LOW)
        d_up[:, more] = (d_product * up[:, cols].astype(F32)).astype(LOW)
    stream(0, up_back)
    side = lambda c, width, base=0: pl.ds(pl.multiple_of(c * width + base, 128), width)
    h_wide = hand(d_up.at[:, side(other_core, FF)], up_sib)
    load("resid", h_resid, resid)
    load("mixed", h_mixed, mixed)
    load("gate", h_gate, gate)
    load("qkv", h_qkv, qkv)
    load("gated", t_gated, lhs_b)
    load("carried", h_carried, carried)
    load("slopes", h_slopes, slopes)
    load("x", h_x, x)
    def grad_half(i, lhs, own, base, shift, sibling, units):
        out = held[i].reshape(D, HELD[i][1])
        for u in units:
            _, _, lo, hi = BACK_UNITS[u]
            a = lo
            while a < hi:
                wide = min(256, hi - a)
                mine = own[:, pl.ds(pl.multiple_of(base + (a - shift), 128), wide)]
                total = dot(lhs[core], mine) + dot(lhs[other_core], sibling[:, a:a + wide])
                out[:, a:a + wide] = total.astype(LOW)
                a += wide
            rs.far((u,), 0)

    loads["second"].wait()
    h_wide.wait_recv()
    grad_half(WIDE, lhs_a, d_up, core * FF, 0, up_sib, G_WIDE)
    load("first", t_first, lhs_a)
    def second_left(k, w):
        work[:, columns_of(k, 256)] = dot(d_up[:, 0:FF], w[...], ((1,), (1,)))
    stream(1, second_left)
    def second_right(k, w):
        work[:, columns_of(k, 256)] += dot(d_up[:, FF:2 * FF], w[...], ((1,), (1,)))
    stream(2, second_right)
    rs.turn(G_DOWN, 0)

    loads["resid"].wait()
    def resid_back(rows):
        v = resid[rows, :]
        factor = rms_factor(v)
        total = cot[rows, :].astype(F32) + norm_back(work[rows, :], v * factor, factor)
        resid[rows, :] = total
        d_attn[rows, :] = total.astype(LOW)
    by_rows(ROWS, 32, resid_back)
    h_attn = hand(d_attn.at[:, side(other_core, D // 2)], attn_sib)
    def gated_back(k, w):
        work[:, columns_of(k, 256)] = dot(d_attn[...], w[...], ((1,), (1,)))
    stream(3, gated_back)
    loads["mixed"].wait()
    loads["gate"].wait()
    def mixed_back(rows):
        v = mixed[rows, :]
        factor = rms_factor(v)
        normed = v * factor
        g = work[rows, :]
        d_mixed[rows, :] = norm_back(g * gate[rows, :].astype(F32), normed, factor).astype(LOW)
        gate[rows, :] = (g * normed).astype(LOW)
    by_rows(ROWS, 32, mixed_back)
    h_gate_out = hand(gate.at[:, side(other_core, D // 2)], pre_sib.at[:, pl.ds(1536, 512)])
    loads["qkv"].wait()
    def back_states(p, _):
        micro, head, rows, cols = pair_at(p)
        start = ids[pl.ds(micro, 1), 0:1]
        opening = jnp.where(ids_down[micro] == start, jnp.exp(-(row_index() + 1.0) * decays[head]), 0.0)
        opened = (qkv[rows, head_of(head, 0)].astype(F32) * opening).astype(LOW)
        local[p] = dot(opened, d_mixed[rows, cols], ((0,), (0,))).astype(LOW)
        return 0
    each_pair(back_states)
    scan.start()
    loads["gated"].wait()
    h_attn.wait_recv()
    grad_half(OUTPUT, lhs_b, d_attn, core * (D // 2), 0, attn_sib, G_OUTPUT)
    loads["first"].wait()
    h_gate_out.wait_recv()
    grad_half(INPUT, lhs_a, gate, core * (D // 2), 1536, pre_sib, G_GATE)
    rs.turn(G_WIDE, 0)
    rs.land(G_DOWN, 0)
    scan.join(tags_all, decays, True)

    h_wide.wait_send()
    loads["slopes"].wait()
    loads["carried"].wait()
    d_pre = d_up.at[:, 0:3 * D]
    def pair_back(p, _):
        micro, head, rows, cols = pair_at(p)
        q, k, v = (qkv[rows, head_of(head, part)] for part in range(3))
        dm = d_mixed[rows, cols]
        mask = allowed[micro] * jnp.exp(jnp.minimum(column_index() - row_index(), 0.0) * decays[head])
        weighted = (dot(q, k, ((1,), (1,))) * mask).astype(LOW)
        d_scores = (dot(dm, v, ((1,), (1,))) * mask).astype(LOW)
        boundary = jnp.where(seq > 0, tags_all[jnp.maximum(seq - 1, 0), pl.ds(2 * micro + 1, 1), :], -1.0)
        reaching = jnp.where(ids_down[micro] == boundary, jnp.exp(-(row_index() + 1.0) * decays[head]), 0.0)
        d_q = dot(d_scores, k) + dot(dm, carried[p], ((1,), (1,))) * reaching
        d_pre[rows, head_of(head, 0)] = (d_q * slopes[rows, head_of(head, 0)].astype(F32)).astype(LOW)
        work[rows, cols] = dot(d_scores, q, ((0,), (0,)))
        mixed[rows, cols] = dot(weighted, dm, ((0,), (0,)))
        return 0
    each_pair(pair_back)
    h_query = hand(d_pre.at[:, side(other_core, D // 2)], pre_sib.at[:, pl.ds(0, 512)])
    h_query.wait_recv()
    grad_half(INPUT, lhs_a, d_pre, core * (D // 2), 0, pre_sib, G_QUERY)
    scan.finish()
    def pair_close(p, _):
        micro, head, rows, cols = pair_at(p)
        after = jnp.where(seq < N_SEQ - 1, tags_all[jnp.minimum(seq + 1, N_SEQ - 1), pl.ds(2 * micro, 1), :], -1.0)
        closing = jnp.where(ids_down[micro] == after, jnp.exp((row_index() - (HD - 1.0)) * decays[head]), 0.0)
        d_k = work[rows, cols] + dot(qkv[rows, head_of(head, 2)], reverse[p], ((1,), (1,))) * closing
        d_v = mixed[rows, cols] + dot(qkv[rows, head_of(head, 1)], reverse[p]) * closing
        d_pre[rows, head_of(head, 1)] = (d_k * slopes[rows, head_of(head, 1)].astype(F32)).astype(LOW)
        d_pre[rows, head_of(head, 2)] = d_v.astype(LOW)
        return 0
    each_pair(pair_close)
    h_key = hand(d_pre.at[:, side(other_core, D // 2, D)], pre_sib.at[:, pl.ds(512, 512)])
    h_value = hand(d_pre.at[:, side(other_core, D // 2, 2 * D)], pre_sib.at[:, pl.ds(1024, 512)])
    rs.land(G_WIDE, 0)
    rs.land(G_DOWN, 1)
    h_key.wait_recv()
    h_value.wait_recv()
    out = held[INPUT].reshape(D, 2 * D)
    for u in G_VALUE:
        _, _, lo, hi = BACK_UNITS[u]
        a = lo
        while a < hi:
            part, within = a // 512, a % 512
            wide = min(256, hi - a, 512 - within)
            mine = d_pre[:, pl.ds(pl.multiple_of(part * D + core * 512 + within, 128), wide)]
            out[:, a:a + wide] = (dot(lhs_a[core], mine) + dot(lhs_a[other_core], pre_sib[:, a:a + wide])).astype(LOW)
            a += wide
        rs.far((u,), 0)
    rs.turn(G_OUTPUT, 0)
    rs.turn(G_GATE, 0)
    rs.turn(G_QUERY, 0)
    def first_gate(k, w):
        work[:, columns_of(k, 256)] = dot(gate[...], w[...], ((1,), (1,)))
    stream(4, first_gate)
    rs.turn(G_VALUE, 0)
    rs.land(G_OUTPUT, 0)
    rs.land(G_GATE, 0)
    rs.land(G_QUERY, 0)
    rs.land(G_WIDE, 1)
    rs.land(G_DOWN, 2)
    def first_keys(k, w):
        work[:, columns_of(k, 256)] += dot(d_pre[:, 0:2 * D], w[...], ((1,), (1,)))
    stream(5, first_keys)
    rs.land(G_VALUE, 0)
    rs.land(G_OUTPUT, 1)
    rs.land(G_GATE, 1)
    rs.land(G_QUERY, 1)
    def first_values(k, w):
        work[:, columns_of(k, 256)] += dot(d_pre[:, 2 * D:3 * D], w[...], ((1,), (1,)))
    stream(6, first_values)
    rs.land(G_VALUE, 1)
    rs.land(G_WIDE, 2)
    loads["x"].wait()
    def input_back(rows):
        v = x[rows, :].astype(F32)
        factor = rms_factor(v)
        input_grad[rows, :] = resid[rows, :] + norm_back(work[rows, :], v * factor, factor)
    by_rows(ROWS, 32, input_back)
    keep(input_grad, o_input)

    rs.land(G_OUTPUT, 2)
    place = me["x"] // 2 * 2 + core
    def owner(j):
        return (dp, me["z"] * 4 + j)
    for j in range(4):
        quarters[j, 0:22, :] = final[DOWN][j * 22:(j + 1) * 22, :]
    def quarter(k):
        j = (place + k) % 4
        return pltpu.make_async_remote_copy(src_ref=quarters.at[j], dst_ref=regroup.at[place], send_sem=q_send.at[j],
            recv_sem=q_recv.at[place], device_id=owner(j), device_id_type=MESH)
    for k in range(1, 4):
        quarter(k).start()
    regroup[place] = quarters[place]
    ends = {}
    def swap(i):
        cp = pltpu.make_async_remote_copy(src_ref=final[i].at[pl.ds(pl.multiple_of(other_core * 8, 8), 8), :], dst_ref=theirs[i - 1],
            send_sem=end_send.at[i - 1], recv_sem=end_recv.at[i - 1], device_id=device(sib), device_id_type=MESH)
        cp.start()
        ends[i] = cp
    def give(i, outs, part):
        ends[i].wait_recv()
        mine, came = final[i][pl.ds(pl.multiple_of(core * 8, 8), 8), :], theirs[i - 1][...]
        both = (jnp.where(core == 0, mine, came), jnp.where(core == 0, came, mine))
        n = part // 128
        for k, out in enumerate(outs):
            for c in range(2 * n):
                out[pl.ds(c, 8, stride=2 * n), :] = both[c // n][:, k * part + (c % n) * 128:k * part + (c % n + 1) * 128]
    swap(WIDE)
    swap(OUTPUT)
    for k in range(1, 4):
        j = (place + k) % 4
        pltpu.make_async_remote_copy(src_ref=regroup.at[j], dst_ref=regroup.at[j], send_sem=q_send.at[j],
            recv_sem=q_recv.at[j], device_id=owner((place + 1) % 4), device_id_type=MESH).wait_recv()
    for j in range(4):
        for k in range(2):
            t = (j % 2) * 4 + (j // 2) * 2 + k
            grads[7][pl.ds(t, 22, stride=8), :] = regroup[j, 0:22, k * 128:(k + 1) * 128]
    keep(grads[7], o_grads[7])
    ends[WIDE].wait_recv()
    mine, came = final[WIDE][pl.ds(pl.multiple_of(core * 8, 8), 8), :], theirs[WIDE - 1][...]
    for k, both in enumerate((jnp.where(core == 0, mine, came), jnp.where(core == 0, came, mine))):
        for c in range(22):
            grads[5 + k][pl.ds(c, 8, stride=22), :] = both[:, c * 128:(c + 1) * 128]
        keep(grads[5 + k], o_grads[5 + k])
    give(OUTPUT, grads[4:5], 512)
    keep(grads[4], o_grads[4])
    rs.land(G_GATE, 2)
    rs.land(G_QUERY, 2)
    rs.land(G_VALUE, 2)
    swap(INPUT)
    give(INPUT, grads[0:4], 512)
    for k in range(4):
        keep(grads[k], o_grads[k])
    for cp in kept:
        cp.wait()
    for cp in ends.values():
        cp.wait_send()
    for k in range(1, 4):
        quarter(k).wait_send()
    for cp in passed[1:]:
        cp.wait_send()
    scan.drain()
    rs.drain()


def backward(ids, tags_all, decays, arrays):
    anywhere = pl.BlockSpec(memory_space=pl.ANY)
    sds = jax.ShapeDtypeStruct
    vm = pltpu.VMEM
    n = len(BACK_UNITS)
    scratch = [vm((ROWS, D), F32)] + [vm((64, 128), F32)] * 5 + [vm((176, 128), F32)] * 3 + [vm((2, HD), F32), vm((N_SEQ, 8, HD), F32)]
    scratch += [vm(live_dims(()) + tail, LOW) for tail in HELD]
    for stage in range(3):
        for i, s, lo, hi in BACK_UNITS:
            tail = (hi - lo, 256) if i == DOWN else (HELD[i][0], hi - lo)
            scratch.append(vm((3,) + live_dims(BACK_ORDERS[s][:stage + 1]) + tail, LOW))
    scratch += [vm(tail, F32) for tail in HELD] + [vm((8, tail[1]), F32) for tail in HELD[1:]]
    full = lambda width, kind=LOW: vm((ROWS, width), kind)
    scratch += [vm((4, 24, 256), F32), vm((4, 24, 256), F32), vm((3, 256, FF), LOW), vm((2, FF, ROWS), LOW),
        vm((2, D, ROWS), LOW), vm((2, D, ROWS), LOW), vm((2, ROWS, D // 2), LOW), full(D), full(2 * FF), full(FF), full(D), full(D // 2),
        full(2 * D), full(2 * FF), full(3 * D), full(2 * D), full(D), full(D, F32), full(D, F32), full(D), full(D, F32), full(D)]
    scratch += [vm((N_SEQ, HD, HD), LOW)] * 5 + [vm((2, HD, HD), F32)] * 2
    scratch += [DMA((16,)), DMA((3,)), DMA((n, 3, 6)), DMA((n, 3, 6))] + [DMA((N_SEQ,))] * 4 + [DMA((6,))] * 2 + [DMA((3,))] * 2 + [DMA((4,))] * 2 + [DMA((9,))]
    return pl.pallas_call(
        backward_kernel,
        out_shape=[sds((ROWS, D), F32)] + [sds((64, 128), F32)] * 5 + [sds((176, 128), F32)] * 3,
        in_specs=[pl.BlockSpec(memory_space=pltpu.VMEM), anywhere, pl.BlockSpec(memory_space=pltpu.SMEM)] + [anywhere] * len(arrays),
        out_specs=[anywhere] * 9,
        scratch_shapes=scratch,
        compiler_params=pltpu.CompilerParams(collective_id=1, has_side_effects=True, vmem_limit_bytes=60 << 20),
        name="backward_and_scatter",
    )(ids, tags_all, decays, *arrays)


def copy_kernel(*refs):
    n = len(refs) // 3
    sems = refs[-1]
    steps = []
    for k in range(n):
        src, dst, via = refs[k], refs[n + k], refs[2 * n + k]
        pieces = [pl.ds(r, 64) for r in range(0, src.shape[0], 64)] if src.shape[0] == ROWS else [slice(None)]
        for piece in pieces:
            at = len(steps)
            steps.append((pltpu.make_async_copy(src.at[piece], via.at[piece], sems.at[0, at]),
                pltpu.make_async_copy(via.at[piece], dst.at[piece], sems.at[1, at])))
    for into, _ in steps:
        into.start()
    for into, out in steps:
        into.wait()
        out.start()
    for _, out in steps:
        out.wait()


def hand_out(arrays):
    anywhere = pl.BlockSpec(memory_space=pl.ANY)
    return pl.pallas_call(
        copy_kernel, out_shape=[jax.ShapeDtypeStruct(a.shape, a.dtype) for a in arrays],
        in_specs=[anywhere] * len(arrays), out_specs=[anywhere] * len(arrays),
        scratch_shapes=[pltpu.VMEM(a.shape, a.dtype) for a in arrays] + [DMA((2, 16))], name="hand_out",
    )(*arrays)


def on_device(hidden_in, seg_ids, decay_rates, grad_out, *weights):
    x, cot = hidden_in.reshape(ROWS, D), grad_out.reshape(ROWS, D)
    ids = seg_ids.reshape(2, HD)
    (act, tags_all, qkv, slopes, gate, mixed, resid, up, carried, w_in, w_output, w_up, w_down, t_first, t_gated, t_second,
     t_product, b_branch) = forward(x, cot, ids, decay_rates, [w.reshape(-1, 128) for w in weights])
    input_grad, *grads = backward(ids, tags_all, decay_rates, [
        x, cot, qkv, slopes, gate, mixed, resid, up, carried, w_in.reshape(D, 4 * D), w_output.reshape(D, D),
        w_up.reshape(D, 2 * FF), w_down, t_first, t_gated, t_second, t_product, b_branch])
    act, input_grad, *grads = hand_out([act, input_grad, *grads])
    return (act.reshape(hidden_in.shape), input_grad.reshape(hidden_in.shape), *(g.reshape(-1) for g in grads))


def solution(mesh):
    tokens = P(None, "dp", "seq", None)
    flat = P(("dp", "seq"))
    return jax.shard_map(
        on_device, mesh=mesh,
        in_specs=(tokens, P(None, "dp", "seq"), P(), tokens) + (flat,) * 8,
        out_specs=(tokens, tokens) + (flat,) * 8,
        check_vma=False,
    )
```

```python
import functools
import jax, jax.numpy as jnp
from jax import lax
from jax.experimental import pallas as pl
from jax.experimental.pallas import tpu as pltpu
from jax.sharding import PartitionSpec as P

MESH = pl.DeviceIdType.MESH
RING = 4
D = 1024
H = 8
HD = 128
FF = 2816
ROWS = 256
N_SEQ = 16
EPSILON = 1e-06
LOW = jnp.bfloat16
F32 = jnp.float32
OWNERS = (4, 2, 4, 2, 2)
DMA = pltpu.SemaphoreType.DMA
ORDERS = (("x", "y", "z"), ("y", "z", "x"), ("z", "x", "y"))
SPLIT_ROWS = (False, False, False, True)


def tiles(array, bounds, grain=128):
    return [(array, s, lo * grain, hi * grain) for s, (lo, hi) in enumerate(zip(bounds[:-1], bounds[1:]))]


CHUNKS = (
    tuple(tiles(0, (0, 11, 22, 32))),
    ((1, 2, 0, 1024),) + tuple(tiles(2, (0, 16, 32, 44))),
    tuple(tiles(3, (0, 8, 16, 22), 8)),
)
UNITS = CHUNKS[0] + CHUNKS[1] + CHUNKS[2]
C1, C2, C3 = (tuple(UNITS.index(u) for u in chunk) for chunk in CHUNKS)
C2_FIRST = C2[:1]


def where_am_i():
    dp = lax.axis_index("dp")
    seq = lax.axis_index("seq")
    return {"x": (seq // 2 % 2) * 2 + dp % 2, "y": dp // 2, "z": seq // 4, "c": seq % 2}


def device(at):
    return (at["y"] * 2 + at["x"] % 2, at["z"] * 4 + (at["x"] // 2) * 2 + at["c"])


def moved(at, axis, by):
    out = dict(at)
    out[axis] = (at[axis] + by) % RING if axis != "c" else 1 - at[axis]
    return out


def block(ref, at, whole, lo, hi, rows):
    every = slice(None)
    pick = lambda axis, value: every if axis in whole else value
    span = pl.ds(lo, hi - lo)
    return ref.at[
        pick("y", at["y"]), pick("x", at["x"] % 2), pick("z", at["z"]), pick("x", at["x"] // 2), at["c"],
        span if rows else every, every if rows else span,
    ]


def middle(lo, hi, rows):
    grain = 8 if rows else 128
    return lo + ((hi - lo) // grain // 2) * grain


def neighbours(me):
    return [moved(me, a, d) for a in "xyz" for d in (1, -1)] + [moved(me, "c", 1)]


def dot(a, b, dims=((1,), (0,))):
    return lax.dot_general(a, b, (dims, ((), ())), preferred_element_type=F32)


def by_rows(count, size, body):
    def one(k, _):
        body(pl.ds(pl.multiple_of(k * size, size), size))
        return 0
    lax.fori_loop(0, count // size, one, 0)


def columns_of(k, size):
    return pl.ds(pl.multiple_of(k * size, size), size)


def sigmoid(u):
    return 1.0 / (1.0 + jnp.exp(-u))


def rms_factor(v):
    return lax.rsqrt(jnp.mean(v * v, axis=-1, keepdims=True) + EPSILON)


class Gather:
    def __init__(self, arrays, me, send_sem, recv_sem, csend_sem, crecv_sem):
        self.arrays, self.me = arrays, me
        self.send_sem, self.recv_sem, self.csend_sem, self.crecv_sem = send_sem, recv_sem, csend_sem, crecv_sem
        self.sends = []

    def copy(self, ref, u, slot, to):
        return pltpu.make_async_remote_copy(src_ref=ref, dst_ref=ref, send_sem=self.send_sem.at[u, slot],
            recv_sem=self.recv_sem.at[u, slot], device_id=device(to), device_id_type=MESH)

    def ccopy(self, ref, u, slot):
        return pltpu.make_async_remote_copy(src_ref=ref, dst_ref=ref, send_sem=self.csend_sem.at[u, slot],
            recv_sem=self.crecv_sem.at[u, slot], device_id=device(moved(self.me, "c", 1)), device_id_type=MESH)

    def go(self, cp):
        cp.start()
        self.sends.append(cp)

    def part(self, u, at, stage, half=None):
        i, s, lo, hi = UNITS[u]
        rows = SPLIT_ROWS[i]
        mid = middle(lo, hi, rows)
        lo, hi = (lo, hi) if half is None else ((lo, mid), (mid, hi))[half]
        return block(self.arrays[i], at, ORDERS[s][:stage], lo, hi, rows)

    def axis(self, u, stage):
        return ORDERS[UNITS[u][1]][stage]

    def begin(self, units, stage):
        for u in units:
            a = self.axis(u, stage)
            if stage == 0:
                for k, by in enumerate((1, -1, 2)):
                    self.go(self.copy(self.part(u, self.me, stage), u, k, moved(self.me, a, by)))
                continue
            for k, (half, by) in enumerate(((0, 1), (1, -1), (1, 1), (0, -1))):
                self.go(self.copy(self.part(u, self.me, stage, half), u, 6 * stage + k, moved(self.me, a, by)))
            if stage == 2:
                self.go(self.ccopy(self.part(u, self.me, stage), u, 0))

    def relay(self, units, stage):
        for u in units:
            a = self.axis(u, stage)
            for half, by in ((0, 1), (1, -1)):
                first = self.part(u, moved(self.me, a, -by), stage, half)
                self.copy(first, u, 6 * stage + half, moved(self.me, a, by)).wait_recv()
                self.go(self.copy(first, u, 6 * stage + 4 + half, moved(self.me, a, by)))

    def finish(self, units, stage):
        for u in units:
            a = self.axis(u, stage)
            if stage == 0:
                for k, by in enumerate((-1, 1, 2)):
                    self.copy(self.part(u, moved(self.me, a, by), stage), u, k, moved(self.me, a, 1)).wait_recv()
                continue
            for k, by, half in ((2, -1, 1), (3, 1, 0), (4, 2, 0), (5, 2, 1)):
                self.copy(self.part(u, moved(self.me, a, by), stage, half), u, 6 * stage + k, moved(self.me, a, 1)).wait_recv()
            if stage == 2:
                for k, by in enumerate((-1, 1, 2)):
                    self.go(self.ccopy(self.part(u, moved(self.me, a, by), stage), u, 1 + k))

    def advance(self, units, stage):
        for u in units:
            self.finish((u,), stage)
            self.begin((u,), stage + 1)

    def arrive(self, units):
        sib = moved(self.me, "c", 1)
        for u in units:
            for k, by in enumerate((0, -1, 1, 2)):
                self.ccopy(self.part(u, moved(sib, self.axis(u, 2), by), 2), u, k).wait_recv()

    def drain(self):
        for cp in self.sends:
            cp.wait_send()


class Scan:
    def __init__(self, local, came, going, carried, sems):
        self.me, self.dp = lax.axis_index("seq"), lax.axis_index("dp")
        self.local, self.came, self.going, self.carried = local, came, going, carried
        self.send1, self.recv1, self.send2, self.recv2 = sems

    def to(self, k):
        return (self.me + k) % N_SEQ

    def out(self, to):
        return pltpu.make_async_remote_copy(src_ref=self.local.at[to], dst_ref=self.came.at[self.me], send_sem=self.send1.at[to],
            recv_sem=self.recv1.at[self.me], device_id=(self.dp, to), device_id_type=MESH)

    def back(self, to):
        return pltpu.make_async_remote_copy(src_ref=self.going.at[to], dst_ref=self.carried.at[self.me], send_sem=self.send2.at[to],
            recv_sem=self.recv2.at[self.me], device_id=(self.dp, to), device_id_type=MESH)

    def arrival(self, ref, ssem, rsem, frm):
        return pltpu.make_async_remote_copy(src_ref=ref.at[frm], dst_ref=ref.at[frm], send_sem=ssem.at[frm],
            recv_sem=rsem.at[frm], device_id=(self.dp, self.to(1)), device_id_type=MESH)

    def each(self, body):
        def one(k, _):
            body(self.to(k))
            return 0
        lax.fori_loop(1, N_SEQ, one, 0)

    def start(self):
        self.each(lambda to: self.out(to).start())
        self.came[self.me] = self.local[self.me]

    def join(self, tags_all, decays, backward):
        self.each(lambda frm: self.arrival(self.came, self.send1, self.recv1, frm).wait_recv())
        micro, head = self.me // H, self.me % H
        fade = jnp.exp(-float(HD) * jnp.full((1, HD), decays[head], F32))
        first = lambda b: tags_all[b, pl.ds(2 * micro, 1), :]
        last = lambda b: tags_all[b, pl.ds(2 * micro + 1, 1), :]
        acc = jnp.zeros((HD, HD), F32)
        previous = None
        for b in (range(N_SEQ - 1, -1, -1) if backward else range(N_SEQ)):
            self.going[b] = acc.astype(LOW)
            if previous is None:
                acc = self.came[b].astype(F32)
            else:
                near = (last(b) == first(previous)) if backward else (first(b) == last(previous))
                acc = self.came[b].astype(F32) + jnp.where((first(b) == last(b)) & near, fade, 0.0) * acc
            previous = b
        self.carried[self.me] = self.going[self.me]
        self.each(lambda to: self.back(to).start())

    def finish(self):
        self.each(lambda frm: self.arrival(self.carried, self.send2, self.recv2, frm).wait_recv())

    def drain(self):
        def one(to):
            self.out(to).wait_send()
            self.back(to).wait_send()
        self.each(one)


def spread(row):
    across = jnp.broadcast_to(row, (HD, HD))
    return across.T, across


def row_index():
    return lax.broadcasted_iota(jnp.int32, (HD, HD), 0).astype(F32)


def column_index():
    return lax.broadcasted_iota(jnp.int32, (HD, HD), 1).astype(F32)


def each_pair(body, together=4):
    def some(k, _):
        for i in range(together):
            body(k * together + i, 0)
        return 0
    lax.fori_loop(0, 2 * H // together, some, 0)


def pair_at(p):
    micro, head = p // H, p % H
    return micro, head, pl.ds(pl.multiple_of(micro * HD, HD), HD), pl.ds(pl.multiple_of(head * HD, HD), HD)


def transpose_into(src, dst, count):
    def one(k, _):
        at = columns_of(k, 128)
        dst[at, :] = src[:, at].T
        return 0
    lax.fori_loop(0, count // 128, one, 0)


def forward_kernel(*refs):
    (x, cot, whole_ids, decays), small = refs[:4], refs[4:12]
    (act, tags_all, o_qkv, o_slopes, o_gate, o_mixed, o_resid, o_up, o_carried, o_in, o_output, o_wide, o_down,
     t_first, t_gated, t_second, t_product, b_branch) = refs[12:30]
    (w_in, w_output, w_up, w_flat, w_down, pre, first_in, qkv, slopes, gate, mixed, resid, up, gated, second, product,
     first_t, gated_t, second_t, product_t, carried, local, came, going, spare, tag, allowed, kept_mask, ids_down,
     send_sem, recv_sem, csend_sem, crecv_sem, tag_send, tag_recv, s1, r1, s2, r2, out_sem, pass_send, pass_recv, ids) = refs[30:]
    me = where_am_i()
    sib = moved(me, "c", 1)
    seq, dp = lax.axis_index("seq"), lax.axis_index("dp")
    to = lambda k: (seq + k) % N_SEQ
    barrier = pltpu.get_barrier_semaphore()
    close = neighbours(me) + [moved(me, a, 2) for a in "xyz"]
    for other in close:
        pl.semaphore_signal(barrier, inc=1, device_id=device(other), device_id_type=MESH)

    def greet(k, _):
        pl.semaphore_signal(barrier, inc=1, device_id=(dp, to(k)), device_id_type=MESH)
        return 0
    lax.fori_loop(1, N_SEQ, greet, 0)

    here = (me["y"], me["x"] % 2, me["z"], me["x"] // 2, me["c"])
    def place(src, target, base, width):
        n = width // 128
        spare[pl.ds(0, 8 * n), :] = src[...].astype(F32)
        for c in range(n):
            target[(*here, slice(None), pl.ds(base + c * 128, 128))] = spare[pl.ds(c, 8, stride=n), :].astype(LOW)
    for k in range(4):
        place(small[k], w_in, k * D, D)
    place(small[4], w_output, 0, D)
    place(small[5], w_up, 0, FF)
    place(small[6], w_up, FF, FF)
    w_flat[here] = small[7][...]
    ids[...] = whole_ids[...].astype(F32)
    tag[...] = jnp.zeros((8, HD), F32)
    for m in range(2):
        tag[2 * m:2 * m + 1, :] = jnp.broadcast_to(ids[m:m + 1, 0:1], (1, HD))
        tag[2 * m + 1:2 * m + 2, :] = jnp.broadcast_to(ids[m:m + 1, HD - 1:HD], (1, HD))
    tags_all[seq] = tag[...]
    pl.semaphore_wait(barrier, len(close) + N_SEQ - 1)

    g = Gather((w_in, w_output, w_up, w_flat), me, send_sem, recv_sem, csend_sem, crecv_sem)
    scan = Scan(local, came, going, carried, (s1, r1, s2, r2))
    g.begin(C1, 0)
    g.begin(C2, 0)
    g.begin(C3, 0)

    kept, passed = [], []
    def keep(src, dst):
        cp = pltpu.make_async_copy(src, dst, out_sem.at[len(kept)])
        cp.start()
        kept.append(cp)
    def hand(mine, theirs, dst):
        keep(mine, dst.at[me["c"]])
        k = len(passed)
        cp = pltpu.make_async_remote_copy(src_ref=theirs, dst_ref=dst.at[me["c"]], send_sem=pass_send.at[k],
            recv_sem=pass_recv.at[k], device_id=device(sib), device_id_type=MESH)
        cp.start()
        passed.append((cp, dst))

    def tag_copy(other):
        return pltpu.make_async_remote_copy(src_ref=tag, dst_ref=tags_all.at[seq], send_sem=tag_send.at[other],
            recv_sem=tag_recv.at[seq], device_id=(dp, other), device_id_type=MESH)
    scan.each(lambda other: tag_copy(other).start())

    def norm_in(rows):
        v = x[rows, :].astype(F32)
        first_in[rows, :] = (v * rms_factor(v)).astype(LOW)
    by_rows(ROWS, 32, norm_in)
    g.advance(C1, 0)
    for m in range(2):
        down, across = spread(ids[m:m + 1, :])
        ids_down[m] = down
        allowed[m] = jnp.where((down == across) & (row_index() >= column_index()), 1.0, 0.0)
        kept_mask[m] = jnp.where(down == jnp.broadcast_to(ids[m:m + 1, HD - 1:HD], (HD, HD)), 1.0, 0.0)
    g.relay(C1, 1)
    g.advance(C2, 0)
    g.advance(C1, 1)
    g.advance(C3, 0)
    half = lambda c: cot.at[:, pl.ds(pl.multiple_of(c * 512, 512), 512)]
    hand(half(me["c"]), half(sib["c"]), b_branch)
    transpose_into(first_in, first_t, D)
    hand(first_t, first_t, t_first)
    g.relay(C2, 1)
    g.relay(C1, 2)
    g.relay(C3, 1)
    g.advance(C2, 1)
    g.finish(C1, 2)
    g.arrive(C1)
    keep(w_in, o_in)

    m_in = w_in.reshape(D, 4 * D)
    def project(k):
        cols = columns_of(k, 512)
        pre[:, cols] = dot(first_in[...], m_in[:, cols])
    def project_kv(k, _):
        project(k + 2)
        return 0
    lax.fori_loop(0, 4, project_kv, 0)
    def swish_rows(rows, k):
        u = pre[rows, k * D:(k + 1) * D]
        s = sigmoid(u)
        qkv[rows, k * D:(k + 1) * D] = (u * s).astype(LOW)
        slopes[rows, k * D:(k + 1) * D] = (s * (1.0 + u * (1.0 - s))).astype(LOW)
    def rows_kv(rows):
        swish_rows(rows, 1)
        qkv[rows, 2 * D:3 * D] = pre[rows, 2 * D:3 * D].astype(LOW)
    by_rows(ROWS, 32, rows_kv)

    def states(p, _):
        micro, head, rows, _ = pair_at(p)
        keeping = jnp.exp((row_index() - (HD - 1.0)) * decays[head]) * kept_mask[micro]
        held = (qkv[rows, head_of(head, 1)].astype(F32) * keeping).astype(LOW)
        local[p] = dot(held, qkv[rows, head_of(head, 2)], ((0,), (0,))).astype(LOW)
        return 0
    each_pair(states)
    scan.start()
    g.relay(C2, 2)
    g.advance(C3, 1)
    def project_qg(k, _):
        project(jnp.where(k < 2, k, k + 4))
        return 0
    lax.fori_loop(0, 4, project_qg, 0)
    def rows_qg(rows):
        swish_rows(rows, 0)
        gate[rows, :] = pre[rows, 3 * D:4 * D].astype(LOW)
    by_rows(ROWS, 32, rows_qg)
    keep(qkv, o_qkv)
    keep(slopes, o_slopes)
    keep(gate, o_gate)

    def within(p, _):
        micro, head, rows, cols = pair_at(p)
        mask = allowed[micro] * jnp.exp(jnp.minimum(column_index() - row_index(), 0.0) * decays[head])
        weighted = (dot(qkv[rows, head_of(head, 0)], qkv[rows, head_of(head, 1)], ((1,), (1,))) * mask).astype(LOW)
        mixed[rows, cols] = dot(weighted, qkv[rows, head_of(head, 2)])
        return 0
    each_pair(within)
    scan.each(lambda frm: pltpu.make_async_remote_copy(src_ref=tag, dst_ref=tags_all.at[frm], send_sem=tag_send.at[frm],
        recv_sem=tag_recv.at[frm], device_id=(dp, to(1)), device_id_type=MESH).wait_recv())
    scan.join(tags_all, decays, False)
    g.finish(C2, 2)
    g.relay(C3, 2)
    g.arrive(C2_FIRST)
    keep(w_output, o_output)
    scan.finish()
    keep(carried, o_carried)

    def crossing(p, _):
        micro, head, rows, cols = pair_at(p)
        boundary = jnp.where(seq > 0, tags_all[jnp.maximum(seq - 1, 0), pl.ds(2 * micro + 1, 1), :], -1.0)
        reaching = jnp.where(ids_down[micro] == boundary, jnp.exp(-(row_index() + 1.0) * decays[head]), 0.0)
        mixed[rows, cols] += dot(qkv[rows, head_of(head, 0)], carried[p]) * reaching
        return 0
    each_pair(crossing)
    keep(mixed, o_mixed)

    def gate_rows(rows):
        v = mixed[rows, :]
        gated[rows, :] = (v * rms_factor(v) * pre[rows, 3 * D:4 * D]).astype(LOW)
    by_rows(ROWS, 32, gate_rows)
    m_output = w_output.reshape(D, D)
    def output(k, _):
        cols = columns_of(k, 512)
        resid[:, cols] = x[:, cols].astype(F32) + dot(gated[...], m_output[:, cols])
        for c in range(4):
            at = columns_of(k * 4 + c, 128)
            gated_t[at, :] = gated[:, at].T
        return 0
    lax.fori_loop(0, 2, output, 0)
    keep(resid, o_resid)
    def norm_second(rows):
        v = resid[rows, :]
        second[rows, :] = (v * rms_factor(v)).astype(LOW)
    by_rows(ROWS, 32, norm_second)
    hand(gated_t, gated_t, t_gated)
    g.finish(C3, 2)
    g.arrive(C2[1:])
    keep(w_up, o_wide)
    m_up = w_up.reshape(D, 2 * FF)
    def widen(k, _):
        cols, more = columns_of(k, 256), pl.ds(pl.multiple_of(k * 256 + FF, 256), 256)
        left = dot(second[...], m_up[:, cols])
        right = dot(second[...], m_up[:, more])
        up[:, cols] = left.astype(LOW)
        up[:, more] = right.astype(LOW)
        both = (left * right).astype(LOW)
        product[:, cols] = both
        product_t[cols, :] = both.T
        return 0
    lax.fori_loop(0, 11, widen, 0)
    keep(up, o_up)
    hand(product_t, product_t, t_product)
    g.arrive(C3)
    flat = w_flat.reshape(128 * 176, 128)
    def arrange(k, _):
        spare[...] = flat[pl.ds(pl.multiple_of(k * 1408, 1408), 1408), :].astype(F32)
        for c in range(8):
            w_down[pl.ds(pl.multiple_of(k * 176, 176), 176), c * 128:(c + 1) * 128] = spare[pl.ds(c, 176, stride=8), :].astype(LOW)
        return 0
    for half_at in range(2):
        lax.fori_loop(8 * half_at, 8 * half_at + 8, arrange, 0)
        some = pl.ds(half_at * FF // 2, FF // 2)
        keep(w_down.at[some, :], o_down.at[some, :])
    def last(k, _):
        cols = columns_of(k, 512)
        act[:, cols] = (resid[:, cols] + dot(product[...], w_down[:, cols])).astype(LOW)
        for c in range(4):
            at = columns_of(k * 4 + c, 128)
            second_t[at, :] = second[:, at].T
        return 0
    lax.fori_loop(0, 2, last, 0)
    hand(second_t, second_t, t_second)
    for cp in kept:
        cp.wait()
    for k, (cp, dst) in enumerate(passed):
        cp.wait_send()
        there = dst.at[sib["c"]]
        pltpu.make_async_remote_copy(src_ref=there, dst_ref=there, send_sem=pass_send.at[k], recv_sem=pass_recv.at[k],
            device_id=device(sib), device_id_type=MESH).wait_recv()
    scan.each(lambda other: tag_copy(other).wait_send())
    scan.drain()
    g.drain()


def forward(x, cot, ids, decays, pieces):
    v = pl.BlockSpec(memory_space=pltpu.VMEM)
    anywhere = pl.BlockSpec(memory_space=pl.ANY)
    sds = jax.ShapeDtypeStruct
    n = len(UNITS)
    outs = [sds((ROWS, D), LOW), sds((N_SEQ, 8, HD), F32), sds((ROWS, 3 * D), LOW), sds((ROWS, 2 * D), LOW), sds((ROWS, D), LOW),
        sds((ROWS, D), F32), sds((ROWS, D), F32), sds((ROWS, 2 * FF), LOW), sds((N_SEQ, HD, HD), LOW),
        sds(OWNERS + (8, 4 * D), LOW), sds(OWNERS + (8, D), LOW), sds(OWNERS + (8, 2 * FF), LOW), sds((FF, D), LOW),
        sds((2, D, ROWS), LOW), sds((2, D, ROWS), LOW), sds((2, D, ROWS), LOW), sds((2, FF, ROWS), LOW), sds((2, ROWS, D // 2), LOW)]
    vm = pltpu.VMEM
    scratch = [vm(OWNERS + (8, 4 * D), LOW), vm(OWNERS + (8, D), LOW), vm(OWNERS + (8, 2 * FF), LOW), vm(OWNERS + (176, 128), LOW),
        vm((FF, D), LOW), vm((ROWS, 4 * D), F32), vm((ROWS, D), LOW), vm((ROWS, 3 * D), LOW), vm((ROWS, 2 * D), LOW), vm((ROWS, D), LOW),
        vm((ROWS, D), F32), vm((ROWS, D), F32), vm((ROWS, 2 * FF), LOW), vm((ROWS, D), LOW), vm((ROWS, D), LOW), vm((ROWS, FF), LOW),
        vm((D, ROWS), LOW), vm((D, ROWS), LOW), vm((D, ROWS), LOW), vm((FF, ROWS), LOW)] + [vm((N_SEQ, HD, HD), LOW)] * 4 + [
        vm((1408, 128), F32), vm((8, HD), F32)] + [vm((2, HD, HD), F32)] * 3 + [
        DMA((n, 18)), DMA((n, 18)), DMA((n, 4)), DMA((n, 4))] + [DMA((N_SEQ,))] * 6 + [DMA((20,)), DMA((5,)), DMA((5,)), vm((2, HD), F32)]
    return pl.pallas_call(
        forward_kernel, out_shape=outs,
        in_specs=[v, v, v, pl.BlockSpec(memory_space=pltpu.SMEM)] + [v] * 8,
        out_specs=[v] * 2 + [anywhere] * 16,
        scratch_shapes=scratch,
        compiler_params=pltpu.CompilerParams(collective_id=0, has_side_effects=True, vmem_limit_bytes=60 << 20),
        name="gather_and_forward",
    )(x, cot, ids, decays, *pieces)


def head_of(head, part):
    return pl.ds(pl.multiple_of(part * D + head * HD, HD), HD)


DOWN, WIDE, OUTPUT, INPUT = range(4)
HELD = ((88, 256), (16, FF), (16, D // 2), (16, 2 * D))
GROUPS = (
    tiles(DOWN, (0, 3, 7, 11), 8),
    tiles(WIDE, (0, 7, 14, 22)),
    [(OUTPUT, 0, 0, 512)],
    [(INPUT, 1, 1536, 2048)],
    [(INPUT, 2, 0, 512)],
    [(INPUT, 0, 512, 896), (INPUT, 1, 896, 1280), (INPUT, 2, 1280, 1536)],
)
BACK_UNITS = tuple(unit for group in GROUPS for unit in group)
G_DOWN, G_WIDE, G_OUTPUT, G_GATE, G_QUERY, G_VALUE = (tuple(BACK_UNITS.index(unit) for unit in group) for group in GROUPS)
BACK_ORDERS = tuple(order[::-1] for order in ORDERS)
DIMS = (("y", 4), ("x", 2), ("z", 4), ("x", 2))


def live_dims(fixed):
    return tuple(n for a, n in DIMS if a not in fixed)


def part_of(ref, at, fixed, gone, lo, hi, rows, lead=()):
    every = slice(None)
    idx = []
    for k, (a, n) in enumerate(DIMS):
        if a in gone:
            continue
        if a in fixed:
            idx.append((at["x"] % 2 if k == 1 else at["x"] // 2) if a == "x" else at[a])
        else:
            idx.append(every)
    span = pl.ds(lo, hi - lo)
    return ref.at[(*lead, *idx, span if rows else every, every if rows else span)]


def accumulate(dst, srcs, dims, out=None):
    target = dst if out is None else out
    rows, width = dst.shape[-2:]
    most = max(1, 64 // max(1, rows * width // 1024))
    cut, inner = len(dims), 1
    while cut > 0 and inner * dims[cut - 1] <= most:
        cut -= 1
        inner *= dims[cut]
    near = [()]
    for d in dims[cut:]:
        near = [at + (i,) for at in near for i in range(d)]
    def group(lead):
        places = [lead + at if dims else ... for at in near]
        totals = []
        for at in places:
            total = dst[at].astype(F32)
            for s in srcs:
                total = total + s[at].astype(F32)
            totals.append(total.astype(target.dtype))
        for at, total in zip(places, totals):
            target[at] = total
    count = 1
    for d in dims[:cut]:
        count *= d
    def one(k, _):
        idx, rest = [], k
        for m, d in enumerate(dims[:cut][::-1]):
            last = m == cut - 1
            idx.append(rest if last else rest % d)
            rest = rest if last else rest // d
        group(tuple(idx[::-1]))
        return 0
    if count == 1:
        group((0,) * cut)
    else:
        lax.fori_loop(0, count, one, 0)


class Scatter:
    def __init__(self, held, slots, final, me, send_sem, recv_sem):
        self.held, self.slots, self.final, self.me = held, slots, final, me
        self.send_sem, self.recv_sem = send_sem, recv_sem
        self.sends = []

    def spans(self, u):
        i, s, lo, hi = BACK_UNITS[u]
        return self.held[i], BACK_ORDERS[s], i == DOWN, lo, middle(lo, hi, i == DOWN), hi

    def slot(self, u, stage, k, lo, hi):
        _, order, rows, base, _, _ = self.spans(u)
        return part_of(self.slots[stage][u], self.me, (), order[:stage + 1], lo - base, hi - base, rows, (k,))

    def send(self, src, dst, u, stage, k, to):
        cp = pltpu.make_async_remote_copy(src_ref=src, dst_ref=dst, send_sem=self.send_sem.at[u, stage, k],
            recv_sem=self.recv_sem.at[u, stage, k], device_id=device(to), device_id_type=MESH)
        cp.start()
        self.sends.append(cp)

    def got(self, ref, u, stage, k):
        pltpu.make_async_remote_copy(src_ref=ref, dst_ref=ref, send_sem=self.send_sem.at[u, stage, k],
            recv_sem=self.recv_sem.at[u, stage, k], device_id=device(moved(self.me, "c", 1)), device_id_type=MESH).wait_recv()

    def far(self, units, stage):
        for u in units:
            held, order, rows, lo, mid, hi = self.spans(u)
            axis, fixed = order[stage], order[:stage + 1]
            above, below, across = (moved(self.me, axis, by) for by in (1, -1, 2))
            mine = lambda at, a, b: part_of(held, at, fixed, (), a, b, rows)
            if stage == 2 or stage == 1 and u not in G_WIDE:
                for k, at in enumerate((across, above, below)):
                    self.send(mine(at, lo, hi), self.slot(u, stage, k, lo, hi), u, stage, k, at)
                continue
            self.send(mine(across, lo, mid), self.slot(u, stage, 0, lo, mid), u, stage, 0, above)
            self.send(mine(across, mid, hi), self.slot(u, stage, 0, mid, hi), u, stage, 1, below)
            self.send(mine(above, mid, hi), self.slot(u, stage, 1, mid, hi), u, stage, 2, above)
            self.send(mine(below, lo, mid), self.slot(u, stage, 2, lo, mid), u, stage, 3, below)

    def turn(self, units, stage):
        for u in units:
            held, order, rows, lo, mid, hi = self.spans(u)
            fixed = order[:stage + 1]
            for k, (by, a, b) in enumerate(((1, lo, mid), (-1, mid, hi))):
                to = moved(self.me, order[stage], by)
                came = self.slot(u, stage, 0, a, b)
                self.got(came, u, stage, k)
                sums = part_of(held, to, fixed, (), a, b, rows)
                accumulate(sums, [came], live_dims(fixed))
                self.send(sums, self.slot(u, stage, 1 + k, a, b), u, stage, 4 + k, to)

    def land(self, units, stage):
        for u in units:
            held, order, rows, lo, mid, hi = self.spans(u)
            fixed = order[:stage + 1]
            mine = part_of(held, self.me, fixed, (), lo, hi, rows)
            if stage == 2 or stage == 1 and u not in G_WIDE:
                came = [self.slot(u, stage, k, lo, hi) for k in range(3)]
                for k in range(3):
                    self.got(came[k], u, stage, k)
                span = pl.ds(lo, hi - lo)
                if stage == 2:
                    accumulate(mine, came, (), self.final[BACK_UNITS[u][0]].at[(span, slice(None)) if rows else (slice(None), span)])
                else:
                    accumulate(mine, came, live_dims(fixed))
                    self.far((u,), 2)
                continue
            for k, (a, b) in ((2, (mid, hi)), (3, (lo, mid)), (4, (lo, mid)), (5, (mid, hi))):
                self.got(self.slot(u, stage, 1 + k % 2, a, b), u, stage, k)
            accumulate(mine, [self.slot(u, stage, 1 + k, lo, hi) for k in range(2)], live_dims(fixed))
            self.far((u,), stage + 1)

    def drain(self):
        for cp in self.sends:
            cp.wait_send()


def norm_back(upstream, normed, factor):
    return factor * (upstream - normed * jnp.mean(upstream * normed, axis=-1, keepdims=True))


def backward_kernel(*refs):
    (whole_ids, h_tags, decays, h_x, h_cot, h_qkv, h_slopes, h_gate, h_mixed, h_resid, h_up, h_carried, w_in, w_output, w_up, w_down,
     t_first, t_gated, t_second, t_product, b_branch) = refs[:21]
    o_input, o_grads = refs[21], refs[22:30]
    refs = refs[30:]
    input_grad, grads, ids, tags_all, refs = refs[0], refs[1:9], refs[9], refs[10], refs[11:]
    n = len(BACK_UNITS)
    held, refs = refs[:4], refs[4:]
    slots = [refs[k * n:(k + 1) * n] for k in range(3)]
    refs = refs[3 * n:]
    final, theirs, refs = refs[:4], refs[4:7], refs[7:]
    (quarters, regroup, wbuf, product_t, lhs_a, lhs_b, branch, cot, d_up, up_sib, d_attn, attn_sib, pre_sib,
     up, qkv, slopes, gate, mixed, resid, x, work, d_mixed, carried, local, came, going, reverse, ids_down, allowed,
     load_sem, wsem, send_sem, recv_sem, s1, r1, s2, r2, pass_send, pass_recv, end_send, end_recv, q_send, q_recv, out_sem) = refs
    me = where_am_i()
    sib = moved(me, "c", 1)
    core, other_core = me["c"], sib["c"]
    seq, dp = lax.axis_index("seq"), lax.axis_index("dp")
    to = lambda k: (seq + k) % N_SEQ
    barrier = pltpu.get_barrier_semaphore()
    close = neighbours(me) + [moved(me, a, 2) for a in "xyz"]
    for other in close:
        pl.semaphore_signal(barrier, inc=1, device_id=device(other), device_id_type=MESH)

    def greet(k, _):
        pl.semaphore_signal(barrier, inc=1, device_id=(dp, to(k)), device_id_type=MESH)
        return 0
    lax.fori_loop(1, N_SEQ, greet, 0)

    loads = {}
    def load(name, src, dst):
        cp = pltpu.make_async_copy(src, dst, load_sem.at[len(loads)])
        cp.start()
        loads[name] = cp
    ids[...] = whole_ids[...].astype(F32)
    load("tags", h_tags, tags_all)
    load("product", t_product, product_t)
    load("branch", b_branch, branch)
    load("cot", h_cot, cot)

    phases = ((w_down, 11, 0, D), (w_up, 4, 0, FF), (w_up, 4, FF, FF), (w_output, 4, 0, D),
        (w_in, 4, 3 * D, D), (w_in, 4, 0, 2 * D), (w_in, 4, 2 * D, D))
    first = [sum(p[1] for p in phases[:k]) for k in range(len(phases))]
    def piece(phase, k):
        w, _, col, width = phases[phase]
        slot = (first[phase] + k) % 3
        row = pl.multiple_of(k * 256, 256)
        return pltpu.make_async_copy(w.at[pl.ds(row, 256), pl.ds(col, width)], wbuf.at[slot, :, pl.ds(0, width)], wsem.at[slot])
    def stream(phase, compute):
        count, width = phases[phase][1], phases[phase][3]
        def one(k, _):
            @pl.when(k + 2 < count)
            def _():
                piece(phase, k + 2).start()
            if phase + 1 < len(phases):
                @pl.when(k + 2 >= count)
                def _():
                    piece(phase + 1, k + 2 - count).start()
            piece(phase, k).wait()
            compute(k, wbuf.at[(first[phase] + k) % 3, :, pl.ds(0, width)])
            return 0
        lax.fori_loop(0, count, one, 0)
    piece(0, 0).start()
    piece(0, 1).start()
    load("up", h_up, up)
    kept = []
    def keep(src, dst):
        cp = pltpu.make_async_copy(src, dst, out_sem.at[len(kept)])
        cp.start()
        kept.append(cp)
    loads["tags"].wait()
    for m in range(2):
        below, across = spread(ids[m:m + 1, :])
        ids_down[m] = below
        allowed[m] = jnp.where((below == across) & (row_index() >= column_index()), 1.0, 0.0)
    rs = Scatter(held, slots, final, me, send_sem, recv_sem)
    scan = Scan(local, came, going, reverse, (s1, r1, s2, r2))
    passed = []
    def hand(src, dst):
        k = len(passed)
        cp = pltpu.make_async_remote_copy(src_ref=src, dst_ref=dst, send_sem=pass_send.at[k], recv_sem=pass_recv.at[k],
            device_id=device(sib), device_id_type=MESH)
        cp.start()
        passed.append(cp)
        return cp

    loads["product"].wait()
    loads["branch"].wait()
    def down_rows(k, _):
        rows = pl.ds(pl.multiple_of(k * 352, 32), 352)
        for j in range(2):
            cols = slice(j * 256, (j + 1) * 256)
            total = dot(product_t[0, rows, :], branch[0, :, cols]) + dot(product_t[1, rows, :], branch[1, :, cols])
            for i in range(4):
                held[DOWN][k // 2, k % 2, i, j] = total[i * 88:(i + 1) * 88].astype(LOW)
        return 0
    lax.fori_loop(0, 8, down_rows, 0)
    pl.semaphore_wait(barrier, len(close) + N_SEQ - 1)
    rs.far(G_DOWN, 0)
    load("second", t_second, lhs_a)

    loads["cot"].wait()
    loads["up"].wait()
    def up_back(k, w):
        cols, more = columns_of(k, 256), pl.ds(pl.multiple_of(k * 256 + FF, 256), 256)
        d_product = dot(cot[...], w[...], ((1,), (1,)))
        d_up[:, cols] = (d_product * up[:, more].astype(F32)).astype(LOW)
        d_up[:, more] = (d_product * up[:, cols].astype(F32)).astype(LOW)
    stream(0, up_back)
    side = lambda c, width, base=0: pl.ds(pl.multiple_of(c * width + base, 128), width)
    h_wide = hand(d_up.at[:, side(other_core, FF)], up_sib)
    load("resid", h_resid, resid)
    load("mixed", h_mixed, mixed)
    load("gate", h_gate, gate)
    load("qkv", h_qkv, qkv)
    load("gated", t_gated, lhs_b)
    load("carried", h_carried, carried)
    load("slopes", h_slopes, slopes)
    load("x", h_x, x)
    def grad_half(i, lhs, own, base, shift, sibling, units):
        out = held[i].reshape(D, HELD[i][1])
        for u in units:
            _, _, lo, hi = BACK_UNITS[u]
            a = lo
            while a < hi:
                wide = min(256, hi - a)
                mine = own[:, pl.ds(pl.multiple_of(base + (a - shift), 128), wide)]
                total = dot(lhs[core], mine) + dot(lhs[other_core], sibling[:, a:a + wide])
                out[:, a:a + wide] = total.astype(LOW)
                a += wide
            rs.far((u,), 0)

    loads["second"].wait()
    h_wide.wait_recv()
    grad_half(WIDE, lhs_a, d_up, core * FF, 0, up_sib, G_WIDE)
    load("first", t_first, lhs_a)
    def second_left(k, w):
        work[:, columns_of(k, 256)] = dot(d_up[:, 0:FF], w[...], ((1,), (1,)))
    stream(1, second_left)
    def second_right(k, w):
        work[:, columns_of(k, 256)] += dot(d_up[:, FF:2 * FF], w[...], ((1,), (1,)))
    stream(2, second_right)
    rs.turn(G_DOWN, 0)

    loads["resid"].wait()
    def resid_back(rows):
        v = resid[rows, :]
        factor = rms_factor(v)
        total = cot[rows, :].astype(F32) + norm_back(work[rows, :], v * factor, factor)
        resid[rows, :] = total
        d_attn[rows, :] = total.astype(LOW)
    by_rows(ROWS, 32, resid_back)
    h_attn = hand(d_attn.at[:, side(other_core, D // 2)], attn_sib)
    def gated_back(k, w):
        work[:, columns_of(k, 256)] = dot(d_attn[...], w[...], ((1,), (1,)))
    stream(3, gated_back)
    loads["mixed"].wait()
    loads["gate"].wait()
    def mixed_back(rows):
        v = mixed[rows, :]
        factor = rms_factor(v)
        normed = v * factor
        g = work[rows, :]
        d_mixed[rows, :] = norm_back(g * gate[rows, :].astype(F32), normed, factor).astype(LOW)
        gate[rows, :] = (g * normed).astype(LOW)
    by_rows(ROWS, 32, mixed_back)
    h_gate_out = hand(gate.at[:, side(other_core, D // 2)], pre_sib.at[:, pl.ds(1536, 512)])
    loads["qkv"].wait()
    def back_states(p, _):
        micro, head, rows, cols = pair_at(p)
        start = ids[pl.ds(micro, 1), 0:1]
        opening = jnp.where(ids_down[micro] == start, jnp.exp(-(row_index() + 1.0) * decays[head]), 0.0)
        opened = (qkv[rows, head_of(head, 0)].astype(F32) * opening).astype(LOW)
        local[p] = dot(opened, d_mixed[rows, cols], ((0,), (0,))).astype(LOW)
        return 0
    each_pair(back_states)
    scan.start()
    loads["gated"].wait()
    h_attn.wait_recv()
    grad_half(OUTPUT, lhs_b, d_attn, core * (D // 2), 0, attn_sib, G_OUTPUT)
    loads["first"].wait()
    h_gate_out.wait_recv()
    grad_half(INPUT, lhs_a, gate, core * (D // 2), 1536, pre_sib, G_GATE)
    rs.turn(G_WIDE, 0)
    rs.land(G_DOWN, 0)
    scan.join(tags_all, decays, True)

    h_wide.wait_send()
    loads["slopes"].wait()
    loads["carried"].wait()
    d_pre = d_up.at[:, 0:3 * D]
    def pair_back(p, _):
        micro, head, rows, cols = pair_at(p)
        q, k, v = (qkv[rows, head_of(head, part)] for part in range(3))
        dm = d_mixed[rows, cols]
        mask = allowed[micro] * jnp.exp(jnp.minimum(column_index() - row_index(), 0.0) * decays[head])
        weighted = (dot(q, k, ((1,), (1,))) * mask).astype(LOW)
        d_scores = (dot(dm, v, ((1,), (1,))) * mask).astype(LOW)
        boundary = jnp.where(seq > 0, tags_all[jnp.maximum(seq - 1, 0), pl.ds(2 * micro + 1, 1), :], -1.0)
        reaching = jnp.where(ids_down[micro] == boundary, jnp.exp(-(row_index() + 1.0) * decays[head]), 0.0)
        d_q = dot(d_scores, k) + dot(dm, carried[p], ((1,), (1,))) * reaching
        d_pre[rows, head_of(head, 0)] = (d_q * slopes[rows, head_of(head, 0)].astype(F32)).astype(LOW)
        work[rows, cols] = dot(d_scores, q, ((0,), (0,)))
        mixed[rows, cols] = dot(weighted, dm, ((0,), (0,)))
        return 0
    each_pair(pair_back)
    h_query = hand(d_pre.at[:, side(other_core, D // 2)], pre_sib.at[:, pl.ds(0, 512)])
    h_query.wait_recv()
    grad_half(INPUT, lhs_a, d_pre, core * (D // 2), 0, pre_sib, G_QUERY)
    scan.finish()
    def pair_close(p, _):
        micro, head, rows, cols = pair_at(p)
        after = jnp.where(seq < N_SEQ - 1, tags_all[jnp.minimum(seq + 1, N_SEQ - 1), pl.ds(2 * micro, 1), :], -1.0)
        closing = jnp.where(ids_down[micro] == after, jnp.exp((row_index() - (HD - 1.0)) * decays[head]), 0.0)
        d_k = work[rows, cols] + dot(qkv[rows, head_of(head, 2)], reverse[p], ((1,), (1,))) * closing
        d_v = mixed[rows, cols] + dot(qkv[rows, head_of(head, 1)], reverse[p]) * closing
        d_pre[rows, head_of(head, 1)] = (d_k * slopes[rows, head_of(head, 1)].astype(F32)).astype(LOW)
        d_pre[rows, head_of(head, 2)] = d_v.astype(LOW)
        return 0
    each_pair(pair_close)
    h_key = hand(d_pre.at[:, side(other_core, D // 2, D)], pre_sib.at[:, pl.ds(512, 512)])
    h_value = hand(d_pre.at[:, side(other_core, D // 2, 2 * D)], pre_sib.at[:, pl.ds(1024, 512)])
    rs.land(G_WIDE, 0)
    rs.land(G_DOWN, 1)
    h_key.wait_recv()
    h_value.wait_recv()
    out = held[INPUT].reshape(D, 2 * D)
    for u in G_VALUE:
        _, _, lo, hi = BACK_UNITS[u]
        a = lo
        while a < hi:
            part, within = a // 512, a % 512
            wide = min(256, hi - a, 512 - within)
            mine = d_pre[:, pl.ds(pl.multiple_of(part * D + core * 512 + within, 128), wide)]
            out[:, a:a + wide] = (dot(lhs_a[core], mine) + dot(lhs_a[other_core], pre_sib[:, a:a + wide])).astype(LOW)
            a += wide
        rs.far((u,), 0)
    rs.turn(G_OUTPUT, 0)
    rs.turn(G_GATE, 0)
    rs.turn(G_QUERY, 0)
    def first_gate(k, w):
        work[:, columns_of(k, 256)] = dot(gate[...], w[...], ((1,), (1,)))
    stream(4, first_gate)
    rs.turn(G_WIDE, 1)
    rs.turn(G_VALUE, 0)
    rs.land(G_OUTPUT, 0)
    rs.land(G_GATE, 0)
    rs.land(G_QUERY, 0)
    rs.land(G_WIDE, 1)
    rs.land(G_DOWN, 2)
    def first_keys(k, w):
        work[:, columns_of(k, 256)] += dot(d_pre[:, 0:2 * D], w[...], ((1,), (1,)))
    stream(5, first_keys)
    rs.land(G_VALUE, 0)
    rs.land(G_OUTPUT, 1)
    rs.land(G_GATE, 1)
    rs.land(G_QUERY, 1)
    def first_values(k, w):
        work[:, columns_of(k, 256)] += dot(d_pre[:, 2 * D:3 * D], w[...], ((1,), (1,)))
    stream(6, first_values)
    rs.land(G_VALUE, 1)
    rs.land(G_WIDE, 2)
    loads["x"].wait()
    def input_back(rows):
        v = x[rows, :].astype(F32)
        factor = rms_factor(v)
        input_grad[rows, :] = resid[rows, :] + norm_back(work[rows, :], v * factor, factor)
    by_rows(ROWS, 32, input_back)
    keep(input_grad, o_input)

    rs.land(G_OUTPUT, 2)
    place = me["x"] // 2 * 2 + core
    def owner(j):
        return (dp, me["z"] * 4 + j)
    for j in range(4):
        quarters[j, 0:22, :] = final[DOWN][j * 22:(j + 1) * 22, :]
    def quarter(k):
        j = (place + k) % 4
        return pltpu.make_async_remote_copy(src_ref=quarters.at[j], dst_ref=regroup.at[place], send_sem=q_send.at[j],
            recv_sem=q_recv.at[place], device_id=owner(j), device_id_type=MESH)
    for k in range(1, 4):
        quarter(k).start()
    regroup[place] = quarters[place]
    ends = {}
    def swap(i):
        cp = pltpu.make_async_remote_copy(src_ref=final[i].at[pl.ds(pl.multiple_of(other_core * 8, 8), 8), :], dst_ref=theirs[i - 1],
            send_sem=end_send.at[i - 1], recv_sem=end_recv.at[i - 1], device_id=device(sib), device_id_type=MESH)
        cp.start()
        ends[i] = cp
    def give(i, outs, part):
        ends[i].wait_recv()
        mine, came = final[i][pl.ds(pl.multiple_of(core * 8, 8), 8), :], theirs[i - 1][...]
        both = (jnp.where(core == 0, mine, came), jnp.where(core == 0, came, mine))
        n = part // 128
        for k, out in enumerate(outs):
            for c in range(2 * n):
                out[pl.ds(c, 8, stride=2 * n), :] = both[c // n][:, k * part + (c % n) * 128:k * part + (c % n + 1) * 128]
    swap(WIDE)
    swap(OUTPUT)
    for k in range(1, 4):
        j = (place + k) % 4
        pltpu.make_async_remote_copy(src_ref=regroup.at[j], dst_ref=regroup.at[j], send_sem=q_send.at[j],
            recv_sem=q_recv.at[j], device_id=owner((place + 1) % 4), device_id_type=MESH).wait_recv()
    for j in range(4):
        for k in range(2):
            t = (j % 2) * 4 + (j // 2) * 2 + k
            grads[7][pl.ds(t, 22, stride=8), :] = regroup[j, 0:22, k * 128:(k + 1) * 128]
    keep(grads[7], o_grads[7])
    ends[WIDE].wait_recv()
    mine, came = final[WIDE][pl.ds(pl.multiple_of(core * 8, 8), 8), :], theirs[WIDE - 1][...]
    for k, both in enumerate((jnp.where(core == 0, mine, came), jnp.where(core == 0, came, mine))):
        for c in range(22):
            grads[5 + k][pl.ds(c, 8, stride=22), :] = both[:, c * 128:(c + 1) * 128]
        keep(grads[5 + k], o_grads[5 + k])
    give(OUTPUT, grads[4:5], 512)
    keep(grads[4], o_grads[4])
    rs.land(G_GATE, 2)
    rs.land(G_QUERY, 2)
    rs.land(G_VALUE, 2)
    swap(INPUT)
    give(INPUT, grads[0:4], 512)
    for k in range(4):
        keep(grads[k], o_grads[k])
    for cp in kept:
        cp.wait()
    for cp in ends.values():
        cp.wait_send()
    for k in range(1, 4):
        quarter(k).wait_send()
    for cp in passed[1:]:
        cp.wait_send()
    scan.drain()
    rs.drain()


def backward(ids, tags_all, decays, arrays):
    anywhere = pl.BlockSpec(memory_space=pl.ANY)
    sds = jax.ShapeDtypeStruct
    vm = pltpu.VMEM
    n = len(BACK_UNITS)
    scratch = [vm((ROWS, D), F32)] + [vm((64, 128), F32)] * 5 + [vm((176, 128), F32)] * 3 + [vm((2, HD), F32), vm((N_SEQ, 8, HD), F32)]
    scratch += [vm(live_dims(()) + tail, LOW) for tail in HELD]
    for stage in range(3):
        for i, s, lo, hi in BACK_UNITS:
            tail = (hi - lo, 256) if i == DOWN else (HELD[i][0], hi - lo)
            scratch.append(vm((3,) + live_dims(BACK_ORDERS[s][:stage + 1]) + tail, LOW))
    scratch += [vm(tail, F32) for tail in HELD] + [vm((8, tail[1]), F32) for tail in HELD[1:]]
    full = lambda width, kind=LOW: vm((ROWS, width), kind)
    scratch += [vm((4, 24, 256), F32), vm((4, 24, 256), F32), vm((3, 256, FF), LOW), vm((2, FF, ROWS), LOW),
        vm((2, D, ROWS), LOW), vm((2, D, ROWS), LOW), vm((2, ROWS, D // 2), LOW), full(D), full(2 * FF), full(FF), full(D), full(D // 2),
        full(2 * D), full(2 * FF), full(3 * D), full(2 * D), full(D), full(D, F32), full(D, F32), full(D), full(D, F32), full(D)]
    scratch += [vm((N_SEQ, HD, HD), LOW)] * 5 + [vm((2, HD, HD), F32)] * 2
    scratch += [DMA((16,)), DMA((3,)), DMA((n, 3, 6)), DMA((n, 3, 6))] + [DMA((N_SEQ,))] * 4 + [DMA((6,))] * 2 + [DMA((3,))] * 2 + [DMA((4,))] * 2 + [DMA((9,))]
    return pl.pallas_call(
        backward_kernel,
        out_shape=[sds((ROWS, D), F32)] + [sds((64, 128), F32)] * 5 + [sds((176, 128), F32)] * 3,
        in_specs=[pl.BlockSpec(memory_space=pltpu.VMEM), anywhere, pl.BlockSpec(memory_space=pltpu.SMEM)] + [anywhere] * len(arrays),
        out_specs=[anywhere] * 9,
        scratch_shapes=scratch,
        compiler_params=pltpu.CompilerParams(collective_id=1, has_side_effects=True, vmem_limit_bytes=60 << 20),
        name="backward_and_scatter",
    )(ids, tags_all, decays, *arrays)


def copy_kernel(*refs):
    n = len(refs) // 3
    sems = refs[-1]
    steps = []
    for k in range(n):
        src, dst, via = refs[k], refs[n + k], refs[2 * n + k]
        pieces = [pl.ds(r, 64) for r in range(0, src.shape[0], 64)] if src.shape[0] == ROWS else [slice(None)]
        for piece in pieces:
            at = len(steps)
            steps.append((pltpu.make_async_copy(src.at[piece], via.at[piece], sems.at[0, at]),
                pltpu.make_async_copy(via.at[piece], dst.at[piece], sems.at[1, at])))
    for into, _ in steps:
        into.start()
    for into, out in steps:
        into.wait()
        out.start()
    for _, out in steps:
        out.wait()


def hand_out(arrays):
    anywhere = pl.BlockSpec(memory_space=pl.ANY)
    return pl.pallas_call(
        copy_kernel, out_shape=[jax.ShapeDtypeStruct(a.shape, a.dtype) for a in arrays],
        in_specs=[anywhere] * len(arrays), out_specs=[anywhere] * len(arrays),
        scratch_shapes=[pltpu.VMEM(a.shape, a.dtype) for a in arrays] + [DMA((2, 16))], name="hand_out",
    )(*arrays)


def on_device(hidden_in, seg_ids, decay_rates, grad_out, *weights):
    x, cot = hidden_in.reshape(ROWS, D), grad_out.reshape(ROWS, D)
    ids = seg_ids.reshape(2, HD)
    (act, tags_all, qkv, slopes, gate, mixed, resid, up, carried, w_in, w_output, w_up, w_down, t_first, t_gated, t_second,
     t_product, b_branch) = forward(x, cot, ids, decay_rates, [w.reshape(-1, 128) for w in weights])
    input_grad, *grads = backward(ids, tags_all, decay_rates, [
        x, cot, qkv, slopes, gate, mixed, resid, up, carried, w_in.reshape(D, 4 * D), w_output.reshape(D, D),
        w_up.reshape(D, 2 * FF), w_down, t_first, t_gated, t_second, t_product, b_branch])
    act, input_grad, *grads = hand_out([act, input_grad, *grads])
    return (act.reshape(hidden_in.shape), input_grad.reshape(hidden_in.shape), *(g.reshape(-1) for g in grads))


def solution(mesh):
    tokens = P(None, "dp", "seq", None)
    flat = P(("dp", "seq"))
    return jax.shard_map(
        on_device, mesh=mesh,
        in_specs=(tokens, P(None, "dp", "seq"), P(), tokens) + (flat,) * 8,
        out_specs=(tokens, tokens) + (flat,) * 8,
        check_vma=False,
    )
```
